512 devices in a mesh: lon: 32 (over z_lo, y), ch: 16 (over z_hi, x, core).
Axes of the slice: x: 4, y: 4, z: 16 (z_hi: 2, z_lo: 8; z = z_hi * 8 + z_lo), core: 2. Of those that a mesh axis runs over, the one named last changes fastest.
Arguments:
- features: bfloat16 [80, 480, 2048], P(None, 'lon', 'ch'), may hold values from -10 to 10
- pointwise_weight: bfloat16 [2048, 256], P('ch'), may hold values from -0.125 to 0.125
- w_atrous: bfloat16 [3, 3, 3, 2048, 256], P(None, None, None, 'ch'), may hold values from -0.046875 to 0.046875
- w_pool: bfloat16 [2048, 256], P('ch'), may hold values from -0.125 to 0.125
- w_proj: bfloat16 [1280, 256], replicated, may hold values from -0.15625 to 0.15625
- norm_gain: float32 [6, 256], replicated, may hold values from 0.1 to 1.9
- norm_shift: float32 [6, 256], replicated, may hold values from -3 to 3
Outputs:
- head_out: bfloat16 [80, 480, 256], P(None, 'lon', 'ch')
The draws below stay inside these ranges and needn't reach their ends.
All inputs are finite; a program needn't handle non-finite values.
Results may differ from the reference program's by a relative error of at most 0.017.
Values may be sent and summed in bfloat16 or wider, within the bound.
A program may use at most 64 MiB of HBM per device.

```python
import math
import jax
import jax.numpy as jnp
from jax import lax

CIN = 2048
OUT = 256
BASE_DILATION = 12
ROWS = 80
WIDTH = 480
N_CH = 16


def draw_features(key, part):
    keys = jax.random.split(key, 6)
    angle = 2.0 * math.pi * jnp.arange(WIDTH, dtype=jnp.float32) / WIDTH
    phases = jax.random.uniform(keys[0], (3,), jnp.float32, 0.0, 2.0 * math.pi)
    rough = jax.random.uniform(keys[1], (WIDTH,), jnp.float32, -0.5, 0.5)
    spread = 0.5 * jnp.exp(jax.random.uniform(keys[2], (CIN,), jnp.float32, -1.15, 1.15))
    offset = 0.5 * jax.random.normal(keys[3], (CIN,), jnp.float32)
    swing_scale = 0.5 * jax.random.normal(keys[4], (CIN,), jnp.float32)
    noise = jax.random.normal(keys[5], (ROWS, WIDTH, CIN), jnp.float32)
    amplitude = 0.7
    level = jnp.exp(amplitude * jnp.sin(angle + phases[0]) + 0.35 * jnp.sin(2.0 * angle + phases[1]) + rough)
    swing = jnp.sin(angle + phases[2]) * (1.0 + rough)
    profile = offset[None, :] * level[:, None] + swing_scale[None, :] * swing[:, None]
    values = noise * spread + profile[None, :, :]
    return jnp.clip(values, -10.0, 10.0).astype(jnp.bfloat16)


def block_levels(stream_key, shape, cuts, least, top_value):
    level, own = 1.0, jax.random.fold_in(stream_key, 6)
    for axis_at, parts in cuts:
        draws = jnp.exp(jax.random.uniform(jax.random.fold_in(own, axis_at), (parts,), jnp.float32, least / len(cuts), top_value / len(cuts)))
        level = level * jnp.repeat(draws, shape[axis_at] // parts).reshape([-1 if axis == axis_at else 1 for axis in range(len(shape))])
    return level


def bell_draw(key, extent, scale, limit, pieces=(), kind=jnp.bfloat16):
    gain = block_levels(key, extent, pieces, -0.22, 0.18) if pieces else 1.0
    drawn = jax.random.normal(key, extent, jnp.float32) * scale * gain
    return jnp.minimum(jnp.maximum(drawn, -limit), limit).astype(kind)


def setup_inputs(seed: int = 0) -> dict:
    arg_keys = jax.random.split(jax.random.key(seed), 8)
    features = draw_features(jax.random.fold_in(arg_keys[7], 71), 0)
    pointwise_weight = bell_draw(arg_keys[1], (CIN, OUT), CIN ** -0.5, 0.125, ((0, 16),))
    w_atrous = bell_draw(arg_keys[2], (3, 3, 3, CIN, OUT), (9 * CIN) ** -0.5, 0.046875, ((3, 16),))
    w_pool = bell_draw(arg_keys[3], (CIN, OUT), CIN ** -0.5, 0.125, ((0, 16),))
    w_proj = bell_draw(arg_keys[4], (5 * OUT, OUT), (5 * OUT) ** -0.5, 0.15625)
    norm_gain = jnp.clip(1.0 + 0.18 * jax.random.normal(arg_keys[5], (6, OUT), jnp.float32), 0.1, 1.9)
    norm_shift = bell_draw(arg_keys[6], (6, OUT), 0.5, 3.0, (), jnp.float32)
    return dict(features=features, pointwise_weight=pointwise_weight, w_atrous=w_atrous, w_pool=w_pool, w_proj=w_proj, norm_gain=norm_gain, norm_shift=norm_shift)


def branch_terms(padded, pointwise_weight, w_atrous, rows, cols, kernel_reach):
    centre = padded[kernel_reach:kernel_reach + rows, kernel_reach:kernel_reach + cols]
    chans = centre.shape[2]
    pixels = rows * cols
    terms = [jnp.dot(centre.reshape(pixels, chans), pointwise_weight, preferred_element_type=jnp.float32)]
    for pyramid_level in range(3):
        step_stride = (pyramid_level + 1) * BASE_DILATION
        taps = []
        for row_off in range(3):
            for col_off in range(3):
                top = kernel_reach + (row_off - 1) * step_stride
                left = kernel_reach + (col_off - 1) * step_stride
                taps.append(padded[top:top + rows, left:left + cols])
        stacked = jnp.concatenate(taps, axis=2).reshape(pixels, 9 * chans)
        kernel = w_atrous[pyramid_level].reshape(9 * chans, w_atrous.shape[-1])
        terms.append(jnp.dot(stacked, kernel, preferred_element_type=jnp.float32))
    return jnp.stack(terms, axis=1)


def reference(features, pointwise_weight, w_atrous, w_pool, w_proj, norm_gain, norm_shift):
    kernel_reach = 3 * BASE_DILATION
    group = CIN // N_CH

    def one_group(total, index):
        start = (index * group).astype(jnp.int32)
        local = lax.dynamic_slice_in_dim(features, start, group, 2)
        wrapped = jnp.concatenate([local[:, -kernel_reach:], local, local[:, :kernel_reach]], axis=1)
        padded = jnp.pad(wrapped, ((kernel_reach, kernel_reach), (0, 0), (0, 0)))
        point = lax.dynamic_slice_in_dim(pointwise_weight, start, group, 0)
        atrous = lax.dynamic_slice_in_dim(w_atrous, start, group, 3)
        part = branch_terms(padded, point, atrous, ROWS, WIDTH, kernel_reach).astype(jnp.bfloat16)
        part = lax.optimization_barrier(part)
        return total + part.astype(jnp.float32), None

    init = jnp.zeros((ROWS * WIDTH, 4, OUT), jnp.float32)
    branch_sum, _ = lax.scan(one_group, init, jnp.arange(N_CH, dtype=jnp.int32))
    branches = jax.nn.relu(branch_sum * norm_gain[:4] + norm_shift[:4]).astype(jnp.bfloat16)
    mean = jnp.sum(features.astype(jnp.float32), axis=(0, 1)) / (ROWS * WIDTH)
    pre = jnp.dot(mean, w_pool.astype(jnp.float32), precision=lax.Precision.HIGHEST)
    pooled = jax.nn.relu(norm_gain[4] * pre + norm_shift[4]).astype(jnp.bfloat16)
    blocks = w_proj.reshape(5, OUT, OUT)
    projected = jnp.einsum("pbk,bko->po", branches.astype(jnp.float32), blocks[:4].astype(jnp.float32))
    projected = projected + jnp.dot(pooled, blocks[4], preferred_element_type=jnp.float32)
    head = jax.nn.relu(norm_gain[5] * projected + norm_shift[5]).astype(jnp.bfloat16)
    return head.reshape(ROWS, WIDTH, OUT)
```

```python
import jax
import jax.numpy as jnp
from jax import lax
from jax.experimental import pallas as pl
from jax.experimental.pallas import tpu as pltpu
from jax.sharding import PartitionSpec as P

MESH_ID = pl.DeviceIdType.MESH
F32 = jnp.float32
BF16 = jnp.bfloat16

PAD = 48


def head_kernel(
    feat, pw, wa, wpool, wproj, gain, shift, out,
    xin, xb, part, cbuf, xbuf, zsrc, zown, zbuf, stage, obuf,
    pwv, wav, wprojv, poolsrc, poolbuf,
    ld_sem, ys, yr, hs, hr, cs, cr, xs, xr, zs, zr, os, orr, ps, pr,
):
    lon = lax.axis_index("lon")
    ch = lax.axis_index("ch")
    zl, y = lon // 4, lon % 4
    zh, x, c = ch // 8, (ch // 2) % 4, ch % 2

    def at(zl_=None, y_=None, zh_=None, x_=None, c_=None):
        zz = zl if zl_ is None else zl_
        yy = y if y_ is None else y_
        hh = zh if zh_ is None else zh_
        xx = x if x_ is None else x_
        cc = c if c_ is None else c_
        return (zz * 4 + yy, hh * 8 + xx * 2 + cc)

    k = c * 8 + x * 2 + zh
    kq, kt = k // 3, k % 3
    kg = 4 * kq + y
    y_dst = kg // 5
    slot = (kg % 5) * 3 + kt
    has_col = k < 15

    loads = [
        pltpu.make_async_copy(feat, xin, ld_sem.at[0]),
        pltpu.make_async_copy(pw, pwv, ld_sem.at[1]),
        pltpu.make_async_copy(wa, wav, ld_sem.at[2]),
        pltpu.make_async_copy(wproj, wprojv, ld_sem.at[3]),
    ]
    for load in loads:
        load.start()

    barrier = pltpu.get_barrier_semaphore()

    def hello(dev):
        pl.semaphore_signal(barrier, inc=1, device_id=dev, device_id_type=MESH_ID)

    for d in range(1, 8):
        hello(at(zl_=(zl + d) % 8))
    hello(at(zh_=1 - zh))
    hello(at(c_=1 - c))
    for d in range(1, 4):
        hello(at(y_=(y + d) % 4))
        hello(at(x_=(x + d) % 4))

    def source(i):
        g = 5 * y + i // 3
        kk = (g // 4) * 3 + i % 3
        return (g % 4), (kk % 2) * 8 + ((kk // 2) % 4) * 2 + kk // 8

    def greet(i, carry):
        sy, sch = source(i)

        @pl.when(jnp.logical_or(sy != y, sch != ch))
        def _():
            hello((zl * 4 + sy, sch))

        return carry

    lax.fori_loop(0, 15, greet, 0)

    zrow = jnp.zeros((3, PAD, 128), BF16)

    def clear(i, carry):
        xb[i, :, pl.ds(0, PAD), :] = zrow
        xb[i, :, pl.ds(PAD + 80, PAD), :] = zrow
        return carry

    lax.fori_loop(0, 11, clear, 0)
    for b in range(4):
        part[b, 15] = jnp.zeros((80, 256), BF16)

    loads[0].wait()
    xb[y + 3, :, pl.ds(PAD, 80), :] = xin[0:3]
    xb[y + 4, :, pl.ds(PAD, 80), :] = xin[12:15]

    def add_col(i, acc):
        return acc + jnp.sum(xin[i].astype(F32).reshape(10, 8, 128), axis=0)

    acc = lax.fori_loop(0, 15, add_col, jnp.zeros((8, 128), F32))
    colsum = jnp.sum(acc, axis=0, keepdims=True)
    pre = jnp.dot(
        jnp.broadcast_to(colsum, (8, 128)), wpool[...].astype(F32),
        precision=lax.Precision.HIGHEST, preferred_element_type=F32,
    )[0:1]
    poolsrc[0] = pre

    own_signals = jnp.where(y_dst == y, 15, 16) * has_col.astype(jnp.int32)
    pl.semaphore_wait(barrier, 15 + own_signals)

    def remote(src, dst, ssem, rsem, dev):
        return pltpu.make_async_remote_copy(
            src_ref=src, dst_ref=dst, send_sem=ssem, recv_sem=rsem,
            device_id=dev, device_id_type=MESH_ID,
        )

    rows = pl.ds(PAD, 80)
    ycopies = []
    for g in range(1, 4):
        q = (5 * y + g) // 4
        copy = remote(
            xin.at[pl.ds(3 * g, 3)], xb.at[q + 3, :, rows, :],
            ys.at[g - 1], yr.at[g - 1], at(y_=(y + g) % 4),
        )
        copy.start()
        ycopies.append(copy)
    psends = []

    def pool_send(stage_i, slot_i, dev):
        copy = remote(poolsrc.at[stage_i], poolbuf.at[slot_i], ps.at[slot_i], pr.at[slot_i], dev)
        copy.start()
        psends.append(copy)

    def pool_sum(stage_i, slots):
        tot = poolsrc[stage_i]
        for s in slots:
            psends[s].wait_recv()
            tot = tot + poolbuf[s]
        return tot

    for d in range(1, 4):
        pool_send(0, d - 1, at(y_=(y + d) % 4))
    for copy in ycopies:
        copy.wait_recv()

    halo = []
    for d in range(3):
        for side in range(2):
            q = (4 - d) if side == 0 else d
            q_to = q - 5 if side == 0 else q + 5
            dev = at(zl_=(zl + 1) % 8) if side == 0 else at(zl_=(zl + 7) % 8)
            copy = remote(
                xb.at[q + 3, :, rows, :], xb.at[q_to + 3, :, rows, :],
                hs.at[2 * d + side], hr.at[2 * d + side], dev,
            )
            copy.start()
            halo.append(copy)

    loads[1].wait()
    loads[2].wait()

    def compute(b):
        def body(q, carry):
            if b == 0:
                lhs = xb[q + 3, :, rows, :].reshape(240, 128)
                res = jnp.dot(lhs, pwv[...], preferred_element_type=F32)
            else:
                taps = []
                for ro in (-1, 0, 1):
                    for co in (-1, 0, 1):
                        taps.append(
                            xb[q + 3 + co * b, :, pl.ds(PAD + ro * b * 12, 80), :].reshape(240, 128)
                        )
                res = jnp.dot(
                    jnp.concatenate(taps, axis=1), wav[b - 1].reshape(1152, 256),
                    preferred_element_type=F32,
                )
            part[b, pl.ds(3 * q, 3)] = res.astype(BF16).reshape(3, 80, 256)
            return carry

        lax.fori_loop(0, 5, body, 0)

    core_copies, x_copies, z_copies = {}, {}, {}

    def core_send(b):
        copy = remote(
            part.at[b, pl.ds((1 - c) * 8, 8)], cbuf.at[b], cs.at[b], cr.at[b], at(c_=1 - c)
        )
        copy.start()
        core_copies[b] = copy

    def core_reduce(b):
        core_copies[b].wait_recv()

        def body(i, carry):
            mine = part[b, c * 8 + i].astype(F32) + cbuf[b, i].astype(F32)
            part[b, c * 8 + i] = mine.astype(BF16)
            return carry

        lax.fori_loop(0, 8, body, 0)
        x_copies[b] = []
        for d in range(1, 4):
            to = (x + d) % 4
            copy = remote(
                part.at[b, pl.ds(c * 8 + to * 2, 2)], xbuf.at[b, d - 1],
                xs.at[b, d - 1], xr.at[b, d - 1], at(x_=to),
            )
            copy.start()
            x_copies[b].append(copy)

    def x_reduce(b):
        for copy in x_copies[b]:
            copy.wait_recv()

        def total(j):
            t = part[b, c * 8 + x * 2 + j].astype(F32)
            for d in range(3):
                t = t + xbuf[b, d, j].astype(F32)
            return t

        zsrc[b] = total(1 - zh).astype(BF16)
        copy = remote(zsrc.at[b], zbuf.at[b], zs.at[b], zr.at[b], at(zh_=1 - zh))
        copy.start()
        z_copies[b] = copy
        zown[b] = total(zh)

    def halo_wait(d):
        halo[2 * d].wait_recv()
        halo[2 * d + 1].wait_recv()

    compute(0)
    core_send(0)
    poolsrc[1] = pool_sum(0, range(0, 3))
    for d in range(1, 8):
        pool_send(1, 2 + d, at(zl_=(zl + d) % 8))
    halo_wait(0)
    compute(1)
    core_send(1)
    core_reduce(0)
    halo_wait(1)
    compute(2)
    core_send(2)
    core_reduce(1)
    x_reduce(0)
    poolsrc[2] = pool_sum(1, range(3, 10))
    pool_send(2, 10, at(c_=1 - c))
    halo_wait(2)
    compute(3)
    core_send(3)
    core_reduce(2)
    poolsrc[3] = pool_sum(2, (10,))
    for d in range(1, 4):
        pool_send(3, 10 + d, at(x_=(x + d) % 4))
    x_reduce(1)
    core_reduce(3)
    poolsrc[4] = pool_sum(3, range(11, 14))
    pool_send(4, 14, at(zh_=1 - zh))
    x_reduce(2)
    x_reduce(3)
    loads[3].wait()

    proj = jnp.zeros((80, 256), F32)
    for b in range(4):
        z_copies[b].wait_recv()
        total = zown[b] + zbuf[b].astype(F32)
        act = jnp.maximum(total * gain[b : b + 1] + shift[b : b + 1], 0.0).astype(BF16)
        proj = proj + jnp.dot(act, wprojv[pl.ds(b * 256, 256), :], preferred_element_type=F32)
    pre_all = pool_sum(4, (14,)) * (1.0 / 38400.0)
    pooled = jnp.maximum(gain[4:5] * pre_all + shift[4:5], 0.0).astype(BF16)
    pool_term = jnp.dot(
        jnp.broadcast_to(pooled, (16, 256)), wprojv[pl.ds(1024, 256), :], preferred_element_type=F32
    )[0:1]
    head = jnp.maximum(gain[5:6] * (proj + pool_term) + shift[5:6], 0.0)
    head = jnp.concatenate([head, jnp.zeros((48, 256), F32)], axis=0)
    stage[...] = jnp.transpose(head).astype(BF16).reshape(16, 16, 128)

    def out_copy(d):
        return remote(stage.at[d], obuf.at[slot], os.at[d], orr.at[slot], (zl * 4 + y_dst, d))

    def is_self(d):
        return jnp.logical_and(y_dst == y, d == ch)

    def out_send(i, carry):
        d = (ch + i) % 16

        @pl.when(jnp.logical_and(has_col, jnp.logical_not(is_self(d))))
        def _():
            out_copy(d).start()

        return carry

    lax.fori_loop(0, 16, out_send, 0)

    @pl.when(jnp.logical_and(has_col, y_dst == y))
    def _():
        pltpu.make_async_copy(stage.at[ch], obuf.at[slot], orr.at[slot]).start()

    def out_recv(i, carry):
        pltpu.make_async_copy(stage.at[0], obuf.at[i], orr.at[i]).wait()
        return carry

    lax.fori_loop(0, 15, out_recv, 0)
    out[...] = obuf[:, :, 0:80]

    def out_sent(d, carry):
        @pl.when(jnp.logical_and(has_col, jnp.logical_not(is_self(d))))
        def _():
            out_copy(d).wait_send()

        return carry

    lax.fori_loop(0, 16, out_sent, 0)
    for copy in ycopies + halo + psends:
        copy.wait_send()
    for b in range(4):
        core_copies[b].wait_send()
        for copy in x_copies[b]:
            copy.wait_send()
        z_copies[b].wait_send()


def local(features, pointwise_weight, w_atrous, w_pool, w_proj, norm_gain, norm_shift):
    feat = jnp.transpose(features, (1, 0, 2))
    vmem = pl.BlockSpec(memory_space=pltpu.VMEM)
    hbm = pl.BlockSpec(memory_space=pl.ANY)
    dma = pltpu.SemaphoreType.DMA
    out = pl.pallas_call(
        head_kernel,
        out_shape=jax.ShapeDtypeStruct((15, 16, 80), BF16),
        in_specs=[hbm, hbm, hbm, vmem, hbm, vmem, vmem],
        out_specs=vmem,
        scratch_shapes=[
            pltpu.VMEM((15, 80, 128), BF16),
            pltpu.VMEM((11, 3, 80 + 2 * PAD, 128), BF16),
            pltpu.VMEM((4, 16, 80, 256), BF16),
            pltpu.VMEM((4, 8, 80, 256), BF16),
            pltpu.VMEM((4, 3, 2, 80, 256), BF16),
            pltpu.VMEM((4, 80, 256), BF16),
            pltpu.VMEM((4, 80, 256), F32),
            pltpu.VMEM((4, 80, 256), BF16),
            pltpu.VMEM((16, 16, 128), BF16),
            pltpu.VMEM((15, 16, 128), BF16),
            pltpu.VMEM((128, 256), BF16),
            pltpu.VMEM((3, 9, 128, 256), BF16),
            pltpu.VMEM((1280, 256), BF16),
            pltpu.VMEM((5, 1, 256), F32),
            pltpu.VMEM((15, 1, 256), F32),
            dma((4,)),
            dma((3,)), dma((3,)),
            dma((6,)), dma((6,)),
            dma((4,)), dma((4,)),
            dma((4, 3)), dma((4, 3)),
            dma((4,)), dma((4,)),
            dma((16,)), dma((15,)),
            dma((15,)), dma((15,)),
        ],
        compiler_params=pltpu.CompilerParams(collective_id=0, has_side_effects=True),
        name="aspp_head",
    )(
        feat, pointwise_weight, w_atrous.reshape(3, 9, 128, 256), w_pool, w_proj,
        norm_gain, norm_shift,
    )
    return jnp.transpose(out, (2, 0, 1))


def solution(mesh):
    return jax.shard_map(
        local,
        mesh=mesh,
        in_specs=(
            P(None, "lon", "ch"),
            P("ch", None),
            P(None, None, None, "ch", None),
            P("ch", None),
            P(),
            P(),
            P(),
        ),
        out_specs=P(None, "lon", "ch"),
        check_vma=False,
    )
```

```python
import jax
import jax.numpy as jnp
from jax import lax
from jax.experimental import pallas as pl
from jax.experimental.pallas import tpu as pltpu
from jax.sharding import PartitionSpec as P

MESH_ID = pl.DeviceIdType.MESH
F32 = jnp.float32
BF16 = jnp.bfloat16

PAD = 48


def head_kernel(
    feat, pw, wa, wpool, wproj, gain, shift, out,
    xin, xb, part, cbuf, xbuf, zsrc, zbuf, stage, obuf,
    pwv, wav, wprojv, poolsrc, poolbuf,
    ld_sem, ys, yr, hs, hr, cs, cr, xs, xr, zs, zr, os, orr, ps, pr,
):
    lon = lax.axis_index("lon")
    ch = lax.axis_index("ch")
    zl, y = lon // 4, lon % 4
    zh, x, c = ch // 8, (ch // 2) % 4, ch % 2
    z = zh * 8 + zl

    def at(zl_=None, y_=None, x_=None, c_=None):
        zz = zl if zl_ is None else zl_
        yy = y if y_ is None else y_
        xx = x if x_ is None else x_
        cc = c if c_ is None else c_
        return (zz * 4 + yy, zh * 8 + xx * 2 + cc)

    def at_z(dz):
        zz = (z + dz) % 16
        return ((zz % 8) * 4 + y, (zz // 8) * 8 + x * 2 + c)

    bit = ((z + 12) % 16) // 8
    k = c * 8 + x * 2 + bit
    kq, kt = k // 3, k % 3
    kg = 4 * kq + y
    y_dst = kg // 5
    slot = (kg % 5) * 3 + kt
    has_col = k < 15
    zl_dst = (zl + 4) % 8

    loads = [
        pltpu.make_async_copy(feat, xin, ld_sem.at[0]),
        pltpu.make_async_copy(pw, pwv, ld_sem.at[1]),
        pltpu.make_async_copy(wa, wav, ld_sem.at[2]),
        pltpu.make_async_copy(wproj, wprojv, ld_sem.at[3]),
    ]
    for load in loads:
        load.start()

    barrier = pltpu.get_barrier_semaphore()

    def hello(dev):
        pl.semaphore_signal(barrier, inc=1, device_id=dev, device_id_type=MESH_ID)

    east, west = at(zl_=(zl + 1) % 8), at(zl_=(zl + 7) % 8)
    hello(east)
    hello(west)
    hello(at_z(4))
    hello(at_z(12))

    def greet(i, carry):
        g = 5 * y + i // 3
        kk = (g // 4) * 3 + i % 3
        zz = (zl + 4 + 8 * (kk % 2)) % 16
        hello(((zz % 8) * 4 + g % 4, (zz // 8) * 8 + ((kk // 2) % 4) * 2 + kk // 8))
        return carry

    lax.fori_loop(0, 15, greet, 0)
    for d in range(1, 4):
        hello(at(y_=(y + d) % 4))
        hello(at(x_=(x + d) % 4))
    hello(at(c_=1 - c))

    zrow = jnp.zeros((3, PAD, 128), BF16)

    def clear(i, carry):
        xb[i, :, pl.ds(0, PAD), :] = zrow
        xb[i, :, pl.ds(PAD + 80, PAD), :] = zrow
        return carry

    lax.fori_loop(0, 11, clear, 0)
    for b in range(4):
        part[b, 15] = jnp.zeros((80, 256), BF16)

    loads[0].wait()

    def add_col(i, acc):
        return acc + jnp.sum(xin[i].astype(F32).reshape(10, 8, 128), axis=0)

    acc = lax.fori_loop(0, 15, add_col, jnp.zeros((8, 128), F32))
    colsum = jnp.sum(acc, axis=0, keepdims=True)
    pre = jnp.dot(
        jnp.broadcast_to(colsum, (8, 128)), wpool[...].astype(F32),
        precision=lax.Precision.HIGHEST, preferred_element_type=F32,
    )[0:1]
    poolsrc[0] = pre

    pl.semaphore_wait(barrier, 11 + 16 * has_col.astype(jnp.int32))

    def remote(src, dst, ssem, rsem, dev):
        return pltpu.make_async_remote_copy(
            src_ref=src, dst_ref=dst, send_sem=ssem, recv_sem=rsem,
            device_id=dev, device_id_type=MESH_ID,
        )

    rows = pl.ds(PAD, 80)
    ycopies = []
    for g in range(1, 4):
        q = (5 * y + g) // 4
        copy = remote(
            xin.at[pl.ds(3 * g, 3)], xb.at[q + 3, :, rows, :],
            ys.at[g - 1], yr.at[g - 1], at(y_=(y + g) % 4),
        )
        copy.start()
        ycopies.append(copy)
    psends = []

    def pool_send(src, slot_i, dev):
        copy = remote(src, poolbuf.at[slot_i], ps.at[slot_i], pr.at[slot_i], dev)
        copy.start()
        psends.append(copy)

    def pool_get(slot_i):
        psends[slot_i].wait_recv()
        return poolbuf[slot_i]

    for d in range(1, 4):
        pool_send(poolsrc.at[0], d - 1, at(y_=(y + d) % 4))
    xb[y + 3, :, rows, :] = xin[0:3]
    xb[y + 4, :, rows, :] = xin[12:15]
    for copy in ycopies:
        copy.wait_recv()

    halo = []
    for d in range(3):
        for side in range(2):
            q = (4 - d) if side == 0 else d
            q_to = q - 5 if side == 0 else q + 5
            copy = remote(
                xb.at[q + 3, :, rows, :], xb.at[q_to + 3, :, rows, :],
                hs.at[2 * d + side], hr.at[2 * d + side], east if side == 0 else west,
            )
            copy.start()
            halo.append(copy)

    late = jnp.where(zl == 0, 0, 1)

    def halo_wait(d, side):
        remote(
            xb.at[3, :, rows, :], xb.at[4, :, rows, :],
            hs.at[2 * d + side], hr.at[2 * d + side], east,
        ).wait_recv()

    loads[1].wait()
    loads[2].wait()

    def compute(b, lo, hi):
        def body(j, carry):
            q = jnp.where(late == 1, j, 4 - j)
            if b == 0:
                lhs = xb[q + 3, :, rows, :].reshape(240, 128)
                res = jnp.dot(lhs, pwv[...], preferred_element_type=F32)
            else:
                taps = []
                for ro in (-1, 0, 1):
                    for co in (-1, 0, 1):
                        taps.append(
                            xb[q + 3 + co * b, :, pl.ds(PAD + ro * b * 12, 80), :].reshape(240, 128)
                        )
                res = jnp.dot(
                    jnp.concatenate(taps, axis=1), wav[b - 1].reshape(1152, 256),
                    preferred_element_type=F32,
                )
            part[b, pl.ds(3 * q, 3)] = res.astype(BF16).reshape(3, 80, 256)
            return carry

        lax.fori_loop(lo, hi, body, 0)

    core_copies, x_copies, z_copies = {}, {}, {}

    def core_send(b):
        copy = remote(
            part.at[b, pl.ds((1 - c) * 8, 8)], cbuf.at[b], cs.at[b], cr.at[b], at(c_=1 - c)
        )
        copy.start()
        core_copies[b] = copy

    def core_reduce(b):
        core_copies[b].wait_recv()

        def body(i, carry):
            mine = part[b, c * 8 + i].astype(F32) + cbuf[b, i].astype(F32)
            part[b, c * 8 + i] = mine.astype(BF16)
            return carry

        lax.fori_loop(0, 8, body, 0)
        x_copies[b] = []
        for d in range(1, 4):
            to = (x + d) % 4
            copy = remote(
                part.at[b, pl.ds(c * 8 + to * 2, 2)], xbuf.at[b, d - 1],
                xs.at[b, d - 1], xr.at[b, d - 1], at(x_=to),
            )
            copy.start()
            x_copies[b].append(copy)

    def x_reduce(b):
        for copy in x_copies[b]:
            copy.wait_recv()
        for j in range(2):
            t = part[b, c * 8 + x * 2 + j].astype(F32)
            for d in range(3):
                t = t + xbuf[b, d, j].astype(F32)
            zsrc[b, j] = t.astype(BF16)
        z_copies[b] = []
        for way in range(2):
            j = zh if way == 0 else 1 - zh
            copy = remote(
                zsrc.at[b, j], zbuf.at[b, way], zs.at[b, way], zr.at[b, way],
                at_z(4) if way == 0 else at_z(12),
            )
            copy.start()
            z_copies[b].append(copy)

    compute(0, 0, 5)
    core_send(0)
    own = poolsrc[0] + pool_get(0) + pool_get(1) + pool_get(2)
    poolsrc[1] = own
    pool_send(poolsrc.at[1], 3, east)
    pool_send(poolsrc.at[1], 4, west)
    core_reduce(0)
    for b in range(1, 4):
        halo_wait(b - 1, 1 - late)
        compute(b, 0, 5 - b)
    halo_wait(0, late)
    compute(1, 4, 5)
    core_send(1)
    x_reduce(0)
    three = own + pool_get(3) + pool_get(4)
    pool_send(poolbuf.at[4], 5, west)
    core_reduce(1)
    halo_wait(1, late)
    compute(2, 3, 5)
    core_send(2)
    x_reduce(1)
    core_reduce(2)
    halo_wait(2, late)
    compute(3, 2, 5)
    core_send(3)
    four = three + pool_get(5)
    poolsrc[2] = four
    pool_send(poolsrc.at[2], 6, at_z(4))
    pool_send(poolsrc.at[2], 7, at_z(12))
    x_reduce(2)
    core_reduce(3)
    twelve = four + pool_get(6) + pool_get(7)
    pool_send(poolbuf.at[7], 8, at_z(12))
    x_reduce(3)
    all_z = twelve + pool_get(8)
    poolsrc[3] = all_z
    pool_send(poolsrc.at[3], 9, at(c_=1 - c))
    loads[3].wait()

    proj = jnp.zeros((80, 256), F32)
    for b in range(4):
        if b == 2:
            both = all_z + pool_get(9)
            poolsrc[4] = both
            for d in range(1, 4):
                pool_send(poolsrc.at[4], 9 + d, at(x_=(x + d) % 4))
        if b == 3:
            pre_all = both + pool_get(10) + pool_get(11) + pool_get(12)
            pre_all = pre_all * (1.0 / 38400.0)
            pooled = jnp.maximum(gain[4:5] * pre_all + shift[4:5], 0.0).astype(BF16)
            pool_term = jnp.dot(
                jnp.broadcast_to(pooled, (16, 256)), wprojv[pl.ds(1024, 256), :],
                preferred_element_type=F32,
            )[0:1]
        for copy in z_copies[b]:
            copy.wait_recv()
        total = zbuf[b, 0].astype(F32) + zbuf[b, 1].astype(F32)
        act = jnp.maximum(total * gain[b : b + 1] + shift[b : b + 1], 0.0).astype(BF16)
        proj = proj + jnp.dot(act, wprojv[pl.ds(b * 256, 256), :], preferred_element_type=F32)
    head = jnp.maximum(gain[5:6] * (proj + pool_term) + shift[5:6], 0.0)
    head = jnp.concatenate([head, jnp.zeros((48, 256), F32)], axis=0)
    stage[...] = jnp.transpose(head).astype(BF16).reshape(16, 16, 128)

    def out_copy(d):
        return remote(stage.at[d], obuf.at[slot], os.at[d], orr.at[slot], (zl_dst * 4 + y_dst, d))

    def out_send(i, carry):
        @pl.when(has_col)
        def _():
            out_copy((ch + i) % 16).start()

        return carry

    lax.fori_loop(0, 16, out_send, 0)
    for copy in ycopies + halo + psends:
        copy.wait_send()
    for b in range(4):
        core_copies[b].wait_send()
        for copy in x_copies[b] + z_copies[b]:
            copy.wait_send()

    def out_recv(i, carry):
        remote(stage.at[0], obuf.at[i], os.at[0], orr.at[i], east).wait_recv()
        return carry

    lax.fori_loop(0, 15, out_recv, 0)
    out[...] = obuf[:, :, 0:80]

    def out_sent(d, carry):
        @pl.when(has_col)
        def _():
            out_copy(d).wait_send()

        return carry

    lax.fori_loop(0, 16, out_sent, 0)


def local(features, pointwise_weight, w_atrous, w_pool, w_proj, norm_gain, norm_shift):
    feat = jnp.transpose(features, (1, 0, 2))
    vmem = pl.BlockSpec(memory_space=pltpu.VMEM)
    hbm = pl.BlockSpec(memory_space=pl.ANY)
    dma = pltpu.SemaphoreType.DMA
    out = pl.pallas_call(
        head_kernel,
        out_shape=jax.ShapeDtypeStruct((15, 16, 80), BF16),
        in_specs=[hbm, hbm, hbm, vmem, hbm, vmem, vmem],
        out_specs=vmem,
        scratch_shapes=[
            pltpu.VMEM((15, 80, 128), BF16),
            pltpu.VMEM((11, 3, 80 + 2 * PAD, 128), BF16),
            pltpu.VMEM((4, 16, 80, 256), BF16),
            pltpu.VMEM((4, 8, 80, 256), BF16),
            pltpu.VMEM((4, 3, 2, 80, 256), BF16),
            pltpu.VMEM((4, 2, 80, 256), BF16),
            pltpu.VMEM((4, 2, 80, 256), BF16),
            pltpu.VMEM((16, 16, 128), BF16),
            pltpu.VMEM((15, 16, 128), BF16),
            pltpu.VMEM((128, 256), BF16),
            pltpu.VMEM((3, 9, 128, 256), BF16),
            pltpu.VMEM((1280, 256), BF16),
            pltpu.VMEM((5, 1, 256), F32),
            pltpu.VMEM((13, 1, 256), F32),
            dma((4,)),
            dma((3,)), dma((3,)),
            dma((6,)), dma((6,)),
            dma((4,)), dma((4,)),
            dma((4, 3)), dma((4, 3)),
            dma((4, 2)), dma((4, 2)),
            dma((16,)), dma((15,)),
            dma((13,)), dma((13,)),
        ],
        compiler_params=pltpu.CompilerParams(collective_id=0, has_side_effects=True),
        name="aspp_head",
    )(
        feat, pointwise_weight, w_atrous.reshape(3, 9, 128, 256), w_pool, w_proj,
        norm_gain, norm_shift,
    )
    return jnp.transpose(out, (2, 0, 1))


def solution(mesh):
    return jax.shard_map(
        local,
        mesh=mesh,
        in_specs=(
            P(None, "lon", "ch"),
            P("ch", None),
            P(None, None, None, "ch", None),
            P("ch", None),
            P(),
            P(),
            P(),
        ),
        out_specs=P(None, "lon", "ch"),
        check_vma=False,
    )
```

```python
import jax
import jax.numpy as jnp
from jax import lax
from jax.experimental import pallas as pl
from jax.experimental.pallas import tpu as pltpu
from jax.sharding import PartitionSpec as P

MESH_ID = pl.DeviceIdType.MESH
F32 = jnp.float32
BF16 = jnp.bfloat16

PAD = 48


def head_kernel(
    feat, pw, wa, wpool, wproj, gain, shift, out,
    xin, xb, part, cbuf, xbuf, zsrc, zbuf, stage, obuf,
    pwv, wav, wprojv, poolsrc, poolbuf,
    ld_sem, ys, yr, hs, hr, cs, cr, xs, xr, zs, zr, os, orr, ps, pr,
):
    lon = lax.axis_index("lon")
    ch = lax.axis_index("ch")
    zl, y = lon // 4, lon % 4
    zh, x, c = ch // 8, (ch // 2) % 4, ch % 2
    z = zh * 8 + zl

    def at(zl_=None, y_=None, x_=None, c_=None):
        zz = zl if zl_ is None else zl_
        yy = y if y_ is None else y_
        xx = x if x_ is None else x_
        cc = c if c_ is None else c_
        return (zz * 4 + yy, zh * 8 + xx * 2 + cc)

    def at_z(dz):
        zz = (z + dz) % 16
        return ((zz % 8) * 4 + y, (zz // 8) * 8 + x * 2 + c)

    bit = ((z + 12) % 16) // 8
    zl_dst = (zl + 4) % 8
    k = bit * 8 + x * 2 + c
    kj, kt = k // 3, k % 3
    kq = jnp.where(zl_dst == 0, 4 - kj, kj)
    kg = 4 * kq + y
    y_dst = kg // 5
    slot = (kg % 5) * 3 + kt
    has_col = k < 15

    loads = [
        pltpu.make_async_copy(feat, xin, ld_sem.at[0]),
        pltpu.make_async_copy(pw, pwv, ld_sem.at[1]),
        pltpu.make_async_copy(wa, wav, ld_sem.at[2]),
        pltpu.make_async_copy(wproj, wprojv, ld_sem.at[3]),
    ]
    for load in loads:
        load.start()

    barrier = pltpu.get_barrier_semaphore()

    def hello(dev):
        pl.semaphore_signal(barrier, inc=1, device_id=dev, device_id_type=MESH_ID)

    east, west = at(zl_=(zl + 1) % 8), at(zl_=(zl + 7) % 8)
    hello(east)
    hello(west)
    hello(at_z(4))
    hello(at_z(12))

    def greet(i, carry):
        g = 5 * y + i // 3
        kk = jnp.where(zl == 0, 4 - g // 4, g // 4) * 3 + i % 3
        zz = (zl + 4 + 8 * (kk // 8)) % 16
        hello(((zz % 8) * 4 + g % 4, (zz // 8) * 8 + kk % 8))
        return carry

    lax.fori_loop(0, 15, greet, 0)
    for d in range(1, 4):
        hello(at(y_=(y + d) % 4))
        hello(at(x_=(x + d) % 4))
    hello(at(c_=1 - c))

    zrow = jnp.zeros((3, PAD, 128), BF16)

    def clear(i, carry):
        xb[i, :, pl.ds(0, PAD), :] = zrow
        xb[i, :, pl.ds(PAD + 80, PAD), :] = zrow
        return carry

    lax.fori_loop(0, 11, clear, 0)
    for b in range(4):
        part[b, 1, 1, 3] = jnp.zeros((80, 256), BF16)

    loads[0].wait()

    def add_col(i, acc):
        return acc + jnp.sum(xin[i].astype(F32).reshape(10, 8, 128), axis=0)

    acc = lax.fori_loop(0, 15, add_col, jnp.zeros((8, 128), F32))
    colsum = jnp.sum(acc, axis=0, keepdims=True)
    pre = jnp.dot(
        jnp.broadcast_to(colsum, (8, 128)), wpool[...].astype(F32),
        precision=lax.Precision.HIGHEST, preferred_element_type=F32,
    )[0:1]
    poolsrc[0] = pre

    pl.semaphore_wait(barrier, 11 + 16 * has_col.astype(jnp.int32))

    def remote(src, dst, ssem, rsem, dev):
        return pltpu.make_async_remote_copy(
            src_ref=src, dst_ref=dst, send_sem=ssem, recv_sem=rsem,
            device_id=dev, device_id_type=MESH_ID,
        )

    rows = pl.ds(PAD, 80)
    ycopies = []
    for g in range(1, 4):
        q = (5 * y + g) // 4
        copy = remote(
            xin.at[pl.ds(3 * g, 3)], xb.at[q + 3, :, rows, :],
            ys.at[g - 1], yr.at[g - 1], at(y_=(y + g) % 4),
        )
        copy.start()
        ycopies.append(copy)
    psends = []

    def pool_send(src, slot_i, dev):
        copy = remote(src, poolbuf.at[slot_i], ps.at[slot_i], pr.at[slot_i], dev)
        copy.start()
        psends.append(copy)

    def pool_get(slot_i):
        psends[slot_i].wait_recv()
        return poolbuf[slot_i]

    for d in range(1, 4):
        pool_send(poolsrc.at[0], d - 1, at(y_=(y + d) % 4))
    xb[y + 3, :, rows, :] = xin[0:3]
    xb[y + 4, :, rows, :] = xin[12:15]
    for copy in ycopies:
        copy.wait_recv()

    halo = []
    for d in range(3):
        for side in range(2):
            q = (4 - d) if side == 0 else d
            q_to = q - 5 if side == 0 else q + 5
            copy = remote(
                xb.at[q + 3, :, rows, :], xb.at[q_to + 3, :, rows, :],
                hs.at[2 * d + side], hr.at[2 * d + side], east if side == 0 else west,
            )
            copy.start()
            halo.append(copy)

    late = jnp.where(zl == 0, 0, 1)

    def halo_wait(d, side):
        remote(
            xb.at[3, :, rows, :], xb.at[4, :, rows, :],
            hs.at[2 * d + side], hr.at[2 * d + side], east,
        ).wait_recv()

    loads[1].wait()
    loads[2].wait()

    def compute(b, lo, hi):
        def body(j, carry):
            q = jnp.where(late == 1, j, 4 - j)
            if b == 0:
                lhs = xb[q + 3, :, rows, :].reshape(240, 128)
                res = jnp.dot(lhs, pwv[...], preferred_element_type=F32)
            else:
                taps = []
                for ro in (-1, 0, 1):
                    for co in (-1, 0, 1):
                        taps.append(
                            xb[q + 3 + co * b, :, pl.ds(PAD + ro * b * 12, 80), :].reshape(240, 128)
                        )
                res = jnp.dot(
                    jnp.concatenate(taps, axis=1), wav[b - 1].reshape(1152, 256),
                    preferred_element_type=F32,
                )
            res = res.astype(BF16).reshape(3, 80, 256)
            for t in range(3):
                s = 3 * j + t
                part[b, s % 2, s // 8, (s // 2) % 4] = res[t]
            return carry

        lax.fori_loop(lo, hi, body, 0)

    core_copies, x_copies, z_copies = {}, {}, {}

    def core_send(b, h):
        copy = remote(
            part.at[b, 1 - c, h], cbuf.at[b, h], cs.at[b, h], cr.at[b, h], at(c_=1 - c)
        )
        copy.start()
        core_copies[b, h] = copy

    def core_reduce(b, h):
        core_copies[b, h].wait_recv()

        def body(i, carry):
            mine = part[b, c, h, i].astype(F32) + cbuf[b, h, i].astype(F32)
            part[b, c, h, i] = mine.astype(BF16)
            return carry

        lax.fori_loop(0, 4, body, 0)
        x_copies[b, h] = []
        for d in (2, 1, 3):
            to = (x + d) % 4
            copy = remote(
                part.at[b, c, h, to], xbuf.at[b, h, d - 1],
                xs.at[b, h, d - 1], xr.at[b, h, d - 1], at(x_=to),
            )
            copy.start()
            x_copies[b, h].append(copy)

    def x_reduce(b, h):
        for copy in x_copies[b, h]:
            copy.wait_recv()
        t = part[b, c, h, x].astype(F32)
        for d in range(3):
            t = t + xbuf[b, h, d].astype(F32)
        zsrc[b, h] = t.astype(BF16)
        up = (zh == h).astype(jnp.int32)
        z_copies[b, h] = remote(
            zsrc.at[b, h], zbuf.at[b, 1 - up], zs.at[b, h], zr.at[b, 1 - up], at_z(12 - 8 * up)
        )
        z_copies[b, h].start()

    compute(0, 0, 5)
    core_send(0, 0)
    core_send(0, 1)
    own = poolsrc[0] + pool_get(0) + pool_get(1) + pool_get(2)
    poolsrc[1] = own
    pool_send(poolsrc.at[1], 3, east)
    pool_send(poolsrc.at[1], 4, west)
    core_reduce(0, 0)
    core_reduce(0, 1)
    halo_wait(0, 1 - late)
    compute(1, 0, 4)
    core_send(1, 0)
    halo_wait(1, 1 - late)
    compute(2, 0, 3)
    core_send(2, 0)
    core_reduce(1, 0)
    x_reduce(0, 0)
    x_reduce(0, 1)
    halo_wait(2, 1 - late)
    compute(3, 0, 2)
    core_reduce(2, 0)
    x_reduce(1, 0)
    halo_wait(0, late)
    compute(3, 2, 3)
    core_send(3, 0)
    compute(1, 4, 5)
    core_send(1, 1)
    core_reduce(3, 0)
    halo_wait(1, late)
    compute(2, 3, 5)
    core_send(2, 1)
    core_reduce(1, 1)
    x_reduce(2, 0)
    three = own + pool_get(3) + pool_get(4)
    pool_send(poolbuf.at[4], 5, west)
    halo_wait(2, late)
    compute(3, 3, 5)
    core_send(3, 1)
    core_reduce(2, 1)
    x_reduce(3, 0)
    core_reduce(3, 1)
    x_reduce(1, 1)
    x_reduce(2, 1)
    four = three + pool_get(5)
    poolsrc[2] = four
    pool_send(poolsrc.at[2], 6, at_z(4))
    pool_send(poolsrc.at[2], 7, at_z(12))
    x_reduce(3, 1)
    twelve = four + pool_get(6) + pool_get(7)
    pool_send(poolbuf.at[7], 8, at_z(12))
    loads[3].wait()

    proj = jnp.zeros((80, 256), F32)
    for b in range(4):
        if b == 2:
            all_z = twelve + pool_get(8)
            poolsrc[3] = all_z
            pool_send(poolsrc.at[3], 9, at(c_=1 - c))
            both = all_z + pool_get(9)
            poolsrc[4] = both
            for d in range(1, 4):
                pool_send(poolsrc.at[4], 9 + d, at(x_=(x + d) % 4))
        if b == 3:
            pre_all = both + pool_get(10) + pool_get(11) + pool_get(12)
            pre_all = pre_all * (1.0 / 38400.0)
            pooled = jnp.maximum(gain[4:5] * pre_all + shift[4:5], 0.0).astype(BF16)
            pool_term = jnp.dot(
                jnp.broadcast_to(pooled, (16, 256)), wprojv[pl.ds(1024, 256), :],
                preferred_element_type=F32,
            )[0:1]
        for way in range(2):
            remote(
                zsrc.at[b, 0], zbuf.at[b, way], zs.at[b, 0], zr.at[b, way], at_z(4)
            ).wait_recv()
        total = zbuf[b, 0].astype(F32) + zbuf[b, 1].astype(F32)
        act = jnp.maximum(total * gain[b : b + 1] + shift[b : b + 1], 0.0).astype(BF16)
        proj = proj + jnp.dot(act, wprojv[pl.ds(b * 256, 256), :], preferred_element_type=F32)
    head = jnp.maximum(gain[5:6] * (proj + pool_term) + shift[5:6], 0.0)
    head = jnp.concatenate([head, jnp.zeros((48, 256), F32)], axis=0)
    stage[...] = jnp.transpose(head).astype(BF16).reshape(16, 16, 128)

    def out_copy(d):
        return remote(stage.at[d], obuf.at[slot], os.at[d], orr.at[slot], (zl_dst * 4 + y_dst, d))

    def out_send(i, carry):
        @pl.when(has_col)
        def _():
            out_copy((ch + i) % 16).start()

        return carry

    lax.fori_loop(0, 16, out_send, 0)
    for copy in ycopies + halo + psends:
        copy.wait_send()
    for u in core_copies:
        for copy in [core_copies[u], z_copies[u]] + x_copies[u]:
            copy.wait_send()

    def out_recv(i, carry):
        remote(stage.at[0], obuf.at[i], os.at[0], orr.at[i], east).wait_recv()
        return carry

    lax.fori_loop(0, 15, out_recv, 0)
    out[...] = obuf[:, :, 0:80]

    def out_sent(d, carry):
        @pl.when(has_col)
        def _():
            out_copy(d).wait_send()

        return carry

    lax.fori_loop(0, 16, out_sent, 0)


def local(features, pointwise_weight, w_atrous, w_pool, w_proj, norm_gain, norm_shift):
    feat = jnp.transpose(features, (1, 0, 2))
    vmem = pl.BlockSpec(memory_space=pltpu.VMEM)
    hbm = pl.BlockSpec(memory_space=pl.ANY)
    dma = pltpu.SemaphoreType.DMA
    out = pl.pallas_call(
        head_kernel,
        out_shape=jax.ShapeDtypeStruct((15, 16, 80), BF16),
        in_specs=[hbm, hbm, hbm, vmem, hbm, vmem, vmem],
        out_specs=vmem,
        scratch_shapes=[
            pltpu.VMEM((15, 80, 128), BF16),
            pltpu.VMEM((11, 3, 80 + 2 * PAD, 128), BF16),
            pltpu.VMEM((4, 2, 2, 4, 80, 256), BF16),
            pltpu.VMEM((4, 2, 4, 80, 256), BF16),
            pltpu.VMEM((4, 2, 3, 80, 256), BF16),
            pltpu.VMEM((4, 2, 80, 256), BF16),
            pltpu.VMEM((4, 2, 80, 256), BF16),
            pltpu.VMEM((16, 16, 128), BF16),
            pltpu.VMEM((15, 16, 128), BF16),
            pltpu.VMEM((128, 256), BF16),
            pltpu.VMEM((3, 9, 128, 256), BF16),
            pltpu.VMEM((1280, 256), BF16),
            pltpu.VMEM((5, 1, 256), F32),
            pltpu.VMEM((13, 1, 256), F32),
            dma((4,)),
            dma((3,)), dma((3,)),
            dma((6,)), dma((6,)),
            dma((4, 2)), dma((4, 2)),
            dma((4, 2, 3)), dma((4, 2, 3)),
            dma((4, 2)), dma((4, 2)),
            dma((16,)), dma((15,)),
            dma((13,)), dma((13,)),
        ],
        compiler_params=pltpu.CompilerParams(collective_id=0, has_side_effects=True),
        name="aspp_head",
    )(
        feat, pointwise_weight, w_atrous.reshape(3, 9, 128, 256), w_pool, w_proj,
        norm_gain, norm_shift,
    )
    return jnp.transpose(out, (2, 0, 1))


def solution(mesh):
    return jax.shard_map(
        local,
        mesh=mesh,
        in_specs=(
            P(None, "lon", "ch"),
            P("ch", None),
            P(None, None, None, "ch", None),
            P("ch", None),
            P(),
            P(),
            P(),
        ),
        out_specs=P(None, "lon", "ch"),
        check_vma=False,
    )
```

```python
import jax
import jax.numpy as jnp
from jax import lax
from jax.experimental import pallas as pl
from jax.experimental.pallas import tpu as pltpu
from jax.sharding import PartitionSpec as P

MESH_ID = pl.DeviceIdType.MESH
F32 = jnp.float32
BF16 = jnp.bfloat16

PAD = 48


def head_kernel(
    feat, pw, wa, wpool, wproj, gain, shift, out,
    xin, xb, part, cbuf, xbuf, zsrc, zbuf, stage, obuf,
    pwv, wav, wprojv, poolsrc, poolbuf,
    part2, cbuf2, xbuf2, zsrc2, zbuf2, acc,
    ld_sem, ys, yr, hs, hr, cs, cr, xs, xr, zs, zr, os, orr, ps, pr,
    cs2, cr2, xs2, xr2, zs2, zr2,
):
    lon = lax.axis_index("lon")
    ch = lax.axis_index("ch")
    zl, y = lon // 4, lon % 4
    zh, x, c = ch // 8, (ch // 2) % 4, ch % 2
    z = zh * 8 + zl

    def at(zl_=None, y_=None, x_=None, c_=None):
        zz = zl if zl_ is None else zl_
        yy = y if y_ is None else y_
        xx = x if x_ is None else x_
        cc = c if c_ is None else c_
        return (zz * 4 + yy, zh * 8 + xx * 2 + cc)

    def at_z(dz):
        zz = (z + dz) % 16
        return ((zz % 8) * 4 + y, (zz // 8) * 8 + x * 2 + c)

    bit = ((z + 12) % 16) // 8
    zl_dst = (zl + 4) % 8
    k = bit * 8 + x * 2 + c
    kj, kt = k // 3, k % 3
    kq = jnp.where(zl_dst == 0, 4 - kj, kj)
    kg = 4 * kq + y
    y_dst = kg // 5
    slot = (kg % 5) * 3 + kt
    has_col = k < 15

    loads = [
        pltpu.make_async_copy(feat, xin, ld_sem.at[0]),
        pltpu.make_async_copy(pw, pwv, ld_sem.at[1]),
        pltpu.make_async_copy(wa, wav, ld_sem.at[2]),
        pltpu.make_async_copy(wproj, wprojv, ld_sem.at[3]),
    ]
    for load in loads:
        load.start()

    barrier = pltpu.get_barrier_semaphore()

    def hello(dev):
        pl.semaphore_signal(barrier, inc=1, device_id=dev, device_id_type=MESH_ID)

    east, west = at(zl_=(zl + 1) % 8), at(zl_=(zl + 7) % 8)
    edge = jnp.logical_or(zl == 0, zl == 7)
    edge_owner = jnp.logical_or(zl == 3, zl == 4)

    @pl.when(edge_owner)
    def _():
        far = jnp.where(zl == 4, 7, 0) * 4 + y
        hello((far, x * 2 + c))
        hello((far, 8 + x * 2 + c))

    @pl.when(zl < 7)
    def _():
        hello(east)

    @pl.when(zl > 0)
    def _():
        hello(west)

    hello(at_z(4))
    hello(at_z(12))

    def greet(i, carry):
        g = 5 * y + i // 3
        kk = jnp.where(zl == 0, 4 - g // 4, g // 4) * 3 + i % 3
        zz = (zl + 4 + 8 * (kk // 8)) % 16
        hello(((zz % 8) * 4 + g % 4, (zz // 8) * 8 + kk % 8))
        return carry

    lax.fori_loop(0, 15, greet, 0)
    for d in range(1, 4):
        hello(at(y_=(y + d) % 4))
        hello(at(x_=(x + d) % 4))
    hello(at(c_=1 - c))

    zrow = jnp.zeros((3, PAD, 128), BF16)

    def clear(i, carry):
        xb[i, :, pl.ds(0, PAD), :] = zrow
        xb[i, :, pl.ds(PAD + 80, PAD), :] = zrow
        return carry

    lax.fori_loop(0, 11, clear, 0)
    for b in range(4):
        part[b, 1, 1, 3] = jnp.zeros((80, 256), BF16)

    blank = jnp.zeros((3, 80, 128), BF16)

    @pl.when(edge)
    def _():
        for d in range(3):
            xb[jnp.where(zl == 0, d, 8 + d), :, pl.ds(PAD, 80), :] = blank
        part2[1, 0, 1, 0] = jnp.zeros((80, 256), BF16)
        for b in range(3):
            part2[b, 1, 1, 3] = jnp.zeros((80, 256), BF16)

    loads[0].wait()

    def add_col(i, tot):
        return tot + jnp.sum(xin[i].astype(F32).reshape(10, 8, 128), axis=0)

    sums = lax.fori_loop(0, 15, add_col, jnp.zeros((8, 128), F32))
    colsum = jnp.sum(sums, axis=0, keepdims=True)
    pre = jnp.dot(
        jnp.broadcast_to(colsum, (8, 128)), wpool[...].astype(F32),
        precision=lax.Precision.HIGHEST, preferred_element_type=F32,
    )[0:1]
    poolsrc[0] = pre

    pl.semaphore_wait(barrier, 11 + edge.astype(jnp.int32) + 16 * has_col.astype(jnp.int32))

    def remote(src, dst, ssem, rsem, dev):
        return pltpu.make_async_remote_copy(
            src_ref=src, dst_ref=dst, send_sem=ssem, recv_sem=rsem,
            device_id=dev, device_id_type=MESH_ID,
        )

    rows = pl.ds(PAD, 80)
    ycopies = []
    for g in range(1, 4):
        q = (5 * y + g) // 4
        copy = remote(
            xin.at[pl.ds(3 * g, 3)], xb.at[q + 3, :, rows, :],
            ys.at[g - 1], yr.at[g - 1], at(y_=(y + g) % 4),
        )
        copy.start()
        ycopies.append(copy)
    psends = {}

    def pool_send(src, slot_i, dev):
        psends[slot_i] = remote(src, poolbuf.at[slot_i], ps.at[slot_i], pr.at[slot_i], dev)
        psends[slot_i].start()

    def pool_get(slot_i):
        psends[slot_i].wait_recv()
        return poolbuf[slot_i]

    for d in range(1, 4):
        pool_send(poolsrc.at[0], d - 1, at(y_=(y + d) % 4))
    xb[y + 3, :, rows, :] = xin[0:3]
    xb[y + 4, :, rows, :] = xin[12:15]
    for copy in ycopies:
        copy.wait_recv()

    def halo_copy(d, side):
        q = (4 - d) if side == 0 else d
        q_to = q - 5 if side == 0 else q + 5
        return remote(
            xb.at[q + 3, :, rows, :], xb.at[q_to + 3, :, rows, :],
            hs.at[2 * d + side], hr.at[2 * d + side], east if side == 0 else west,
        )

    halo_out = (zl < 7, zl > 0)
    halo_in = (zl > 0, zl < 7)
    for d in range(3):
        for side in range(2):
            pl.when(halo_out[side])(halo_copy(d, side).start)

    def halo_wait(d):
        for side in range(2):
            pl.when(halo_in[side])(halo_copy(d, side).wait_recv)

    late = jnp.where(zl == 0, 0, 1)

    own = poolsrc[0] + pool_get(0) + pool_get(1) + pool_get(2)
    poolsrc[1] = own
    pool_send(poolsrc.at[1], 3, at_z(4))
    pool_send(poolsrc.at[1], 4, at_z(12))
    loads[1].wait()
    loads[2].wait()

    def compute(b, lo, hi):
        def body(j, carry):
            q = jnp.where(late == 1, j, 4 - j)
            if b == 0:
                lhs = xb[q + 3, :, rows, :].reshape(240, 128)
                res = jnp.dot(lhs, pwv[...], preferred_element_type=F32)
            else:
                taps = []
                for ro in (-1, 0, 1):
                    for co in (-1, 0, 1):
                        taps.append(
                            xb[q + 3 + co * b, :, pl.ds(PAD + ro * b * 12, 80), :].reshape(240, 128)
                        )
                res = jnp.dot(
                    jnp.concatenate(taps, axis=1), wav[b - 1].reshape(1152, 256),
                    preferred_element_type=F32,
                )
            res = res.astype(BF16).reshape(3, 80, 256)
            for t in range(3):
                s = 3 * j + t
                part[b, s % 2, s // 8, (s // 2) % 4] = res[t]
            return carry

        lax.fori_loop(lo, hi, body, 0)

    core_copies, x_copies, z_copies = {}, {}, {}

    def core_send(b, h):
        copy = remote(
            part.at[b, 1 - c, h], cbuf.at[b, h], cs.at[b, h], cr.at[b, h], at(c_=1 - c)
        )
        copy.start()
        core_copies[b, h] = copy

    def core_reduce(b, h):
        core_copies[b, h].wait_recv()

        def body(i, carry):
            mine = part[b, c, h, i].astype(F32) + cbuf[b, h, i].astype(F32)
            part[b, c, h, i] = mine.astype(BF16)
            return carry

        lax.fori_loop(0, 4, body, 0)
        x_copies[b, h] = []
        for d in (2, 1, 3):
            to = (x + d) % 4
            copy = remote(
                part.at[b, c, h, to], xbuf.at[b, h, d - 1],
                xs.at[b, h, d - 1], xr.at[b, h, d - 1], at(x_=to),
            )
            copy.start()
            x_copies[b, h].append(copy)

    def x_reduce(b, h):
        for copy in x_copies[b, h]:
            copy.wait_recv()
        t = part[b, c, h, x].astype(F32)
        for d in range(3):
            t = t + xbuf[b, h, d].astype(F32)
        zsrc[b, h] = t.astype(BF16)
        up = (zh == h).astype(jnp.int32)
        z_copies[b, h] = remote(
            zsrc.at[b, h], zbuf.at[b, 1 - up], zs.at[b, h], zr.at[b, 1 - up], at_z(12 - 8 * up)
        )
        z_copies[b, h].start()

    extra = ((3, 0, 3), (3, 1, 0), (2, 1, 0), (1, 1, 2))

    def extra_compute(b):
        col = jnp.where(zl == 7, 0, 2)
        kernel = jnp.concatenate([wav[b - 1, r * 3 + col] for r in range(3)], axis=0)

        def body(j, carry):
            q = jnp.where(zl == 7, 9 - j - b, j + b - 5)
            lhs = jnp.concatenate(
                [
                    xb[q + 3, :, pl.ds(PAD + ro * b * 12, 80), :].reshape(240, 128)
                    for ro in (-1, 0, 1)
                ],
                axis=1,
            )
            res = jnp.dot(lhs, kernel, preferred_element_type=F32)
            res = res.astype(BF16).reshape(3, 80, 256)
            for t in range(3):
                s = 3 * j + t
                part2[b - 1, s % 2, s // 8, (s // 2) % 4] = res[t]
            return carry

        lax.fori_loop(5 - b, 5, body, 0)

    def extra_core(b, h, lo):
        n = 4 - lo
        return remote(
            part2.at[b - 1, 1 - c, h, pl.ds(lo, n)], cbuf2.at[b - 1, h, pl.ds(lo, n)],
            cs2.at[b - 1, h], cr2.at[b - 1, h], at(c_=1 - c),
        )

    def extra_x(b, h, d):
        to = (x + d) % 4
        return remote(
            part2.at[b - 1, c, h, to], xbuf2.at[b - 1, h, d - 1],
            xs2.at[b - 1, h, d - 1], xr2.at[b - 1, h, d - 1], at(x_=to),
        )

    def extra_z(b, h):
        zz = (7 - zl + 4 + 8 * h) % 16
        return remote(
            zsrc2.at[b - 1, h], zbuf2.at[b - 1, zh], zs2.at[b - 1, h], zr2.at[b - 1, zh],
            ((zz % 8) * 4 + y, (zz // 8) * 8 + x * 2 + c),
        )

    def extra_core_reduce(b, h, lo):
        extra_core(b, h, lo).wait_recv()
        for i in range(lo, 4):
            mine = part2[b - 1, c, h, i].astype(F32) + cbuf2[b - 1, h, i].astype(F32)
            part2[b - 1, c, h, i] = mine.astype(BF16)
        for d in (2, 1, 3):
            pl.when((x + d) % 4 >= lo)(extra_x(b, h, d).start)

    def extra_x_reduce(b, h, lo):
        @pl.when(x >= lo)
        def _():
            t = part2[b - 1, c, h, x].astype(F32)
            for d in (2, 1, 3):
                extra_x(b, h, d).wait_recv()
                t = t + xbuf2[b - 1, h, d - 1].astype(F32)
            zsrc2[b - 1, h] = t.astype(BF16)
            extra_z(b, h).start()

    def extra_sent(b, h, lo):
        extra_core(b, h, lo).wait_send()
        for d in (2, 1, 3):
            pl.when((x + d) % 4 >= lo)(extra_x(b, h, d).wait_send)
        pl.when(x >= lo)(extra_z(b, h).wait_send)

    compute(0, 0, 5)
    core_send(0, 0)
    core_send(0, 1)

    @pl.when(edge)
    def _():
        extra_compute(3)
        extra_core(*extra[0]).start()
        extra_core(*extra[1]).start()
        extra_compute(2)
        extra_core(*extra[2]).start()
        extra_compute(1)
        extra_core(*extra[3]).start()

    core_reduce(0, 0)
    core_reduce(0, 1)

    @pl.when(edge)
    def _():
        for u in extra:
            extra_core_reduce(*u)

    halo_wait(0)
    compute(1, 0, 5)
    core_send(1, 0)
    core_send(1, 1)
    three = own + pool_get(3) + pool_get(4)
    pool_send(poolbuf.at[4], 5, at_z(12))
    halo_wait(1)
    compute(2, 0, 5)
    core_send(2, 0)
    core_send(2, 1)
    core_reduce(1, 0)
    core_reduce(1, 1)
    x_reduce(0, 0)
    x_reduce(0, 1)
    halo_wait(2)
    compute(3, 0, 5)
    core_send(3, 0)
    core_send(3, 1)
    core_reduce(2, 0)
    core_reduce(2, 1)
    four = three + pool_get(5)
    poolsrc[2] = four
    pool_send(poolsrc.at[2], 6, at(zl_=zl + 1 - 2 * (zl % 2)))

    @pl.when(edge)
    def _():
        for u in extra:
            extra_x_reduce(*u)

    x_reduce(1, 0)
    x_reduce(1, 1)
    core_reduce(3, 0)
    core_reduce(3, 1)

    pair = four + pool_get(6)
    poolsrc[3] = pair
    place = zl % 4
    middle = jnp.logical_or(place == 1, place == 2)

    def pool_copy(src, slot_i, dev):
        return remote(poolsrc.at[src], poolbuf.at[slot_i], ps.at[slot_i], pr.at[slot_i], dev)

    inward = pool_copy(3, 7, at(zl_=(zl + jnp.where(place == 1, 1, 7)) % 8))
    outward = pool_copy(4, 8, at(zl_=(zl + jnp.where(place == 1, 7, 1)) % 8))
    pl.when(middle)(inward.start)
    x_reduce(2, 0)
    x_reduce(2, 1)

    @pl.when(middle)
    def _():
        inward.wait_recv()
        poolsrc[4] = poolsrc[3] + poolbuf[7]
        outward.start()

    x_reduce(3, 0)
    x_reduce(3, 1)

    @pl.when(jnp.logical_not(middle))
    def _():
        outward.wait_recv()
        poolsrc[4] = poolbuf[8]

    pool_send(poolsrc.at[4], 9, at(c_=1 - c))
    loads[3].wait()

    proj = jnp.zeros((80, 256), F32)
    for b in range(4):
        if b == 1:
            both = poolsrc[4] + pool_get(9)
            poolsrc[5] = both
            for d in range(1, 4):
                pool_send(poolsrc.at[5], 9 + d, at(x_=(x + d) % 4))
        if b == 3:
            pre_all = both + pool_get(10) + pool_get(11) + pool_get(12)
            pre_all = pre_all * (1.0 / 38400.0)
            pooled = jnp.maximum(gain[4:5] * pre_all + shift[4:5], 0.0).astype(BF16)
            pool_term = jnp.dot(
                jnp.broadcast_to(pooled, (16, 256)), wprojv[pl.ds(1024, 256), :],
                preferred_element_type=F32,
            )[0:1]
        for way in range(2):
            remote(
                zsrc.at[b, 0], zbuf.at[b, way], zs.at[b, 0], zr.at[b, way], at_z(4)
            ).wait_recv()
        acc[b] = zbuf[b, 0].astype(F32) + zbuf[b, 1].astype(F32)
        if b > 0:
            over = jnp.logical_and(bit == 1, x >= (2 if b == 1 else 0))
            if b == 3:
                over = jnp.logical_or(over, jnp.logical_and(bit == 0, x == 3))

            @pl.when(jnp.logical_and(edge_owner, over))
            def _():
                for half in range(2):
                    remote(
                        zsrc2.at[b - 1, 0], zbuf2.at[b - 1, half],
                        zs2.at[b - 1, 0], zr2.at[b - 1, half], at_z(4),
                    ).wait_recv()
                acc[b] += zbuf2[b - 1, 0].astype(F32) + zbuf2[b - 1, 1].astype(F32)

        act = jnp.maximum(acc[b] * gain[b : b + 1] + shift[b : b + 1], 0.0).astype(BF16)
        proj = proj + jnp.dot(act, wprojv[pl.ds(b * 256, 256), :], preferred_element_type=F32)
    head = jnp.maximum(gain[5:6] * (proj + pool_term) + shift[5:6], 0.0)
    head = jnp.concatenate([head, jnp.zeros((48, 256), F32)], axis=0)
    stage[...] = jnp.transpose(head).astype(BF16).reshape(16, 16, 128)

    def out_copy(d):
        return remote(stage.at[d], obuf.at[slot], os.at[d], orr.at[slot], (zl_dst * 4 + y_dst, d))

    def out_send(i, carry):
        @pl.when(has_col)
        def _():
            out_copy((ch + i) % 16).start()

        return carry

    lax.fori_loop(0, 16, out_send, 0)
    for copy in ycopies + list(psends.values()):
        copy.wait_send()
    for d in range(3):
        for side in range(2):
            pl.when(halo_out[side])(halo_copy(d, side).wait_send)

    @pl.when(middle)
    def _():
        inward.wait_send()
        outward.wait_send()

    @pl.when(edge)
    def _():
        for u in extra:
            extra_sent(*u)

    for u in core_copies:
        for copy in [core_copies[u], z_copies[u]] + x_copies[u]:
            copy.wait_send()

    def out_recv(i, carry):
        remote(stage.at[0], obuf.at[i], os.at[0], orr.at[i], east).wait_recv()
        return carry

    lax.fori_loop(0, 15, out_recv, 0)
    out[...] = obuf[:, :, 0:80]

    def out_sent(d, carry):
        @pl.when(has_col)
        def _():
            out_copy(d).wait_send()

        return carry

    lax.fori_loop(0, 16, out_sent, 0)


def local(features, pointwise_weight, w_atrous, w_pool, w_proj, norm_gain, norm_shift):
    feat = jnp.transpose(features, (1, 0, 2))
    vmem = pl.BlockSpec(memory_space=pltpu.VMEM)
    hbm = pl.BlockSpec(memory_space=pl.ANY)
    dma = pltpu.SemaphoreType.DMA
    out = pl.pallas_call(
        head_kernel,
        out_shape=jax.ShapeDtypeStruct((15, 16, 80), BF16),
        in_specs=[hbm, hbm, hbm, vmem, hbm, vmem, vmem],
        out_specs=vmem,
        scratch_shapes=[
            pltpu.VMEM((15, 80, 128), BF16),
            pltpu.VMEM((11, 3, 80 + 2 * PAD, 128), BF16),
            pltpu.VMEM((4, 2, 2, 4, 80, 256), BF16),
            pltpu.VMEM((4, 2, 4, 80, 256), BF16),
            pltpu.VMEM((4, 2, 3, 80, 256), BF16),
            pltpu.VMEM((4, 2, 80, 256), BF16),
            pltpu.VMEM((4, 2, 80, 256), BF16),
            pltpu.VMEM((16, 16, 128), BF16),
            pltpu.VMEM((15, 16, 128), BF16),
            pltpu.VMEM((128, 256), BF16),
            pltpu.VMEM((3, 9, 128, 256), BF16),
            pltpu.VMEM((1280, 256), BF16),
            pltpu.VMEM((6, 1, 256), F32),
            pltpu.VMEM((13, 1, 256), F32),
            pltpu.VMEM((3, 2, 2, 4, 80, 256), BF16),
            pltpu.VMEM((3, 2, 4, 80, 256), BF16),
            pltpu.VMEM((3, 2, 3, 80, 256), BF16),
            pltpu.VMEM((3, 2, 80, 256), BF16),
            pltpu.VMEM((3, 2, 80, 256), BF16),
            pltpu.VMEM((4, 80, 256), F32),
            dma((4,)),
            dma((3,)), dma((3,)),
            dma((6,)), dma((6,)),
            dma((4, 2)), dma((4, 2)),
            dma((4, 2, 3)), dma((4, 2, 3)),
            dma((4, 2)), dma((4, 2)),
            dma((16,)), dma((15,)),
            dma((13,)), dma((13,)),
            dma((3, 2)), dma((3, 2)),
            dma((3, 2, 3)), dma((3, 2, 3)),
            dma((3, 2)), dma((3, 2)),
        ],
        compiler_params=pltpu.CompilerParams(collective_id=0, has_side_effects=True),
        name="aspp_head",
    )(
        feat, pointwise_weight, w_atrous.reshape(3, 9, 128, 256), w_pool, w_proj,
        norm_gain, norm_shift,
    )
    return jnp.transpose(out, (2, 0, 1))


def solution(mesh):
    return jax.shard_map(
        local,
        mesh=mesh,
        in_specs=(
            P(None, "lon", "ch"),
            P("ch", None),
            P(None, None, None, "ch", None),
            P("ch", None),
            P(),
            P(),
            P(),
        ),
        out_specs=P(None, "lon", "ch"),
        check_vma=False,
    )
```

```python
import jax
import jax.numpy as jnp
from jax import lax
from jax.experimental import pallas as pl
from jax.experimental.pallas import tpu as pltpu
from jax.sharding import PartitionSpec as P

MESH_ID = pl.DeviceIdType.MESH
F32 = jnp.float32
BF16 = jnp.bfloat16

PAD = 48


def head_kernel(
    feat, pw, wa, wpool, wproj, gain, shift, out,
    xin, xb, part, cbuf, xbuf, zsrc, zbuf, stage, obuf,
    pwv, wav, wprojv, poolsrc, poolbuf,
    part2, cbuf2, xbuf2, zsrc2, zbuf2, acc, xacc,
    ld_sem, ys, yr, hs, hr, cs, cr, xs, xr, zs, zr, os, orr, ps, pr,
    cs2, cr2, xs2, xr2, zs2, zr2,
):
    lon = lax.axis_index("lon")
    ch = lax.axis_index("ch")
    zl, y = lon // 4, lon % 4
    zh, x, c = ch // 8, (ch // 2) % 4, ch % 2
    z = zh * 8 + zl

    def at(zl_=None, y_=None, x_=None, c_=None):
        zz = zl if zl_ is None else zl_
        yy = y if y_ is None else y_
        xx = x if x_ is None else x_
        cc = c if c_ is None else c_
        return (zz * 4 + yy, zh * 8 + xx * 2 + cc)

    def at_z(dz):
        zz = (z + dz) % 16
        return ((zz % 8) * 4 + y, (zz // 8) * 8 + x * 2 + c)

    def block_of(j, level):
        q = (j + 1) % 5
        return jnp.where(level == 0, 4 - q, q)

    bit = ((z + 12) % 16) // 8
    zl_dst = (zl + 4) % 8
    k = bit * 8 + x * 2 + c
    kj, kt = k // 3, k % 3
    kq = block_of(kj, zl_dst)
    kg = 4 * kq + y
    y_dst = kg // 5
    slot = (kg % 5) * 3 + kt
    has_col = k < 15

    loads = [
        pltpu.make_async_copy(feat, xin, ld_sem.at[0]),
        pltpu.make_async_copy(pw, pwv, ld_sem.at[1]),
        pltpu.make_async_copy(wa, wav, ld_sem.at[2]),
        pltpu.make_async_copy(wproj, wprojv, ld_sem.at[3]),
    ]
    for load in loads:
        load.start()

    barrier = pltpu.get_barrier_semaphore()

    def hello(dev):
        pl.semaphore_signal(barrier, inc=1, device_id=dev, device_id_type=MESH_ID)

    east, west = at(zl_=(zl + 1) % 8), at(zl_=(zl + 7) % 8)
    edge = jnp.logical_or(zl == 0, zl == 7)
    edge_owner = jnp.logical_or(zl == 3, zl == 4)

    @pl.when(edge_owner)
    def _():
        far = jnp.where(zl == 4, 7, 0) * 4 + y
        hello((far, x * 2 + c))
        hello((far, 8 + x * 2 + c))

    @pl.when(zl < 7)
    def _():
        hello(east)

    @pl.when(zl > 0)
    def _():
        hello(west)

    hello(at_z(4))
    hello(at_z(12))

    for d in range(1, 4):
        hello(at(y_=(y + d) % 4))
        hello(at(x_=(x + d) % 4))
    hello(at(c_=1 - c))

    zrow = jnp.zeros((3, PAD, 128), BF16)

    def clear(i, carry):
        xb[i, :, pl.ds(0, PAD), :] = zrow
        xb[i, :, pl.ds(PAD + 80, PAD), :] = zrow
        return carry

    lax.fori_loop(0, 11, clear, 0)
    for b in range(4):
        part[b, 1, 1, 3] = jnp.zeros((80, 256), BF16)

    blank = jnp.zeros((3, 80, 128), BF16)

    @pl.when(edge)
    def _():
        for d in range(3):
            xb[jnp.where(zl == 0, d, 8 + d), :, pl.ds(PAD, 80), :] = blank
        part2[0, 0, 1, 0] = jnp.zeros((80, 256), BF16)
        part2[2, 0, 0, 1] = jnp.zeros((80, 256), BF16)

    loads[0].wait()
    xb[y + 3, :, pl.ds(PAD, 80), :] = xin[0:3]
    xb[y + 4, :, pl.ds(PAD, 80), :] = xin[12:15]

    def add_col(i, tot):
        return tot + jnp.sum(xin[i].astype(F32).reshape(10, 8, 128), axis=0)

    sums = lax.fori_loop(0, 15, add_col, jnp.zeros((8, 128), F32))
    colsum = jnp.sum(sums, axis=0, keepdims=True)
    pre = jnp.dot(
        jnp.broadcast_to(colsum, (8, 128)), wpool[...].astype(F32),
        precision=lax.Precision.HIGHEST, preferred_element_type=F32,
    )[0:1]
    poolsrc[0] = pre

    pl.semaphore_wait(barrier, 11 + edge.astype(jnp.int32))

    def remote(src, dst, ssem, rsem, dev):
        return pltpu.make_async_remote_copy(
            src_ref=src, dst_ref=dst, send_sem=ssem, recv_sem=rsem,
            device_id=dev, device_id_type=MESH_ID,
        )

    rows = pl.ds(PAD, 80)
    ycopies = []
    for g in range(1, 4):
        q = (5 * y + g) // 4
        copy = remote(
            xin.at[pl.ds(3 * g, 3)], xb.at[q + 3, :, rows, :],
            ys.at[g - 1], yr.at[g - 1], at(y_=(y + g) % 4),
        )
        copy.start()
        ycopies.append(copy)
    psends = {}

    def pool_send(src, slot_i, dev):
        psends[slot_i] = remote(src, poolbuf.at[slot_i], ps.at[slot_i], pr.at[slot_i], dev)
        psends[slot_i].start()

    def pool_get(slot_i):
        psends[slot_i].wait_recv()
        return poolbuf[slot_i]

    for d in range(1, 4):
        pool_send(poolsrc.at[0], d - 1, at(y_=(y + d) % 4))

    def halo_copy(d, side):
        q = (4 - d) if side == 0 else d
        q_to = q - 5 if side == 0 else q + 5
        return remote(
            xb.at[q + 3, :, rows, :], xb.at[q_to + 3, :, rows, :],
            hs.at[2 * d + side], hr.at[2 * d + side], east if side == 0 else west,
        )

    halo_out = (zl < 7, zl > 0)
    halo_in = (zl > 0, zl < 7)
    for d, sides in ((0, (0,)), (0, (1,)), (1, (0,)), (1, (1,)), (2, (0, 1))):
        q = (4 - d) if sides[0] == 0 else d
        g = (4 * q + y) % 5

        @pl.when(jnp.logical_and(g > 0, g < 4))
        def _():
            gi = jnp.clip(g - 1, 0, 2)
            remote(
                xin.at[pl.ds(0, 3)], xb.at[q + 3, :, rows, :], ys.at[gi], yr.at[gi], east
            ).wait_recv()

        for side in sides:
            pl.when(halo_out[side])(halo_copy(d, side).start)

    def halo_wait(d):
        for side in range(2):
            pl.when(halo_in[side])(halo_copy(d, side).wait_recv)

    loads[1].wait()
    loads[2].wait()

    def compute(b, lo, hi):
        def body(j, carry):
            q = block_of(j, zl)
            if b == 0:
                lhs = xb[q + 3, :, rows, :].reshape(240, 128)
                res = jnp.dot(lhs, pwv[...], preferred_element_type=F32)
            else:
                taps = []
                for ro in (-1, 0, 1):
                    for co in (-1, 0, 1):
                        taps.append(
                            xb[q + 3 + co * b, :, pl.ds(PAD + ro * b * 12, 80), :].reshape(240, 128)
                        )
                res = jnp.dot(
                    jnp.concatenate(taps, axis=1), wav[b - 1].reshape(1152, 256),
                    preferred_element_type=F32,
                )
            res = res.astype(BF16).reshape(3, 80, 256)
            for t in range(3):
                s = 3 * j + t
                part[b, s % 2, s // 8, (s // 2) % 4] = res[t]
            return carry

        lax.fori_loop(lo, hi, body, 0)

    core_copies, x_copies, z_copies = {}, {}, {}

    def core_send(b, h):
        copy = remote(
            part.at[b, 1 - c, h], cbuf.at[b, h], cs.at[b, h], cr.at[b, h], at(c_=1 - c)
        )
        copy.start()
        core_copies[b, h] = copy

    def core_reduce(b, h):
        core_copies[b, h].wait_recv()

        def body(i, carry):
            mine = part[b, c, h, i].astype(F32) + cbuf[b, h, i].astype(F32)
            part[b, c, h, i] = mine.astype(BF16)
            return carry

        lax.fori_loop(0, 4, body, 0)
        first = flip if h == 0 else 3 - x
        x_copies[b, h] = []
        for i, col in enumerate((first, (x + 2) % 4)):
            copy = remote(
                part.at[b, c, h, col], xbuf.at[b, h, i], xs.at[b, h, i], xr.at[b, h, i],
                at(x_=first),
            )
            copy.start()
            x_copies[b, h].append(copy)

    flip = x + 1 - 2 * (x % 2)

    def x_half(b, h):
        second = 3 - x if h == 0 else flip
        for copy in x_copies[b, h]:
            copy.wait_recv()
        give = part[b, c, h, second].astype(F32) + xbuf[b, h, 1].astype(F32)
        part[b, c, h, second] = give.astype(BF16)
        copy = remote(
            part.at[b, c, h, second], xbuf.at[b, h, 2], xs.at[b, h, 2], xr.at[b, h, 2],
            at(x_=second),
        )
        copy.start()
        x_copies[b, h].append(copy)
        xacc[b, h] = part[b, c, h, x].astype(F32) + xbuf[b, h, 0].astype(F32)

    def x_reduce(b, h):
        x_copies[b, h][2].wait_recv()
        zsrc[b, h] = (xacc[b, h] + xbuf[b, h, 2].astype(F32)).astype(BF16)
        up = (zh == h).astype(jnp.int32)
        z_copies[b, h] = remote(
            zsrc.at[b, h], zbuf.at[b, 1 - up], zs.at[b, h], zr.at[b, 1 - up], at_z(12 - 8 * up)
        )
        z_copies[b, h].start()

    extra = ((3, 0, 1, 4), (3, 1, 0, 2), (2, 0, 3, 4), (2, 1, 0, 2), (1, 1, 0, 2))

    def within(to, lo, hi):
        return jnp.logical_and(to >= lo, to < hi)

    def extra_compute(b):
        col = jnp.where(zl == 7, 0, 2)
        kernel = jnp.concatenate([wav[b - 1, r * 3 + col] for r in range(3)], axis=0)

        def body(j, carry):
            q = jnp.where(zl == 7, 8 - j - b, j + b - 4)
            lhs = jnp.concatenate(
                [
                    xb[q + 3, :, pl.ds(PAD + ro * b * 12, 80), :].reshape(240, 128)
                    for ro in (-1, 0, 1)
                ],
                axis=1,
            )
            res = jnp.dot(lhs, kernel, preferred_element_type=F32)
            res = res.astype(BF16).reshape(3, 80, 256)
            for t in range(3):
                s = 3 * j + t
                part2[b - 1, s % 2, s // 8, (s // 2) % 4] = res[t]
            return carry

        lax.fori_loop(4 - b, 4, body, 0)

    def extra_core(b, h, lo, hi):
        n = hi - lo
        return remote(
            part2.at[b - 1, 1 - c, h, pl.ds(lo, n)], cbuf2.at[b - 1, h, pl.ds(lo, n)],
            cs2.at[b - 1, h], cr2.at[b - 1, h], at(c_=1 - c),
        )

    def extra_x(b, h, d):
        to = (x + d) % 4
        return remote(
            part2.at[b - 1, c, h, to], xbuf2.at[b - 1, h, d - 1],
            xs2.at[b - 1, h, d - 1], xr2.at[b - 1, h, d - 1], at(x_=to),
        )

    def extra_z(b, h):
        zz = (7 - zl + 4 + 8 * h) % 16
        return remote(
            zsrc2.at[b - 1, h], zbuf2.at[b - 1, zh], zs2.at[b - 1, h], zr2.at[b - 1, zh],
            ((zz % 8) * 4 + y, (zz // 8) * 8 + x * 2 + c),
        )

    def extra_core_reduce(b, h, lo, hi):
        extra_core(b, h, lo, hi).wait_recv()
        for i in range(lo, hi):
            mine = part2[b - 1, c, h, i].astype(F32) + cbuf2[b - 1, h, i].astype(F32)
            part2[b - 1, c, h, i] = mine.astype(BF16)
        for d in (2, 1, 3):
            pl.when(within((x + d) % 4, lo, hi))(extra_x(b, h, d).start)

    def extra_x_reduce(b, h, lo, hi):
        @pl.when(within(x, lo, hi))
        def _():
            t = part2[b - 1, c, h, x].astype(F32)
            for d in (2, 1, 3):
                extra_x(b, h, d).wait_recv()
                t = t + xbuf2[b - 1, h, d - 1].astype(F32)
            zsrc2[b - 1, h] = t.astype(BF16)
            extra_z(b, h).start()

    def extra_sent(b, h, lo, hi):
        extra_core(b, h, lo, hi).wait_send()
        for d in (2, 1, 3):
            pl.when(within((x + d) % 4, lo, hi))(extra_x(b, h, d).wait_send)
        pl.when(within(x, lo, hi))(extra_z(b, h).wait_send)

    compute(0, 0, 3)
    core_send(0, 0)
    compute(0, 3, 5)
    core_send(0, 1)
    compute(1, 0, 3)
    core_send(1, 0)
    own = poolsrc[0] + pool_get(0) + pool_get(1) + pool_get(2)
    poolsrc[1] = own
    pool_send(poolsrc.at[1], 3, at_z(4))
    pool_send(poolsrc.at[1], 4, at_z(12))
    core_reduce(0, 0)
    core_reduce(0, 1)

    @pl.when(edge)
    def _():
        extra_compute(3)
        extra_core(*extra[0]).start()
        extra_core(*extra[1]).start()
        extra_compute(2)
        extra_core(*extra[2]).start()
        extra_core(*extra[3]).start()
        extra_compute(1)
        extra_core(*extra[4]).start()

    core_reduce(1, 0)
    halo_wait(0)
    compute(2, 0, 3)
    core_send(2, 0)
    compute(1, 3, 5)
    core_send(1, 1)

    @pl.when(edge)
    def _():
        for u in extra:
            extra_core_reduce(*u)

    x_half(0, 0)
    x_half(0, 1)
    core_reduce(2, 0)
    core_reduce(1, 1)
    halo_wait(1)
    compute(3, 0, 3)
    core_send(3, 0)
    compute(2, 3, 5)
    core_send(2, 1)
    three = own + pool_get(3) + pool_get(4)
    pool_send(poolbuf.at[4], 5, at_z(12))
    x_reduce(0, 0)
    x_reduce(0, 1)
    x_half(1, 0)
    core_reduce(3, 0)
    core_reduce(2, 1)
    halo_wait(2)
    compute(3, 3, 5)
    core_send(3, 1)
    x_half(2, 0)
    x_half(1, 1)
    x_reduce(1, 0)
    core_reduce(3, 1)
    four = three + pool_get(5)
    poolsrc[2] = four
    pool_send(poolsrc.at[2], 6, at(zl_=zl + 1 - 2 * (zl % 2)))

    @pl.when(edge)
    def _():
        for u in extra:
            extra_x_reduce(*u)

    x_half(3, 0)
    x_half(2, 1)
    x_reduce(2, 0)
    x_reduce(1, 1)

    pair = four + pool_get(6)
    poolsrc[3] = pair
    place = zl % 4
    middle = jnp.logical_or(place == 1, place == 2)

    def pool_copy(src, slot_i, dev):
        return remote(poolsrc.at[src], poolbuf.at[slot_i], ps.at[slot_i], pr.at[slot_i], dev)

    inward = pool_copy(3, 7, at(zl_=(zl + jnp.where(place == 1, 1, 7)) % 8))
    outward = pool_copy(4, 8, at(zl_=(zl + jnp.where(place == 1, 7, 1)) % 8))
    pl.when(middle)(inward.start)
    x_half(3, 1)
    x_reduce(3, 0)
    x_reduce(2, 1)

    @pl.when(middle)
    def _():
        inward.wait_recv()
        poolsrc[4] = poolsrc[3] + poolbuf[7]
        outward.start()

    x_reduce(3, 1)

    @pl.when(jnp.logical_not(middle))
    def _():
        outward.wait_recv()
        poolsrc[4] = poolbuf[8]

    pool_send(poolsrc.at[4], 9, at(c_=1 - c))
    loads[3].wait()

    proj = jnp.zeros((80, 256), F32)
    for b in range(4):
        if b == 1:
            both = poolsrc[4] + pool_get(9)
            poolsrc[5] = both
            for d in range(1, 4):
                pool_send(poolsrc.at[5], 9 + d, at(x_=(x + d) % 4))
        if b == 3:
            pre_all = both + pool_get(10) + pool_get(11) + pool_get(12)
            pre_all = pre_all * (1.0 / 38400.0)
            pooled = jnp.maximum(gain[4:5] * pre_all + shift[4:5], 0.0).astype(BF16)
            pool_term = jnp.dot(
                jnp.broadcast_to(pooled, (16, 256)), wprojv[pl.ds(1024, 256), :],
                preferred_element_type=F32,
            )[0:1]
        for way in range(2):
            remote(
                zsrc.at[b, 0], zbuf.at[b, way], zs.at[b, 0], zr.at[b, way], at_z(4)
            ).wait_recv()
        acc[b] = zbuf[b, 0].astype(F32) + zbuf[b, 1].astype(F32)
        if b > 0:
            over = jnp.logical_and(bit == 1, x < 2)
            if b > 1:
                over = jnp.logical_or(over, jnp.logical_and(bit == 0, x >= (3 if b == 2 else 1)))

            @pl.when(jnp.logical_and(edge_owner, over))
            def _():
                for half in range(2):
                    remote(
                        zsrc2.at[b - 1, 0], zbuf2.at[b - 1, half],
                        zs2.at[b - 1, 0], zr2.at[b - 1, half], at_z(4),
                    ).wait_recv()
                acc[b] += zbuf2[b - 1, 0].astype(F32) + zbuf2[b - 1, 1].astype(F32)

        act = jnp.maximum(acc[b] * gain[b : b + 1] + shift[b : b + 1], 0.0).astype(BF16)
        proj = proj + jnp.dot(act, wprojv[pl.ds(b * 256, 256), :], preferred_element_type=F32)
    head = jnp.maximum(gain[5:6] * (proj + pool_term) + shift[5:6], 0.0)
    head = jnp.concatenate([head, jnp.zeros((48, 256), F32)], axis=0)
    stage[...] = jnp.transpose(head).astype(BF16).reshape(16, 16, 128)

    def out_copy(d):
        return remote(stage.at[d], obuf.at[slot], os.at[d], orr.at[slot], (zl_dst * 4 + y_dst, d))

    def out_send(i, carry):
        @pl.when(has_col)
        def _():
            out_copy((ch + i) % 16).start()

        return carry

    lax.fori_loop(0, 16, out_send, 0)
    for copy in ycopies + list(psends.values()):
        copy.wait_send()
    for d in range(3):
        for side in range(2):
            pl.when(halo_out[side])(halo_copy(d, side).wait_send)

    @pl.when(middle)
    def _():
        inward.wait_send()
        outward.wait_send()

    @pl.when(edge)
    def _():
        for u in extra:
            extra_sent(*u)

    for u in core_copies:
        for copy in [core_copies[u], z_copies[u]] + x_copies[u]:
            copy.wait_send()

    def out_recv(i, carry):
        remote(stage.at[0], obuf.at[i], os.at[0], orr.at[i], east).wait_recv()
        return carry

    lax.fori_loop(0, 15, out_recv, 0)
    out[...] = obuf[:, :, 0:80]

    def out_sent(d, carry):
        @pl.when(has_col)
        def _():
            out_copy(d).wait_send()

        return carry

    lax.fori_loop(0, 16, out_sent, 0)


def local(features, pointwise_weight, w_atrous, w_pool, w_proj, norm_gain, norm_shift):
    feat = jnp.transpose(features, (1, 0, 2))
    vmem = pl.BlockSpec(memory_space=pltpu.VMEM)
    hbm = pl.BlockSpec(memory_space=pl.ANY)
    dma = pltpu.SemaphoreType.DMA
    out = pl.pallas_call(
        head_kernel,
        out_shape=jax.ShapeDtypeStruct((15, 16, 80), BF16),
        in_specs=[hbm, hbm, hbm, vmem, hbm, vmem, vmem],
        out_specs=vmem,
        scratch_shapes=[
            pltpu.VMEM((15, 80, 128), BF16),
            pltpu.VMEM((11, 3, 80 + 2 * PAD, 128), BF16),
            pltpu.VMEM((4, 2, 2, 4, 80, 256), BF16),
            pltpu.VMEM((4, 2, 4, 80, 256), BF16),
            pltpu.VMEM((4, 2, 3, 80, 256), BF16),
            pltpu.VMEM((4, 2, 80, 256), BF16),
            pltpu.VMEM((4, 2, 80, 256), BF16),
            pltpu.VMEM((16, 16, 128), BF16),
            pltpu.VMEM((15, 16, 128), BF16),
            pltpu.VMEM((128, 256), BF16),
            pltpu.VMEM((3, 9, 128, 256), BF16),
            pltpu.VMEM((1280, 256), BF16),
            pltpu.VMEM((6, 1, 256), F32),
            pltpu.VMEM((13, 1, 256), F32),
            pltpu.VMEM((3, 2, 2, 4, 80, 256), BF16),
            pltpu.VMEM((3, 2, 4, 80, 256), BF16),
            pltpu.VMEM((3, 2, 3, 80, 256), BF16),
            pltpu.VMEM((3, 2, 80, 256), BF16),
            pltpu.VMEM((3, 2, 80, 256), BF16),
            pltpu.VMEM((4, 80, 256), F32),
            pltpu.VMEM((4, 2, 80, 256), F32),
            dma((4,)),
            dma((3,)), dma((3,)),
            dma((6,)), dma((6,)),
            dma((4, 2)), dma((4, 2)),
            dma((4, 2, 3)), dma((4, 2, 3)),
            dma((4, 2)), dma((4, 2)),
            dma((16,)), dma((15,)),
            dma((13,)), dma((13,)),
            dma((3, 2)), dma((3, 2)),
            dma((3, 2, 3)), dma((3, 2, 3)),
            dma((3, 2)), dma((3, 2)),
        ],
        compiler_params=pltpu.CompilerParams(collective_id=0, has_side_effects=True),
        name="aspp_head",
    )(
        feat, pointwise_weight, w_atrous.reshape(3, 9, 128, 256), w_pool, w_proj,
        norm_gain, norm_shift,
    )
    return jnp.transpose(out, (2, 0, 1))


def solution(mesh):
    return jax.shard_map(
        local,
        mesh=mesh,
        in_specs=(
            P(None, "lon", "ch"),
            P("ch", None),
            P(None, None, None, "ch", None),
            P("ch", None),
            P(),
            P(),
            P(),
        ),
        out_specs=P(None, "lon", "ch"),
        check_vma=False,
    )
```

```python
import jax
import jax.numpy as jnp
from jax import lax
from jax.experimental import pallas as pl
from jax.experimental.pallas import tpu as pltpu
from jax.sharding import PartitionSpec as P

MESH_ID = pl.DeviceIdType.MESH
F32 = jnp.float32
BF16 = jnp.bfloat16

PAD = 48


def head_kernel(
    feat, pw, wa, wpool_h, wproj, gain_h, shift_h, out,
    xin, xb, part, cbuf, xbuf, zsrc, zbuf, stage, obuf,
    pwv, wav, wprojv, wpool, gain, shift, poolsrc, poolbuf,
    part2, cbuf2, xbuf2, zsrc2, zbuf2, acc, xacc,
    ld_sem, ys, yr, hs, hr, cs, cr, xs, xr, zs, zr, os, orr, ps, pr,
    cs2, cr2, xs2, xr2, zs2, zr2,
):
    lon = lax.axis_index("lon")
    ch = lax.axis_index("ch")
    zl, y = lon // 4, lon % 4
    zh, x, c = ch // 8, (ch // 2) % 4, ch % 2
    z = zh * 8 + zl

    def at(zl_=None, y_=None, x_=None, c_=None):
        zz = zl if zl_ is None else zl_
        yy = y if y_ is None else y_
        xx = x if x_ is None else x_
        cc = c if c_ is None else c_
        return (zz * 4 + yy, zh * 8 + xx * 2 + cc)

    def at_z(dz):
        zz = (z + dz) % 16
        return ((zz % 8) * 4 + y, (zz // 8) * 8 + x * 2 + c)

    def block_of(j, level):
        q = (j + 1) % 5
        return jnp.where(level == 0, 4 - q, q)

    bit = ((z + 12) % 16) // 8
    zl_dst = (zl + 4) % 8
    k = bit * 8 + c * 4 + x
    kj, kt = k // 3, k % 3
    kq = block_of(kj, zl_dst)
    kg = 4 * kq + y
    y_dst = kg // 5
    slot = (kg % 5) * 3 + kt
    has_col = k < 15

    barrier = pltpu.get_barrier_semaphore()

    def hello(dev):
        pl.semaphore_signal(barrier, inc=1, device_id=dev, device_id_type=MESH_ID)

    east, west = at(zl_=(zl + 1) % 8), at(zl_=(zl + 7) % 8)
    edge = jnp.logical_or(zl == 0, zl == 7)
    edge_owner = jnp.logical_or(zl == 3, zl == 4)

    @pl.when(edge_owner)
    def _():
        far = jnp.where(zl == 4, 7, 0) * 4 + y
        hello((far, x * 2 + c))
        hello((far, 8 + x * 2 + c))

    @pl.when(zl < 7)
    def _():
        hello(east)

    @pl.when(zl > 0)
    def _():
        hello(west)

    hello(at_z(4))
    hello(at_z(12))

    for d in range(1, 4):
        hello(at(y_=(y + d) % 4))
        hello(at(x_=(x + d) % 4))
    hello(at(c_=1 - c))

    loads = [
        pltpu.make_async_copy(src, dst, ld_sem.at[i])
        for i, (src, dst) in enumerate((
            (feat, xin), (wpool_h, wpool), (pw, pwv), (wa, wav),
            (wproj, wprojv), (gain_h, gain), (shift_h, shift),
        ))
    ]
    for load in loads:
        load.start()

    zrow = jnp.zeros((3, PAD, 128), BF16)

    def clear(i, carry):
        xb[i, :, pl.ds(0, PAD), :] = zrow
        xb[i, :, pl.ds(PAD + 80, PAD), :] = zrow
        return carry

    lax.fori_loop(0, 11, clear, 0)
    for b in range(4):
        part[b, 1, 1, 3] = jnp.zeros((80, 256), BF16)

    blank = jnp.zeros((3, 80, 128), BF16)

    @pl.when(edge)
    def _():
        for d in range(3):
            xb[jnp.where(zl == 0, d, 8 + d), :, pl.ds(PAD, 80), :] = blank

    loads[0].wait()
    loads[1].wait()
    xb[y + 3, :, pl.ds(PAD, 80), :] = xin[0:3]
    xb[y + 4, :, pl.ds(PAD, 80), :] = xin[12:15]

    def add_col(i, tot):
        return tot + jnp.sum(xin[i].astype(F32).reshape(10, 8, 128), axis=0)

    sums = lax.fori_loop(0, 15, add_col, jnp.zeros((8, 128), F32))
    colsum = jnp.sum(sums, axis=0, keepdims=True)
    pre = jnp.dot(
        jnp.broadcast_to(colsum, (8, 128)), wpool[...].astype(F32),
        precision=lax.Precision.HIGHEST, preferred_element_type=F32,
    )[0:1]
    poolsrc[0] = pre

    pl.semaphore_wait(barrier, 11 + edge.astype(jnp.int32))

    def remote(src, dst, ssem, rsem, dev):
        return pltpu.make_async_remote_copy(
            src_ref=src, dst_ref=dst, send_sem=ssem, recv_sem=rsem,
            device_id=dev, device_id_type=MESH_ID,
        )

    rows = pl.ds(PAD, 80)
    ycopies = []
    for g in range(1, 4):
        q = (5 * y + g) // 4
        copy = remote(
            xin.at[pl.ds(3 * g, 3)], xb.at[q + 3, :, rows, :],
            ys.at[g - 1], yr.at[g - 1], at(y_=(y + g) % 4),
        )
        copy.start()
        ycopies.append(copy)
    psends = {}

    def pool_send(src, slot_i, dev):
        psends[slot_i] = remote(src, poolbuf.at[slot_i], ps.at[slot_i], pr.at[slot_i], dev)
        psends[slot_i].start()

    def pool_get(slot_i):
        psends[slot_i].wait_recv()
        return poolbuf[slot_i]

    for d in range(1, 4):
        pool_send(poolsrc.at[0], d - 1, at(y_=(y + d) % 4))

    def halo_copy(d, side):
        q = (4 - d) if side == 0 else d
        q_to = q - 5 if side == 0 else q + 5
        return remote(
            xb.at[q + 3, :, rows, :], xb.at[q_to + 3, :, rows, :],
            hs.at[2 * d + side], hr.at[2 * d + side], east if side == 0 else west,
        )

    halo_out = (zl < 7, zl > 0)
    halo_in = (zl > 0, zl < 7)
    for d, sides in ((0, (0,)), (0, (1,)), (1, (0,)), (1, (1,)), (2, (0, 1))):
        q = (4 - d) if sides[0] == 0 else d
        g = (4 * q + y) % 5

        @pl.when(jnp.logical_and(g > 0, g < 4))
        def _():
            gi = jnp.clip(g - 1, 0, 2)
            remote(
                xin.at[pl.ds(0, 3)], xb.at[q + 3, :, rows, :], ys.at[gi], yr.at[gi], east
            ).wait_recv()

        for side in sides:
            pl.when(halo_out[side])(halo_copy(d, side).start)

    def halo_wait(d):
        for side in range(2):
            pl.when(halo_in[side])(halo_copy(d, side).wait_recv)

    loads[2].wait()
    loads[3].wait()

    def compute(b, lo, hi):
        def body(j, carry):
            q = block_of(j, zl)
            if b == 0:
                lhs = xb[q + 3, :, rows, :].reshape(240, 128)
                res = jnp.dot(lhs, pwv[...], preferred_element_type=F32)
            else:
                taps = []
                for ro in (-1, 0, 1):
                    for co in (-1, 0, 1):
                        taps.append(
                            xb[q + 3 + co * b, :, pl.ds(PAD + ro * b * 12, 80), :].reshape(240, 128)
                        )
                res = jnp.dot(
                    jnp.concatenate(taps, axis=1), wav[b - 1].reshape(1152, 256),
                    preferred_element_type=F32,
                )
            res = res.astype(BF16).reshape(3, 80, 256)
            for t in range(3):
                s = 3 * j + t
                part[b, (s // 4) % 2, s // 8, s % 4] = res[t]
            return carry

        lax.fori_loop(lo, hi, body, 0)

    core_copies, x_copies, z_copies = {}, {}, {}

    def core_send(b, h):
        copy = remote(
            part.at[b, 1 - c, h], cbuf.at[b, h], cs.at[b, h], cr.at[b, h], at(c_=1 - c)
        )
        copy.start()
        core_copies[b, h] = copy

    def core_reduce(b, h):
        core_copies[b, h].wait_recv()

        def body(i, carry):
            mine = part[b, c, h, i].astype(F32) + cbuf[b, h, i].astype(F32)
            part[b, c, h, i] = mine.astype(BF16)
            return carry

        lax.fori_loop(0, 4, body, 0)
        first = flip if h == 0 else 3 - x
        x_copies[b, h] = []
        for i, col in enumerate((first, (x + 2) % 4)):
            copy = remote(
                part.at[b, c, h, col], xbuf.at[b, h, i], xs.at[b, h, i], xr.at[b, h, i],
                at(x_=first),
            )
            copy.start()
            x_copies[b, h].append(copy)

    flip = x + 1 - 2 * (x % 2)

    def x_half(b, h):
        second = 3 - x if h == 0 else flip
        for copy in x_copies[b, h]:
            copy.wait_recv()
        give = part[b, c, h, second].astype(F32) + xbuf[b, h, 1].astype(F32)
        part[b, c, h, second] = give.astype(BF16)
        copy = remote(
            part.at[b, c, h, second], xbuf.at[b, h, 2], xs.at[b, h, 2], xr.at[b, h, 2],
            at(x_=second),
        )
        copy.start()
        x_copies[b, h].append(copy)
        xacc[b, h] = part[b, c, h, x].astype(F32) + xbuf[b, h, 0].astype(F32)

    def x_reduce(b, h):
        x_copies[b, h][2].wait_recv()
        zsrc[b, h] = (xacc[b, h] + xbuf[b, h, 2].astype(F32)).astype(BF16)
        up = (zh == h).astype(jnp.int32)
        z_copies[b, h] = remote(
            zsrc.at[b, h], zbuf.at[b, 1 - up], zs.at[b, h], zr.at[b, 1 - up], at_z(12 - 8 * up)
        )
        z_copies[b, h].start()

    extra = (
        (3, 0, 0, 3, 4), (3, 0, 1, 0, 4), (3, 1, 0, 0, 4),
        (2, 0, 1, 2, 4), (2, 1, 0, 0, 4), (1, 1, 0, 1, 4),
    )

    def within(to, lo, hi):
        return jnp.logical_and(to >= lo, to < hi)

    def extra_compute(b):
        col = jnp.where(zl == 7, 0, 2)
        kernel = jnp.concatenate([wav[b - 1, r * 3 + col] for r in range(3)], axis=0)

        def body(j, carry):
            q = jnp.where(zl == 7, 8 - j - b, j + b - 4)
            lhs = jnp.concatenate(
                [
                    xb[q + 3, :, pl.ds(PAD + ro * b * 12, 80), :].reshape(240, 128)
                    for ro in (-1, 0, 1)
                ],
                axis=1,
            )
            res = jnp.dot(lhs, kernel, preferred_element_type=F32)
            res = res.astype(BF16).reshape(3, 80, 256)
            for t in range(3):
                s = 3 * j + t
                part2[b - 1, (s // 4) % 2, s // 8, s % 4] = res[t]
            return carry

        lax.fori_loop(4 - b, 4, body, 0)

    def extra_core(b, h, cc, lo, hi):
        n = hi - lo
        return remote(
            part2.at[b - 1, cc, h, pl.ds(lo, n)], cbuf2.at[b - 1, h, pl.ds(lo, n)],
            cs2.at[b - 1, h], cr2.at[b - 1, h], at(c_=1 - c),
        )

    def extra_core_send(b):
        for u in extra:
            if u[0] == b:
                pl.when(c != u[2])(extra_core(*u).start)

    def extra_x(b, h, d):
        to = (x + d) % 4
        return remote(
            part2.at[b - 1, c, h, to], xbuf2.at[b - 1, h, d - 1],
            xs2.at[b - 1, h, d - 1], xr2.at[b - 1, h, d - 1], at(x_=to),
        )

    def extra_z(b, h):
        zz = (7 - zl + 4 + 8 * h) % 16
        return remote(
            zsrc2.at[b - 1, h], zbuf2.at[b - 1, zh], zs2.at[b - 1, h], zr2.at[b - 1, zh],
            ((zz % 8) * 4 + y, (zz // 8) * 8 + x * 2 + c),
        )

    def extra_core_reduce(b, h, cc, lo, hi):
        @pl.when(c == cc)
        def _():
            extra_core(b, h, cc, lo, hi).wait_recv()
            for i in range(lo, hi):
                mine = part2[b - 1, cc, h, i].astype(F32) + cbuf2[b - 1, h, i].astype(F32)
                part2[b - 1, cc, h, i] = mine.astype(BF16)
            for d in (2, 1, 3):
                pl.when(within((x + d) % 4, lo, hi))(extra_x(b, h, d).start)

    def extra_x_reduce(b, h, cc, lo, hi):
        @pl.when(jnp.logical_and(c == cc, within(x, lo, hi)))
        def _():
            t = part2[b - 1, cc, h, x].astype(F32)
            for d in (2, 1, 3):
                extra_x(b, h, d).wait_recv()
                t = t + xbuf2[b - 1, h, d - 1].astype(F32)
            zsrc2[b - 1, h] = t.astype(BF16)
            extra_z(b, h).start()

    def extra_sent(b, h, cc, lo, hi):
        pl.when(c != cc)(extra_core(b, h, cc, lo, hi).wait_send)

        @pl.when(c == cc)
        def _():
            for d in (2, 1, 3):
                pl.when(within((x + d) % 4, lo, hi))(extra_x(b, h, d).wait_send)
            pl.when(within(x, lo, hi))(extra_z(b, h).wait_send)

    compute(0, 0, 3)
    core_send(0, 0)
    compute(0, 3, 5)
    core_send(0, 1)
    compute(1, 0, 3)
    core_send(1, 0)
    own = poolsrc[0] + pool_get(0) + pool_get(1) + pool_get(2)
    poolsrc[1] = own
    pool_send(poolsrc.at[1], 3, at_z(4))
    pool_send(poolsrc.at[1], 4, at_z(12))
    core_reduce(0, 0)
    core_reduce(0, 1)

    @pl.when(edge)
    def _():
        for b in (3, 2, 1):
            extra_compute(b)
            extra_core_send(b)

    core_reduce(1, 0)
    halo_wait(0)
    compute(2, 0, 3)
    core_send(2, 0)
    compute(1, 3, 5)
    core_send(1, 1)

    @pl.when(edge)
    def _():
        for u in extra:
            extra_core_reduce(*u)

    x_half(0, 0)
    x_half(0, 1)
    core_reduce(2, 0)
    core_reduce(1, 1)
    halo_wait(1)
    compute(3, 0, 3)
    core_send(3, 0)
    compute(2, 3, 5)
    core_send(2, 1)
    three = own + pool_get(3) + pool_get(4)
    pool_send(poolbuf.at[4], 5, at_z(12))
    x_reduce(0, 0)
    x_reduce(0, 1)
    x_half(1, 0)
    core_reduce(3, 0)
    core_reduce(2, 1)
    halo_wait(2)
    compute(3, 3, 5)
    core_send(3, 1)
    x_half(2, 0)
    x_half(1, 1)
    x_reduce(1, 0)
    core_reduce(3, 1)
    four = three + pool_get(5)
    poolsrc[2] = four
    pool_send(poolsrc.at[2], 6, at(zl_=zl + 1 - 2 * (zl % 2)))

    @pl.when(edge)
    def _():
        for u in extra:
            extra_x_reduce(*u)

    x_half(3, 0)
    x_half(2, 1)
    x_reduce(2, 0)
    x_reduce(1, 1)

    pair = four + pool_get(6)
    poolsrc[3] = pair
    place = zl % 4
    middle = jnp.logical_or(place == 1, place == 2)

    def pool_copy(src, slot_i, dev):
        return remote(poolsrc.at[src], poolbuf.at[slot_i], ps.at[slot_i], pr.at[slot_i], dev)

    inward = pool_copy(3, 7, at(zl_=(zl + jnp.where(place == 1, 1, 7)) % 8))
    outward = pool_copy(4, 8, at(zl_=(zl + jnp.where(place == 1, 7, 1)) % 8))
    pl.when(middle)(inward.start)
    x_half(3, 1)
    x_reduce(3, 0)
    x_reduce(2, 1)

    @pl.when(middle)
    def _():
        inward.wait_recv()
        poolsrc[4] = poolsrc[3] + poolbuf[7]
        outward.start()

    x_reduce(3, 1)

    @pl.when(jnp.logical_not(middle))
    def _():
        outward.wait_recv()
        poolsrc[4] = poolbuf[8]

    pool_send(poolsrc.at[4], 9, at(c_=1 - c))
    for load in loads[4:]:
        load.wait()

    proj = jnp.zeros((80, 256), F32)
    for b in range(4):
        if b == 1:
            both = poolsrc[4] + pool_get(9)
            poolsrc[5] = both
            for d in range(1, 4):
                pool_send(poolsrc.at[5], 9 + d, at(x_=(x + d) % 4))
        if b == 3:
            pre_all = both + pool_get(10) + pool_get(11) + pool_get(12)
            pre_all = pre_all * (1.0 / 38400.0)
            pooled = jnp.maximum(gain[4:5] * pre_all + shift[4:5], 0.0).astype(BF16)
            pool_term = jnp.dot(
                jnp.broadcast_to(pooled, (16, 256)), wprojv[pl.ds(1024, 256), :],
                preferred_element_type=F32,
            )[0:1]
        for way in range(2):
            remote(
                zsrc.at[b, 0], zbuf.at[b, way], zs.at[b, 0], zr.at[b, way], at_z(4)
            ).wait_recv()
        acc[b] = zbuf[b, 0].astype(F32) + zbuf[b, 1].astype(F32)
        if b > 0:
            over = jnp.zeros((), jnp.bool_)
            for eb, eh, ec, lo, hi in extra:
                if eb == b:
                    mine = jnp.logical_and(bit == eh, c == ec)
                    over = jnp.logical_or(over, jnp.logical_and(mine, within(x, lo, hi)))

            @pl.when(jnp.logical_and(edge_owner, over))
            def _():
                for half in range(2):
                    remote(
                        zsrc2.at[b - 1, 0], zbuf2.at[b - 1, half],
                        zs2.at[b - 1, 0], zr2.at[b - 1, half], at_z(4),
                    ).wait_recv()
                acc[b] += zbuf2[b - 1, 0].astype(F32) + zbuf2[b - 1, 1].astype(F32)

        act = jnp.maximum(acc[b] * gain[b : b + 1] + shift[b : b + 1], 0.0).astype(BF16)
        proj = proj + jnp.dot(act, wprojv[pl.ds(b * 256, 256), :], preferred_element_type=F32)
    head = jnp.maximum(gain[5:6] * (proj + pool_term) + shift[5:6], 0.0)
    head = jnp.concatenate([head, jnp.zeros((48, 256), F32)], axis=0)
    stage[...] = jnp.transpose(head).astype(BF16).reshape(16, 16, 128)

    def out_copy(d):
        return remote(stage.at[d], obuf.at[slot], os.at[d], orr.at[slot], (zl_dst * 4 + y_dst, d))

    def out_send(i, carry):
        @pl.when(has_col)
        def _():
            out_copy((ch + i) % 16).start()

        return carry

    lax.fori_loop(0, 16, out_send, 0)
    for copy in ycopies + list(psends.values()):
        copy.wait_send()
    for d in range(3):
        for side in range(2):
            pl.when(halo_out[side])(halo_copy(d, side).wait_send)

    @pl.when(middle)
    def _():
        inward.wait_send()
        outward.wait_send()

    @pl.when(edge)
    def _():
        for u in extra:
            extra_sent(*u)

    for u in core_copies:
        for copy in [core_copies[u], z_copies[u]] + x_copies[u]:
            copy.wait_send()

    def out_recv(i, carry):
        remote(stage.at[0], obuf.at[i], os.at[0], orr.at[i], east).wait_recv()
        return carry

    lax.fori_loop(0, 15, out_recv, 0)
    out[...] = obuf[:, :, 0:80]

    def out_sent(d, carry):
        @pl.when(has_col)
        def _():
            out_copy(d).wait_send()

        return carry

    lax.fori_loop(0, 16, out_sent, 0)


def local(features, pointwise_weight, w_atrous, w_pool, w_proj, norm_gain, norm_shift):
    feat = jnp.transpose(features, (1, 0, 2))
    vmem = pl.BlockSpec(memory_space=pltpu.VMEM)
    hbm = pl.BlockSpec(memory_space=pl.ANY)
    dma = pltpu.SemaphoreType.DMA
    out = pl.pallas_call(
        head_kernel,
        out_shape=jax.ShapeDtypeStruct((15, 16, 80), BF16),
        in_specs=[hbm] * 7,
        out_specs=vmem,
        scratch_shapes=[
            pltpu.VMEM((15, 80, 128), BF16),
            pltpu.VMEM((11, 3, 80 + 2 * PAD, 128), BF16),
            pltpu.VMEM((4, 2, 2, 4, 80, 256), BF16),
            pltpu.VMEM((4, 2, 4, 80, 256), BF16),
            pltpu.VMEM((4, 2, 3, 80, 256), BF16),
            pltpu.VMEM((4, 2, 80, 256), BF16),
            pltpu.VMEM((4, 2, 80, 256), BF16),
            pltpu.VMEM((16, 16, 128), BF16),
            pltpu.VMEM((15, 16, 128), BF16),
            pltpu.VMEM((128, 256), BF16),
            pltpu.VMEM((3, 9, 128, 256), BF16),
            pltpu.VMEM((1280, 256), BF16),
            pltpu.VMEM((128, 256), BF16),
            pltpu.VMEM((6, 256), F32),
            pltpu.VMEM((6, 256), F32),
            pltpu.VMEM((6, 1, 256), F32),
            pltpu.VMEM((13, 1, 256), F32),
            pltpu.VMEM((3, 2, 2, 4, 80, 256), BF16),
            pltpu.VMEM((3, 2, 4, 80, 256), BF16),
            pltpu.VMEM((3, 2, 3, 80, 256), BF16),
            pltpu.VMEM((3, 2, 80, 256), BF16),
            pltpu.VMEM((3, 2, 80, 256), BF16),
            pltpu.VMEM((4, 80, 256), F32),
            pltpu.VMEM((4, 2, 80, 256), F32),
            dma((7,)),
            dma((3,)), dma((3,)),
            dma((6,)), dma((6,)),
            dma((4, 2)), dma((4, 2)),
            dma((4, 2, 3)), dma((4, 2, 3)),
            dma((4, 2)), dma((4, 2)),
            dma((16,)), dma((15,)),
            dma((13,)), dma((13,)),
            dma((3, 2)), dma((3, 2)),
            dma((3, 2, 3)), dma((3, 2, 3)),
            dma((3, 2)), dma((3, 2)),
        ],
        compiler_params=pltpu.CompilerParams(collective_id=0, has_side_effects=True),
        name="aspp_head",
    )(
        feat, pointwise_weight, w_atrous.reshape(3, 9, 128, 256), w_pool, w_proj,
        norm_gain, norm_shift,
    )
    return jnp.transpose(out, (2, 0, 1))


def solution(mesh):
    return jax.shard_map(
        local,
        mesh=mesh,
        in_specs=(
            P(None, "lon", "ch"),
            P("ch", None),
            P(None, None, None, "ch", None),
            P("ch", None),
            P(),
            P(),
            P(),
        ),
        out_specs=P(None, "lon", "ch"),
        check_vma=False,
    )
```

```python
import jax
import jax.numpy as jnp
from jax import lax
from jax.experimental import pallas as pl
from jax.experimental.pallas import tpu as pltpu
from jax.sharding import PartitionSpec as P

MESH_ID = pl.DeviceIdType.MESH
F32 = jnp.float32
BF16 = jnp.bfloat16

PAD = 48


def head_kernel(
    feat, pw, wa, wpool_h, wproj, gain_h, shift_h, out,
    xin, xb, part, cbuf, xbuf, zsrc, zbuf, stage, obuf,
    pwv, wav, wprojv, wpool, gain, shift, poolsrc, poolbuf,
    part2, cbuf2, xbuf2, zsrc2, zbuf2, acc, xacc,
    ld_sem, ys, yr, hs, hr, cs, cr, xs, xr, zs, zr, os, orr, ps, pr,
    cs2, cr2, xs2, xr2, zs2, zr2,
):
    lon = lax.axis_index("lon")
    ch = lax.axis_index("ch")
    zl, y = lon // 4, lon % 4
    zh, x, c = ch // 8, (ch // 2) % 4, ch % 2
    z = zh * 8 + zl

    def at(zl_=None, y_=None, x_=None, c_=None):
        zz = zl if zl_ is None else zl_
        yy = y if y_ is None else y_
        xx = x if x_ is None else x_
        cc = c if c_ is None else c_
        return (zz * 4 + yy, zh * 8 + xx * 2 + cc)

    def at_z(dz):
        zz = (z + dz) % 16
        return ((zz % 8) * 4 + y, (zz // 8) * 8 + x * 2 + c)

    def block_of(j, level):
        q = (j + 1) % 5
        return jnp.where(level == 0, 4 - q, q)

    bit = ((z + 12) % 16) // 8
    zl_dst = (zl + 4) % 8
    k = bit * 8 + c * 4 + x
    kj, kt = k // 3, k % 3
    kq = block_of(kj, zl_dst)
    kg = 4 * kq + y
    y_dst = kg // 5
    slot = (kg % 5) * 3 + kt
    has_col = k < 15

    barrier = pltpu.get_barrier_semaphore()

    def hello(dev):
        pl.semaphore_signal(barrier, inc=1, device_id=dev, device_id_type=MESH_ID)

    east, west = at(zl_=(zl + 1) % 8), at(zl_=(zl + 7) % 8)
    edge = jnp.logical_or(zl == 0, zl == 7)
    edge_owner = jnp.logical_or(zl == 3, zl == 4)

    @pl.when(edge_owner)
    def _():
        far = jnp.where(zl == 4, 7, 0) * 4 + y
        hello((far, x * 2 + c))
        hello((far, 8 + x * 2 + c))

    @pl.when(zl < 7)
    def _():
        hello(east)

    @pl.when(zl > 0)
    def _():
        hello(west)

    hello(at_z(4))
    hello(at_z(12))

    for d in range(1, 4):
        hello(at(y_=(y + d) % 4))
        hello(at(x_=(x + d) % 4))
    hello(at(c_=1 - c))

    loads = [
        pltpu.make_async_copy(src, dst, ld_sem.at[i])
        for i, (src, dst) in enumerate((
            (feat, xin), (wpool_h, wpool), (pw, pwv), (wa, wav),
            (wproj, wprojv), (gain_h, gain), (shift_h, shift),
        ))
    ]
    for load in loads:
        load.start()

    zrow = jnp.zeros((3, PAD, 128), BF16)

    def clear(i, carry):
        xb[i, :, pl.ds(0, PAD), :] = zrow
        xb[i, :, pl.ds(PAD + 80, PAD), :] = zrow
        return carry

    lax.fori_loop(0, 11, clear, 0)
    for b in range(4):
        part[b, 1, 1, 3] = jnp.zeros((80, 256), BF16)

    blank = jnp.zeros((3, 80, 128), BF16)

    @pl.when(edge)
    def _():
        for d in range(3):
            xb[jnp.where(zl == 0, d, 8 + d), :, pl.ds(PAD, 80), :] = blank

    loads[0].wait()
    loads[1].wait()
    xb[y + 3, :, pl.ds(PAD, 80), :] = xin[0:3]
    xb[y + 4, :, pl.ds(PAD, 80), :] = xin[12:15]

    def add_col(i, tot):
        return tot + jnp.sum(xin[i].astype(F32).reshape(10, 8, 128), axis=0)

    sums = lax.fori_loop(0, 15, add_col, jnp.zeros((8, 128), F32))
    colsum = jnp.sum(sums, axis=0, keepdims=True)
    pre = jnp.dot(
        jnp.broadcast_to(colsum, (8, 128)), wpool[...].astype(F32),
        precision=lax.Precision.HIGHEST, preferred_element_type=F32,
    )[0:1]
    poolsrc[0] = pre

    pl.semaphore_wait(barrier, 11 + edge.astype(jnp.int32))

    def remote(src, dst, ssem, rsem, dev):
        return pltpu.make_async_remote_copy(
            src_ref=src, dst_ref=dst, send_sem=ssem, recv_sem=rsem,
            device_id=dev, device_id_type=MESH_ID,
        )

    rows = pl.ds(PAD, 80)
    ycopies = []
    for g in range(1, 4):
        q = (5 * y + g) // 4
        copy = remote(
            xin.at[pl.ds(3 * g, 3)], xb.at[q + 3, :, rows, :],
            ys.at[g - 1], yr.at[g - 1], at(y_=(y + g) % 4),
        )
        copy.start()
        ycopies.append(copy)
    psends = {}

    def pool_send(src, slot_i, dev):
        psends[slot_i] = remote(src, poolbuf.at[slot_i], ps.at[slot_i], pr.at[slot_i], dev)
        psends[slot_i].start()

    def pool_get(slot_i):
        psends[slot_i].wait_recv()
        return poolbuf[slot_i]

    for d in range(1, 4):
        pool_send(poolsrc.at[0], d - 1, at(y_=(y + d) % 4))

    def halo_copy(d, side):
        q = (4 - d) if side == 0 else d
        q_to = q - 5 if side == 0 else q + 5
        return remote(
            xb.at[q + 3, :, rows, :], xb.at[q_to + 3, :, rows, :],
            hs.at[2 * d + side], hr.at[2 * d + side], east if side == 0 else west,
        )

    halo_out = (zl < 7, zl > 0)
    halo_in = (zl > 0, zl < 7)
    for d, sides in ((0, (0,)), (0, (1,)), (1, (0,)), (1, (1,)), (2, (0, 1))):
        q = (4 - d) if sides[0] == 0 else d
        g = (4 * q + y) % 5

        @pl.when(jnp.logical_and(g > 0, g < 4))
        def _():
            gi = jnp.clip(g - 1, 0, 2)
            remote(
                xin.at[pl.ds(0, 3)], xb.at[q + 3, :, rows, :], ys.at[gi], yr.at[gi], east
            ).wait_recv()

        for side in sides:
            pl.when(halo_out[side])(halo_copy(d, side).start)

    def halo_wait(d):
        for side in range(2):
            pl.when(halo_in[side])(halo_copy(d, side).wait_recv)

    loads[2].wait()
    loads[3].wait()

    def compute(b, lo, hi):
        def body(j, carry):
            q = block_of(j, zl)
            if b == 0:
                lhs = xb[q + 3, :, rows, :].reshape(240, 128)
                res = jnp.dot(lhs, pwv[...], preferred_element_type=F32)
            else:
                taps = []
                for ro in (-1, 0, 1):
                    for co in (-1, 0, 1):
                        taps.append(
                            xb[q + 3 + co * b, :, pl.ds(PAD + ro * b * 12, 80), :].reshape(240, 128)
                        )
                res = jnp.dot(
                    jnp.concatenate(taps, axis=1), wav[b - 1].reshape(1152, 256),
                    preferred_element_type=F32,
                )
            res = res.astype(BF16).reshape(3, 80, 256)
            for t in range(3):
                s = 3 * j + t
                part[b, (s // 4) % 2, s // 8, s % 4] = res[t]
            return carry

        lax.fori_loop(lo, hi, body, 0)

    core_copies, x_copies, z_copies = {}, {}, {}

    def core_send(b, h):
        copy = remote(
            part.at[b, 1 - c, h], cbuf.at[b, h], cs.at[b, h], cr.at[b, h], at(c_=1 - c)
        )
        copy.start()
        core_copies[b, h] = copy

    def core_reduce(b, h):
        core_copies[b, h].wait_recv()

        def body(i, carry):
            mine = part[b, c, h, i].astype(F32) + cbuf[b, h, i].astype(F32)
            part[b, c, h, i] = mine.astype(BF16)
            return carry

        lax.fori_loop(0, 4, body, 0)
        first = flip if h == 0 else 3 - x
        x_copies[b, h] = []
        for i, col in enumerate((first, (x + 2) % 4)):
            copy = remote(
                part.at[b, c, h, col], xbuf.at[b, h, i], xs.at[b, h, i], xr.at[b, h, i],
                at(x_=first),
            )
            copy.start()
            x_copies[b, h].append(copy)

    flip = x + 1 - 2 * (x % 2)

    def x_half(b, h):
        second = 3 - x if h == 0 else flip
        for copy in x_copies[b, h]:
            copy.wait_recv()
        give = part[b, c, h, second].astype(F32) + xbuf[b, h, 1].astype(F32)
        part[b, c, h, second] = give.astype(BF16)
        copy = remote(
            part.at[b, c, h, second], xbuf.at[b, h, 2], xs.at[b, h, 2], xr.at[b, h, 2],
            at(x_=second),
        )
        copy.start()
        x_copies[b, h].append(copy)
        xacc[b, h] = part[b, c, h, x].astype(F32) + xbuf[b, h, 0].astype(F32)

    def x_reduce(b, h):
        x_copies[b, h][2].wait_recv()
        zsrc[b, h] = (xacc[b, h] + xbuf[b, h, 2].astype(F32)).astype(BF16)
        up = (zh == h).astype(jnp.int32)
        z_copies[b, h] = remote(
            zsrc.at[b, h], zbuf.at[b, 1 - up], zs.at[b, h], zr.at[b, 1 - up], at_z(12 - 8 * up)
        )
        z_copies[b, h].start()

    extra = (
        (3, 0, 0, 3, 4), (3, 0, 1, 0, 4), (3, 1, 0, 0, 4),
        (2, 0, 1, 2, 4), (2, 1, 0, 0, 4), (1, 1, 0, 1, 4),
    )

    def within(to, lo, hi):
        return jnp.logical_and(to >= lo, to < hi)

    def extra_compute(b):
        col = jnp.where(zl == 7, 0, 2)
        kernel = jnp.concatenate([wav[b - 1, r * 3 + col] for r in range(3)], axis=0)

        def body(j, carry):
            q = jnp.where(zl == 7, 8 - j - b, j + b - 4)
            lhs = jnp.concatenate(
                [
                    xb[q + 3, :, pl.ds(PAD + ro * b * 12, 80), :].reshape(240, 128)
                    for ro in (-1, 0, 1)
                ],
                axis=1,
            )
            res = jnp.dot(lhs, kernel, preferred_element_type=F32)
            res = res.astype(BF16).reshape(3, 80, 256)
            for t in range(3):
                s = 3 * j + t
                part2[b - 1, (s // 4) % 2, s // 8, s % 4] = res[t]
            return carry

        lax.fori_loop(4 - b, 4, body, 0)

    def extra_core(b, h, cc, lo, hi):
        n = hi - lo
        return remote(
            part2.at[b - 1, cc, h, pl.ds(lo, n)], cbuf2.at[b - 1, h, pl.ds(lo, n)],
            cs2.at[b - 1, h], cr2.at[b - 1, h], at(c_=1 - c),
        )

    def extra_core_send(b):
        for u in extra:
            if u[0] == b:
                pl.when(c != u[2])(extra_core(*u).start)

    def extra_x(b, h, d):
        to = (x + d) % 4
        return remote(
            part2.at[b - 1, c, h, to], xbuf2.at[b - 1, h, d - 1],
            xs2.at[b - 1, h, d - 1], xr2.at[b - 1, h, d - 1], at(x_=to),
        )

    def extra_z(b, h):
        zz = (7 - zl + 4 + 8 * h) % 16
        return remote(
            zsrc2.at[b - 1, h], zbuf2.at[b - 1, zh], zs2.at[b - 1, h], zr2.at[b - 1, zh],
            ((zz % 8) * 4 + y, (zz // 8) * 8 + x * 2 + c),
        )

    def extra_core_reduce(b, h, cc, lo, hi):
        @pl.when(c == cc)
        def _():
            extra_core(b, h, cc, lo, hi).wait_recv()
            for i in range(lo, hi):
                mine = part2[b - 1, cc, h, i].astype(F32) + cbuf2[b - 1, h, i].astype(F32)
                part2[b - 1, cc, h, i] = mine.astype(BF16)
            for d in (2, 1, 3):
                pl.when(within((x + d) % 4, lo, hi))(extra_x(b, h, d).start)

    def extra_x_reduce(b, h, cc, lo, hi):
        @pl.when(jnp.logical_and(c == cc, within(x, lo, hi)))
        def _():
            t = part2[b - 1, cc, h, x].astype(F32)
            for d in (2, 1, 3):
                extra_x(b, h, d).wait_recv()
                t = t + xbuf2[b - 1, h, d - 1].astype(F32)
            zsrc2[b - 1, h] = t.astype(BF16)
            extra_z(b, h).start()

    def extra_sent(b, h, cc, lo, hi):
        pl.when(c != cc)(extra_core(b, h, cc, lo, hi).wait_send)

        @pl.when(c == cc)
        def _():
            for d in (2, 1, 3):
                pl.when(within((x + d) % 4, lo, hi))(extra_x(b, h, d).wait_send)
            pl.when(within(x, lo, hi))(extra_z(b, h).wait_send)

    def extra_step(step):
        @pl.when(edge)
        def _():
            for u in extra:
                step(*u)

    own = poolsrc[0] + pool_get(0) + pool_get(1) + pool_get(2)
    poolsrc[1] = own
    pool_send(poolsrc.at[1], 9, at(c_=1 - c))
    compute(0, 0, 3)
    core_send(0, 0)
    compute(0, 3, 5)
    core_send(0, 1)
    compute(1, 0, 3)
    core_send(1, 0)
    both = own + pool_get(9)
    poolsrc[5] = both
    for d in range(1, 4):
        pool_send(poolsrc.at[5], 9 + d, at(x_=(x + d) % 4))
    core_reduce(0, 0)
    core_reduce(0, 1)

    @pl.when(edge)
    def _():
        for b in (3, 2, 1):
            extra_compute(b)
            extra_core_send(b)

    core_reduce(1, 0)
    extra_step(extra_core_reduce)
    here = both + pool_get(10) + pool_get(11) + pool_get(12)
    poolsrc[2] = here
    pool_send(poolsrc.at[2], 3, at_z(4))
    pool_send(poolsrc.at[2], 4, at_z(12))
    halo_wait(0)
    compute(2, 0, 3)
    core_send(2, 0)
    compute(1, 3, 5)
    core_send(1, 1)
    x_half(0, 0)
    x_half(0, 1)
    core_reduce(2, 0)
    core_reduce(1, 1)
    halo_wait(1)
    compute(3, 0, 3)
    core_send(3, 0)
    compute(2, 3, 5)
    core_send(2, 1)
    x_reduce(0, 0)
    x_reduce(0, 1)
    x_half(1, 0)
    core_reduce(3, 0)
    core_reduce(2, 1)
    three = here + pool_get(3) + pool_get(4)
    pool_send(poolbuf.at[4], 5, at_z(12))
    halo_wait(2)
    compute(3, 3, 5)
    core_send(3, 1)
    extra_step(extra_x_reduce)
    x_half(2, 0)
    x_half(1, 1)
    x_reduce(1, 0)
    core_reduce(3, 1)
    x_half(3, 0)
    x_half(2, 1)
    four = three + pool_get(5)
    poolsrc[3] = four
    pool_send(poolsrc.at[3], 6, at(zl_=zl + 1 - 2 * (zl % 2)))
    x_reduce(2, 0)
    x_reduce(1, 1)

    place = zl % 4
    middle = jnp.logical_or(place == 1, place == 2)

    def pool_copy(src, slot_i, dev):
        return remote(poolsrc.at[src], poolbuf.at[slot_i], ps.at[slot_i], pr.at[slot_i], dev)

    inward = pool_copy(6, 7, at(zl_=(zl + jnp.where(place == 1, 1, 7)) % 8))
    outward = pool_copy(4, 8, at(zl_=(zl + jnp.where(place == 1, 7, 1)) % 8))
    x_half(3, 1)
    x_reduce(3, 0)
    poolsrc[6] = four + pool_get(6)
    pl.when(middle)(inward.start)
    x_reduce(2, 1)
    x_reduce(3, 1)

    @pl.when(middle)
    def _():
        inward.wait_recv()
        poolsrc[4] = poolsrc[6] + poolbuf[7]
        outward.start()

    for load in loads[4:]:
        load.wait()

    proj = jnp.zeros((80, 256), F32)
    for b in range(4):
        if b == 3:
            @pl.when(jnp.logical_not(middle))
            def _():
                outward.wait_recv()
                poolsrc[4] = poolbuf[8]

            pre_all = poolsrc[4] * (1.0 / 38400.0)
            pooled = jnp.maximum(gain[4:5] * pre_all + shift[4:5], 0.0).astype(BF16)
            pool_term = jnp.dot(
                jnp.broadcast_to(pooled, (16, 256)), wprojv[pl.ds(1024, 256), :],
                preferred_element_type=F32,
            )[0:1]
        for way in range(2):
            remote(
                zsrc.at[b, 0], zbuf.at[b, way], zs.at[b, 0], zr.at[b, way], at_z(4)
            ).wait_recv()
        acc[b] = zbuf[b, 0].astype(F32) + zbuf[b, 1].astype(F32)
        if b > 0:
            over = jnp.zeros((), jnp.bool_)
            for eb, eh, ec, lo, hi in extra:
                if eb == b:
                    mine = jnp.logical_and(bit == eh, c == ec)
                    over = jnp.logical_or(over, jnp.logical_and(mine, within(x, lo, hi)))

            @pl.when(jnp.logical_and(edge_owner, over))
            def _():
                for half in range(2):
                    remote(
                        zsrc2.at[b - 1, 0], zbuf2.at[b - 1, half],
                        zs2.at[b - 1, 0], zr2.at[b - 1, half], at_z(4),
                    ).wait_recv()
                acc[b] += zbuf2[b - 1, 0].astype(F32) + zbuf2[b - 1, 1].astype(F32)

        act = jnp.maximum(acc[b] * gain[b : b + 1] + shift[b : b + 1], 0.0).astype(BF16)
        proj = proj + jnp.dot(act, wprojv[pl.ds(b * 256, 256), :], preferred_element_type=F32)
    head = jnp.maximum(gain[5:6] * (proj + pool_term) + shift[5:6], 0.0)
    head = jnp.concatenate([head, jnp.zeros((48, 256), F32)], axis=0)
    stage[...] = jnp.transpose(head).astype(BF16).reshape(16, 16, 128)

    def out_copy(d):
        return remote(stage.at[d], obuf.at[slot], os.at[d], orr.at[slot], (zl_dst * 4 + y_dst, d))

    def out_send(i, carry):
        @pl.when(has_col)
        def _():
            out_copy((ch + i) % 16).start()

        return carry

    lax.fori_loop(0, 16, out_send, 0)
    for copy in ycopies + list(psends.values()):
        copy.wait_send()
    for d in range(3):
        for side in range(2):
            pl.when(halo_out[side])(halo_copy(d, side).wait_send)

    @pl.when(middle)
    def _():
        inward.wait_send()
        outward.wait_send()

    @pl.when(edge)
    def _():
        for u in extra:
            extra_sent(*u)

    for u in core_copies:
        for copy in [core_copies[u], z_copies[u]] + x_copies[u]:
            copy.wait_send()

    def out_recv(i, carry):
        remote(stage.at[0], obuf.at[i], os.at[0], orr.at[i], east).wait_recv()
        return carry

    lax.fori_loop(0, 15, out_recv, 0)
    out[...] = obuf[:, :, 0:80]

    def out_sent(d, carry):
        @pl.when(has_col)
        def _():
            out_copy(d).wait_send()

        return carry

    lax.fori_loop(0, 16, out_sent, 0)


def local(features, pointwise_weight, w_atrous, w_pool, w_proj, norm_gain, norm_shift):
    feat = jnp.transpose(features, (1, 0, 2))
    vmem = pl.BlockSpec(memory_space=pltpu.VMEM)
    hbm = pl.BlockSpec(memory_space=pl.ANY)
    dma = pltpu.SemaphoreType.DMA
    out = pl.pallas_call(
        head_kernel,
        out_shape=pltpu.VMEM((15, 16, 80), BF16),
        in_specs=[hbm] * 7,
        out_specs=vmem,
        scratch_shapes=[
            pltpu.VMEM((15, 80, 128), BF16),
            pltpu.VMEM((11, 3, 80 + 2 * PAD, 128), BF16),
            pltpu.VMEM((4, 2, 2, 4, 80, 256), BF16),
            pltpu.VMEM((4, 2, 4, 80, 256), BF16),
            pltpu.VMEM((4, 2, 3, 80, 256), BF16),
            pltpu.VMEM((4, 2, 80, 256), BF16),
            pltpu.VMEM((4, 2, 80, 256), BF16),
            pltpu.VMEM((16, 16, 128), BF16),
            pltpu.VMEM((15, 16, 128), BF16),
            pltpu.VMEM((128, 256), BF16),
            pltpu.VMEM((3, 9, 128, 256), BF16),
            pltpu.VMEM((1280, 256), BF16),
            pltpu.VMEM((128, 256), BF16),
            pltpu.VMEM((6, 256), F32),
            pltpu.VMEM((6, 256), F32),
            pltpu.VMEM((7, 1, 256), F32),
            pltpu.VMEM((13, 1, 256), F32),
            pltpu.VMEM((3, 2, 2, 4, 80, 256), BF16),
            pltpu.VMEM((3, 2, 4, 80, 256), BF16),
            pltpu.VMEM((3, 2, 3, 80, 256), BF16),
            pltpu.VMEM((3, 2, 80, 256), BF16),
            pltpu.VMEM((3, 2, 80, 256), BF16),
            pltpu.VMEM((4, 80, 256), F32),
            pltpu.VMEM((4, 2, 80, 256), F32),
            dma((7,)),
            dma((3,)), dma((3,)),
            dma((6,)), dma((6,)),
            dma((4, 2)), dma((4, 2)),
            dma((4, 2, 3)), dma((4, 2, 3)),
            dma((4, 2)), dma((4, 2)),
            dma((16,)), dma((15,)),
            dma((13,)), dma((13,)),
            dma((3, 2)), dma((3, 2)),
            dma((3, 2, 3)), dma((3, 2, 3)),
            dma((3, 2)), dma((3, 2)),
        ],
        compiler_params=pltpu.CompilerParams(collective_id=0, has_side_effects=True),
        name="aspp_head",
    )(
        feat, pointwise_weight, w_atrous.reshape(3, 9, 128, 256), w_pool, w_proj,
        norm_gain, norm_shift,
    )
    return jnp.transpose(out, (2, 0, 1))


def solution(mesh):
    return jax.shard_map(
        local,
        mesh=mesh,
        in_specs=(
            P(None, "lon", "ch"),
            P("ch", None),
            P(None, None, None, "ch", None),
            P("ch", None),
            P(),
            P(),
            P(),
        ),
        out_specs=P(None, "lon", "ch"),
        check_vma=False,
    )
```

```python
import jax
import jax.numpy as jnp
from jax import lax
from jax.experimental import pallas as pl
from jax.experimental.pallas import tpu as pltpu
from jax.sharding import PartitionSpec as P

MESH_ID = pl.DeviceIdType.MESH
F32 = jnp.float32
BF16 = jnp.bfloat16

PAD = 48


def head_kernel(
    feat, pw, wa, wpool_h, wproj, gain_h, shift_h, out,
    xin, xb, part, cbuf, xbuf, zsrc, zbuf, stage, obuf,
    pwv, wav, wprojv, wpool, gain, shift, poolsrc, poolbuf,
    part2, cbuf2, xbuf2, zsrc2, zbuf2, acc, xacc,
    ld_sem, ys, yr, hs, hr, cs, cr, xs, xr, zs, zr, os, orr, ps, pr,
    cs2, cr2, xs2, xr2, zs2, zr2, reach,
):
    lon = lax.axis_index("lon")
    ch = lax.axis_index("ch")
    zl, y = lon // 4, lon % 4
    zh, x, c = ch // 8, (ch // 2) % 4, ch % 2
    z = zh * 8 + zl

    def at(zl_=None, y_=None, x_=None, c_=None):
        zz = zl if zl_ is None else zl_
        yy = y if y_ is None else y_
        xx = x if x_ is None else x_
        cc = c if c_ is None else c_
        return (zz * 4 + yy, zh * 8 + xx * 2 + cc)

    def at_z(dz):
        zz = (z + dz) % 16
        return ((zz % 8) * 4 + y, (zz // 8) * 8 + x * 2 + c)

    def block_of(j, level):
        q = (j + 1) % 5
        return jnp.where(level == 0, 4 - q, q)

    bit = ((z + 12) % 16) // 8
    zl_dst = (zl + 4) % 8
    k = bit * 8 + c * 4 + x
    kj, kt = k // 3, k % 3
    kq = block_of(kj, zl_dst)
    kg = 4 * kq + y
    y_dst = kg // 5
    slot = (kg % 5) * 3 + kt
    has_col = k < 15

    barrier = pltpu.get_barrier_semaphore()

    def hello(dev):
        pl.semaphore_signal(barrier, inc=1, device_id=dev, device_id_type=MESH_ID)

    east, west = at(zl_=(zl + 1) % 8), at(zl_=(zl + 7) % 8)
    edge = jnp.logical_or(zl == 0, zl == 7)
    edge_owner = jnp.logical_or(zl == 3, zl == 4)

    hello(at_z(1))
    hello(at_z(15))
    for d in range(1, 4):
        hello(at(y_=(y + d) % 4))
        hello(at(x_=(x + d) % 4))
    hello(at(c_=1 - c))

    loads = [
        pltpu.make_async_copy(src, dst, ld_sem.at[i])
        for i, (src, dst) in enumerate((
            (feat, xin), (wpool_h, wpool), (pw, pwv), (wa, wav),
            (wproj, wprojv), (gain_h, gain), (shift_h, shift),
        ))
    ]
    for load in loads:
        load.start()

    pl.semaphore_wait(barrier, 9)

    def remote(src, dst, ssem, rsem, dev):
        return pltpu.make_async_remote_copy(
            src_ref=src, dst_ref=dst, send_sem=ssem, recv_sem=rsem,
            device_id=dev, device_id_type=MESH_ID,
        )

    def reach_signal(r):
        for dz in (1, 15):
            pl.semaphore_signal(
                reach.at[r], inc=1, device_id=at_z(dz), device_id_type=MESH_ID
            )

    def reach_wait(r):
        pl.semaphore_wait(reach.at[r], 2)

    rows = pl.ds(PAD, 80)
    ycopies = []
    for g in range(1, 4):
        q = (5 * y + g) // 4
        copy = remote(
            feat.at[pl.ds(3 * g, 3)], xb.at[q + 3, :, rows, :],
            ys.at[g - 1], yr.at[g - 1], at(y_=(y + g) % 4),
        )
        copy.start()
        ycopies.append(copy)
    psends = {}

    def pool_send(src, slot_i, dev):
        psends[slot_i] = remote(src, poolbuf.at[slot_i], ps.at[slot_i], pr.at[slot_i], dev)
        psends[slot_i].start()

    def pool_get(slot_i):
        psends[slot_i].wait_recv()
        return poolbuf[slot_i]

    loads[0].wait()
    xb[y + 3, :, rows, :] = xin[0:3]
    xb[y + 4, :, rows, :] = xin[12:15]
    reach_signal(0)

    def halo_copy(d, side):
        q = (4 - d) if side == 0 else d
        q_to = q - 5 if side == 0 else q + 5
        return remote(
            xb.at[q + 3, :, rows, :], xb.at[q_to + 3, :, rows, :],
            hs.at[2 * d + side], hr.at[2 * d + side], east if side == 0 else west,
        )

    halo_out = (zl < 7, zl > 0)
    halo_in = (zl > 0, zl < 7)
    for d, sides in ((0, (0,)), (0, (1,)), (1, (0,)), (1, (1,)), (2, (0, 1))):
        q = (4 - d) if sides[0] == 0 else d
        g = (4 * q + y) % 5

        @pl.when(jnp.logical_and(g > 0, g < 4))
        def _():
            gi = jnp.clip(g - 1, 0, 2)
            remote(
                xin.at[pl.ds(0, 3)], xb.at[q + 3, :, rows, :], ys.at[gi], yr.at[gi], east
            ).wait_recv()

        for side in sides:
            pl.when(halo_out[side])(halo_copy(d, side).start)

    reach_wait(0)
    reach_signal(1)
    zrow = jnp.zeros((3, PAD, 128), BF16)

    def clear(i, carry):
        xb[i, :, pl.ds(0, PAD), :] = zrow
        xb[i, :, pl.ds(PAD + 80, PAD), :] = zrow
        return carry

    lax.fori_loop(0, 11, clear, 0)
    for b in range(4):
        part[b, 1, 1, 3] = jnp.zeros((80, 256), BF16)

    blank = jnp.zeros((3, 80, 128), BF16)

    @pl.when(edge)
    def _():
        for d in range(3):
            xb[jnp.where(zl == 0, d, 8 + d), :, pl.ds(PAD, 80), :] = blank

    loads[1].wait()

    def add_col(i, tot):
        return tot + jnp.sum(xin[i].astype(F32).reshape(10, 8, 128), axis=0)

    sums = lax.fori_loop(0, 15, add_col, jnp.zeros((8, 128), F32))
    colsum = jnp.sum(sums, axis=0, keepdims=True)
    pre = jnp.dot(
        jnp.broadcast_to(colsum, (8, 128)), wpool[...].astype(F32),
        precision=lax.Precision.HIGHEST, preferred_element_type=F32,
    )[0:1]
    poolsrc[0] = pre

    for d in range(1, 4):
        pool_send(poolsrc.at[0], d - 1, at(y_=(y + d) % 4))

    def halo_wait(d):
        for side in range(2):
            pl.when(halo_in[side])(halo_copy(d, side).wait_recv)

    loads[2].wait()
    loads[3].wait()

    def compute(b, lo, hi):
        def body(j, carry):
            q = block_of(j, zl)
            if b == 0:
                lhs = xb[q + 3, :, rows, :].reshape(240, 128)
                res = jnp.dot(lhs, pwv[...], preferred_element_type=F32)
            else:
                taps = []
                for ro in (-1, 0, 1):
                    for co in (-1, 0, 1):
                        taps.append(
                            xb[q + 3 + co * b, :, pl.ds(PAD + ro * b * 12, 80), :].reshape(240, 128)
                        )
                res = jnp.dot(
                    jnp.concatenate(taps, axis=1), wav[b - 1].reshape(1152, 256),
                    preferred_element_type=F32,
                )
            res = res.astype(BF16).reshape(3, 80, 256)
            for t in range(3):
                s = 3 * j + t
                part[b, (s // 4) % 2, s // 8, s % 4] = res[t]
            return carry

        lax.fori_loop(lo, hi, body, 0)

    core_copies, x_copies, z_copies = {}, {}, {}

    def core_send(b, h):
        copy = remote(
            part.at[b, 1 - c, h], cbuf.at[b, h], cs.at[b, h], cr.at[b, h], at(c_=1 - c)
        )
        copy.start()
        core_copies[b, h] = copy

    def core_reduce(b, h):
        core_copies[b, h].wait_recv()

        def body(i, carry):
            mine = part[b, c, h, i].astype(F32) + cbuf[b, h, i].astype(F32)
            part[b, c, h, i] = mine.astype(BF16)
            return carry

        lax.fori_loop(0, 4, body, 0)
        first = flip if h == 0 else 3 - x
        x_copies[b, h] = []
        for i, col in enumerate((first, (x + 2) % 4)):
            copy = remote(
                part.at[b, c, h, col], xbuf.at[b, h, i], xs.at[b, h, i], xr.at[b, h, i],
                at(x_=first),
            )
            copy.start()
            x_copies[b, h].append(copy)

    flip = x + 1 - 2 * (x % 2)

    def x_half(b, h):
        second = 3 - x if h == 0 else flip
        for copy in x_copies[b, h]:
            copy.wait_recv()
        give = part[b, c, h, second].astype(F32) + xbuf[b, h, 1].astype(F32)
        part[b, c, h, second] = give.astype(BF16)
        copy = remote(
            part.at[b, c, h, second], xbuf.at[b, h, 2], xs.at[b, h, 2], xr.at[b, h, 2],
            at(x_=second),
        )
        copy.start()
        x_copies[b, h].append(copy)
        xacc[b, h] = part[b, c, h, x].astype(F32) + xbuf[b, h, 0].astype(F32)

    def x_reduce(b, h):
        x_copies[b, h][2].wait_recv()
        zsrc[b, h] = (xacc[b, h] + xbuf[b, h, 2].astype(F32)).astype(BF16)
        up = (zh == h).astype(jnp.int32)
        z_copies[b, h] = remote(
            zsrc.at[b, h], zbuf.at[b, 1 - up], zs.at[b, h], zr.at[b, 1 - up], at_z(12 - 8 * up)
        )
        z_copies[b, h].start()

    extra = (
        (3, 0, 0, 3, 4), (3, 0, 1, 0, 4), (3, 1, 0, 0, 4),
        (2, 0, 1, 2, 4), (2, 1, 0, 0, 4), (1, 1, 0, 1, 4),
    )

    def within(to, lo, hi):
        return jnp.logical_and(to >= lo, to < hi)

    def extra_compute(b):
        col = jnp.where(zl == 7, 0, 2)
        kernel = jnp.concatenate([wav[b - 1, r * 3 + col] for r in range(3)], axis=0)

        def body(j, carry):
            q = jnp.where(zl == 7, 8 - j - b, j + b - 4)
            lhs = jnp.concatenate(
                [
                    xb[q + 3, :, pl.ds(PAD + ro * b * 12, 80), :].reshape(240, 128)
                    for ro in (-1, 0, 1)
                ],
                axis=1,
            )
            res = jnp.dot(lhs, kernel, preferred_element_type=F32)
            res = res.astype(BF16).reshape(3, 80, 256)
            for t in range(3):
                s = 3 * j + t
                part2[b - 1, (s // 4) % 2, s // 8, s % 4] = res[t]
            return carry

        lax.fori_loop(4 - b, 4, body, 0)

    def extra_core(b, h, cc, lo, hi):
        n = hi - lo
        return remote(
            part2.at[b - 1, cc, h, pl.ds(lo, n)], cbuf2.at[b - 1, h, pl.ds(lo, n)],
            cs2.at[b - 1, h], cr2.at[b - 1, h], at(c_=1 - c),
        )

    def extra_core_send(b):
        for u in extra:
            if u[0] == b:
                pl.when(c != u[2])(extra_core(*u).start)

    def extra_x(b, h, d):
        to = (x + d) % 4
        return remote(
            part2.at[b - 1, c, h, to], xbuf2.at[b - 1, h, d - 1],
            xs2.at[b - 1, h, d - 1], xr2.at[b - 1, h, d - 1], at(x_=to),
        )

    def extra_z(b, h):
        zz = (7 - zl + 4 + 8 * h) % 16
        return remote(
            zsrc2.at[b - 1, h], zbuf2.at[b - 1, zh], zs2.at[b - 1, h], zr2.at[b - 1, zh],
            ((zz % 8) * 4 + y, (zz // 8) * 8 + x * 2 + c),
        )

    def extra_core_reduce(b, h, cc, lo, hi):
        @pl.when(c == cc)
        def _():
            extra_core(b, h, cc, lo, hi).wait_recv()
            for i in range(lo, hi):
                mine = part2[b - 1, cc, h, i].astype(F32) + cbuf2[b - 1, h, i].astype(F32)
                part2[b - 1, cc, h, i] = mine.astype(BF16)
            for d in (2, 1, 3):
                pl.when(within((x + d) % 4, lo, hi))(extra_x(b, h, d).start)

    def extra_x_reduce(b, h, cc, lo, hi):
        @pl.when(jnp.logical_and(c == cc, within(x, lo, hi)))
        def _():
            t = part2[b - 1, cc, h, x].astype(F32)
            for d in (2, 1, 3):
                extra_x(b, h, d).wait_recv()
                t = t + xbuf2[b - 1, h, d - 1].astype(F32)
            zsrc2[b - 1, h] = t.astype(BF16)
            extra_z(b, h).start()

    def extra_sent(b, h, cc, lo, hi):
        pl.when(c != cc)(extra_core(b, h, cc, lo, hi).wait_send)

        @pl.when(c == cc)
        def _():
            for d in (2, 1, 3):
                pl.when(within((x + d) % 4, lo, hi))(extra_x(b, h, d).wait_send)
            pl.when(within(x, lo, hi))(extra_z(b, h).wait_send)

    def extra_step(step):
        @pl.when(edge)
        def _():
            for u in extra:
                step(*u)

    compute(0, 0, 3)
    core_send(0, 0)
    compute(0, 3, 5)
    core_send(0, 1)
    own = poolsrc[0] + pool_get(0) + pool_get(1) + pool_get(2)
    poolsrc[1] = own
    pool_send(poolsrc.at[1], 9, at(c_=1 - c))
    reach_wait(1)
    reach_signal(2)
    compute(1, 0, 3)
    core_send(1, 0)
    core_reduce(0, 0)
    core_reduce(0, 1)
    both = own + pool_get(9)
    poolsrc[5] = both
    for d in range(1, 4):
        pool_send(poolsrc.at[5], 9 + d, at(x_=(x + d) % 4))

    @pl.when(edge)
    def _():
        for b in (3, 2, 1):
            extra_compute(b)
            extra_core_send(b)

    reach_wait(2)
    reach_signal(3)
    core_reduce(1, 0)
    extra_step(extra_core_reduce)
    x_half(0, 0)
    x_half(0, 1)
    halo_wait(0)
    compute(2, 0, 3)
    core_send(2, 0)
    compute(1, 3, 5)
    core_send(1, 1)
    reach_wait(3)
    here = both + pool_get(10) + pool_get(11) + pool_get(12)
    poolsrc[2] = here
    pool_send(poolsrc.at[2], 3, at_z(4))
    pool_send(poolsrc.at[2], 4, at_z(12))
    x_half(1, 0)
    x_reduce(0, 0)
    x_reduce(0, 1)
    core_reduce(2, 0)
    core_reduce(1, 1)
    halo_wait(1)
    compute(3, 0, 3)
    core_send(3, 0)
    compute(2, 3, 5)
    core_send(2, 1)
    x_reduce(1, 0)
    extra_step(extra_x_reduce)
    x_half(2, 0)
    x_half(1, 1)
    core_reduce(3, 0)
    core_reduce(2, 1)
    halo_wait(2)
    compute(3, 3, 5)
    core_send(3, 1)
    three = here + pool_get(3) + pool_get(4)
    pool_send(poolbuf.at[4], 5, at_z(12))
    x_reduce(2, 0)
    x_reduce(1, 1)
    x_half(3, 0)
    x_half(2, 1)
    core_reduce(3, 1)
    four = three + pool_get(5)
    poolsrc[3] = four
    pool_send(poolsrc.at[3], 6, at(zl_=zl + 1 - 2 * (zl % 2)))

    place = zl % 4
    middle = jnp.logical_or(place == 1, place == 2)

    def pool_copy(src, slot_i, dev):
        return remote(poolsrc.at[src], poolbuf.at[slot_i], ps.at[slot_i], pr.at[slot_i], dev)

    inward = pool_copy(6, 7, at(zl_=(zl + jnp.where(place == 1, 1, 7)) % 8))
    outward = pool_copy(4, 8, at(zl_=(zl + jnp.where(place == 1, 7, 1)) % 8))
    x_reduce(3, 0)
    x_half(3, 1)
    x_reduce(2, 1)
    poolsrc[6] = four + pool_get(6)
    pl.when(middle)(inward.start)
    x_reduce(3, 1)

    @pl.when(middle)
    def _():
        inward.wait_recv()
        poolsrc[4] = poolsrc[6] + poolbuf[7]
        outward.start()

    for load in loads[4:]:
        load.wait()

    proj = jnp.zeros((80, 256), F32)
    for b in range(4):
        if b == 3:
            @pl.when(jnp.logical_not(middle))
            def _():
                outward.wait_recv()
                poolsrc[4] = poolbuf[8]

            pre_all = poolsrc[4] * (1.0 / 38400.0)
            pooled = jnp.maximum(gain[4:5] * pre_all + shift[4:5], 0.0).astype(BF16)
            pool_term = jnp.dot(
                jnp.broadcast_to(pooled, (16, 256)), wprojv[pl.ds(1024, 256), :],
                preferred_element_type=F32,
            )[0:1]
        for way in range(2):
            remote(
                zsrc.at[b, 0], zbuf.at[b, way], zs.at[b, 0], zr.at[b, way], at_z(4)
            ).wait_recv()
        acc[b] = zbuf[b, 0].astype(F32) + zbuf[b, 1].astype(F32)
        if b > 0:
            over = jnp.zeros((), jnp.bool_)
            for eb, eh, ec, lo, hi in extra:
                if eb == b:
                    mine = jnp.logical_and(bit == eh, c == ec)
                    over = jnp.logical_or(over, jnp.logical_and(mine, within(x, lo, hi)))

            @pl.when(jnp.logical_and(edge_owner, over))
            def _():
                for half in range(2):
                    remote(
                        zsrc2.at[b - 1, 0], zbuf2.at[b - 1, half],
                        zs2.at[b - 1, 0], zr2.at[b - 1, half], at_z(4),
                    ).wait_recv()
                acc[b] += zbuf2[b - 1, 0].astype(F32) + zbuf2[b - 1, 1].astype(F32)

        act = jnp.maximum(acc[b] * gain[b : b + 1] + shift[b : b + 1], 0.0).astype(BF16)
        proj = proj + jnp.dot(act, wprojv[pl.ds(b * 256, 256), :], preferred_element_type=F32)
    head = jnp.maximum(gain[5:6] * (proj + pool_term) + shift[5:6], 0.0)
    head = jnp.concatenate([head, jnp.zeros((48, 256), F32)], axis=0)
    stage[...] = jnp.transpose(head).astype(BF16).reshape(16, 16, 128)

    def out_copy(d):
        return remote(stage.at[d], obuf.at[slot], os.at[d], orr.at[slot], (zl_dst * 4 + y_dst, d))

    def out_send(i, carry):
        @pl.when(has_col)
        def _():
            out_copy((ch + i) % 16).start()

        return carry

    lax.fori_loop(0, 16, out_send, 0)
    for copy in ycopies + list(psends.values()):
        copy.wait_send()
    for d in range(3):
        for side in range(2):
            pl.when(halo_out[side])(halo_copy(d, side).wait_send)

    @pl.when(middle)
    def _():
        inward.wait_send()
        outward.wait_send()

    @pl.when(edge)
    def _():
        for u in extra:
            extra_sent(*u)

    for u in core_copies:
        for copy in [core_copies[u], z_copies[u]] + x_copies[u]:
            copy.wait_send()

    def out_recv(i, carry):
        remote(stage.at[0], obuf.at[i], os.at[0], orr.at[i], east).wait_recv()
        return carry

    lax.fori_loop(0, 15, out_recv, 0)
    out[...] = obuf[:, :, 0:80]

    def out_sent(d, carry):
        @pl.when(has_col)
        def _():
            out_copy(d).wait_send()

        return carry

    lax.fori_loop(0, 16, out_sent, 0)


def local(features, pointwise_weight, w_atrous, w_pool, w_proj, norm_gain, norm_shift):
    feat = jnp.transpose(features, (1, 0, 2))
    vmem = pl.BlockSpec(memory_space=pltpu.VMEM)
    hbm = pl.BlockSpec(memory_space=pl.ANY)
    dma = pltpu.SemaphoreType.DMA
    out = pl.pallas_call(
        head_kernel,
        out_shape=pltpu.VMEM((15, 16, 80), BF16),
        in_specs=[hbm] * 7,
        out_specs=vmem,
        scratch_shapes=[
            pltpu.VMEM((15, 80, 128), BF16),
            pltpu.VMEM((11, 3, 80 + 2 * PAD, 128), BF16),
            pltpu.VMEM((4, 2, 2, 4, 80, 256), BF16),
            pltpu.VMEM((4, 2, 4, 80, 256), BF16),
            pltpu.VMEM((4, 2, 3, 80, 256), BF16),
            pltpu.VMEM((4, 2, 80, 256), BF16),
            pltpu.VMEM((4, 2, 80, 256), BF16),
            pltpu.VMEM((16, 16, 128), BF16),
            pltpu.VMEM((15, 16, 128), BF16),
            pltpu.VMEM((128, 256), BF16),
            pltpu.VMEM((3, 9, 128, 256), BF16),
            pltpu.VMEM((1280, 256), BF16),
            pltpu.VMEM((128, 256), BF16),
            pltpu.VMEM((6, 256), F32),
            pltpu.VMEM((6, 256), F32),
            pltpu.VMEM((7, 1, 256), F32),
            pltpu.VMEM((13, 1, 256), F32),
            pltpu.VMEM((3, 2, 2, 4, 80, 256), BF16),
            pltpu.VMEM((3, 2, 4, 80, 256), BF16),
            pltpu.VMEM((3, 2, 3, 80, 256), BF16),
            pltpu.VMEM((3, 2, 80, 256), BF16),
            pltpu.VMEM((3, 2, 80, 256), BF16),
            pltpu.VMEM((4, 80, 256), F32),
            pltpu.VMEM((4, 2, 80, 256), F32),
            dma((7,)),
            dma((3,)), dma((3,)),
            dma((6,)), dma((6,)),
            dma((4, 2)), dma((4, 2)),
            dma((4, 2, 3)), dma((4, 2, 3)),
            dma((4, 2)), dma((4, 2)),
            dma((16,)), dma((15,)),
            dma((13,)), dma((13,)),
            dma((3, 2)), dma((3, 2)),
            dma((3, 2, 3)), dma((3, 2, 3)),
            dma((3, 2)), dma((3, 2)),
            pltpu.SemaphoreType.REGULAR((4,)),
        ],
        compiler_params=pltpu.CompilerParams(collective_id=0, has_side_effects=True),
        name="aspp_head",
    )(
        feat, pointwise_weight, w_atrous.reshape(3, 9, 128, 256), w_pool, w_proj,
        norm_gain, norm_shift,
    )
    return jnp.transpose(out, (2, 0, 1))


def solution(mesh):
    return jax.shard_map(
        local,
        mesh=mesh,
        in_specs=(
            P(None, "lon", "ch"),
            P("ch", None),
            P(None, None, None, "ch", None),
            P("ch", None),
            P(),
            P(),
            P(),
        ),
        out_specs=P(None, "lon", "ch"),
        check_vma=False,
    )
```

```python
import jax
import jax.numpy as jnp
from jax import lax
from jax.experimental import pallas as pl
from jax.experimental.pallas import tpu as pltpu
from jax.sharding import PartitionSpec as P

MESH_ID = pl.DeviceIdType.MESH
F32 = jnp.float32
BF16 = jnp.bfloat16

PAD = 48


def head_kernel(
    feat, pw, wa, wpool_h, wproj, gain_h, shift_h, out,
    xin, xb, part, cbuf, xbuf, zsrc, zbuf, stage, obuf,
    pwv, wav, wprojv, wpool, gain, shift, poolsrc, poolbuf,
    part2, cbuf2, xbuf2, zsrc2, zbuf2, acc, xacc,
    ld_sem, ys, yr, hs, hr, cs, cr, xs, xr, zs, zr, os, orr, ps, pr,
    cs2, cr2, xs2, xr2, zs2, zr2, reach,
):
    lon = lax.axis_index("lon")
    ch = lax.axis_index("ch")
    zl, y = lon // 4, lon % 4
    zh, x, c = ch // 8, (ch // 2) % 4, ch % 2
    z = zh * 8 + zl

    def at(zl_=None, y_=None, x_=None, c_=None):
        zz = zl if zl_ is None else zl_
        yy = y if y_ is None else y_
        xx = x if x_ is None else x_
        cc = c if c_ is None else c_
        return (zz * 4 + yy, zh * 8 + xx * 2 + cc)

    def at_z(dz):
        zz = (z + dz) % 16
        return ((zz % 8) * 4 + y, (zz // 8) * 8 + x * 2 + c)

    def block_of(j, level):
        q = (j + 1) % 5
        return jnp.where(level == 0, 4 - q, q)

    bit = ((z + 12) % 16) // 8
    zl_dst = (zl + 4) % 8
    k = bit * 8 + c * 4 + x
    kj, kt = k // 3, k % 3
    kq = block_of(kj, zl_dst)
    kg = 4 * kq + y
    y_dst = kg // 5
    slot = (kg % 5) * 3 + kt
    has_col = k < 15

    barrier = pltpu.get_barrier_semaphore()

    def hello(dev):
        pl.semaphore_signal(barrier, inc=1, device_id=dev, device_id_type=MESH_ID)

    east, west = at(zl_=(zl + 1) % 8), at(zl_=(zl + 7) % 8)
    edge = jnp.logical_or(zl == 0, zl == 7)
    edge_owner = jnp.logical_or(zl == 3, zl == 4)

    hello(at_z(1))
    hello(at_z(15))
    for d in range(1, 4):
        hello(at(y_=(y + d) % 4))
        hello(at(x_=(x + d) % 4))
    hello(at(c_=1 - c))

    loads = [
        pltpu.make_async_copy(src, dst, ld_sem.at[i])
        for i, (src, dst) in enumerate((
            (feat, xin), (wpool_h, wpool), (pw, pwv), (wa, wav),
            (wproj, wprojv), (gain_h, gain), (shift_h, shift),
        ))
    ]
    for load in loads:
        load.start()

    pl.semaphore_wait(barrier, 9)

    def remote(src, dst, ssem, rsem, dev):
        return pltpu.make_async_remote_copy(
            src_ref=src, dst_ref=dst, send_sem=ssem, recv_sem=rsem,
            device_id=dev, device_id_type=MESH_ID,
        )

    def reach_signal(r):
        for dz in (1, 15):
            pl.semaphore_signal(
                reach.at[r], inc=1, device_id=at_z(dz), device_id_type=MESH_ID
            )

    def reach_wait(r):
        pl.semaphore_wait(reach.at[r], 2)

    rows = pl.ds(PAD, 80)
    ycopies = []
    for g in range(1, 4):
        q = (5 * y + g) // 4
        copy = remote(
            feat.at[pl.ds(3 * g, 3)], xb.at[q + 3, :, rows, :],
            ys.at[g - 1], yr.at[g - 1], at(y_=(y + g) % 4),
        )
        copy.start()
        ycopies.append(copy)
    psends = {}

    def pool_send(src, slot_i, dev):
        psends[slot_i] = remote(src, poolbuf.at[slot_i], ps.at[slot_i], pr.at[slot_i], dev)
        psends[slot_i].start()

    def pool_get(slot_i):
        psends[slot_i].wait_recv()
        return poolbuf[slot_i]

    loads[0].wait()
    xb[y + 3, :, rows, :] = xin[0:3]
    xb[y + 4, :, rows, :] = xin[12:15]
    reach_signal(0)

    def halo_copy(d, side):
        q = (4 - d) if side == 0 else d
        q_to = q - 5 if side == 0 else q + 5
        return remote(
            xb.at[q + 3, :, rows, :], xb.at[q_to + 3, :, rows, :],
            hs.at[2 * d + side], hr.at[2 * d + side], east if side == 0 else west,
        )

    halo_out = (zl < 7, zl > 0)
    halo_in = (zl > 0, zl < 7)
    for d, sides in ((0, (0,)), (0, (1,)), (1, (0,)), (1, (1,)), (2, (0, 1))):
        q = (4 - d) if sides[0] == 0 else d
        g = (4 * q + y) % 5

        @pl.when(jnp.logical_and(g > 0, g < 4))
        def _():
            gi = jnp.clip(g - 1, 0, 2)
            remote(
                xin.at[pl.ds(0, 3)], xb.at[q + 3, :, rows, :], ys.at[gi], yr.at[gi], east
            ).wait_recv()

        for side in sides:
            pl.when(halo_out[side])(halo_copy(d, side).start)

    reach_wait(0)
    reach_signal(1)
    zrow = jnp.zeros((3, PAD, 128), BF16)

    def clear(i, carry):
        xb[i, :, pl.ds(0, PAD), :] = zrow
        xb[i, :, pl.ds(PAD + 80, PAD), :] = zrow
        return carry

    lax.fori_loop(0, 11, clear, 0)
    for b in range(4):
        part[b, 1, 1, 3] = jnp.zeros((80, 256), BF16)

    blank = jnp.zeros((3, 80, 128), BF16)

    @pl.when(edge)
    def _():
        for d in range(3):
            xb[jnp.where(zl == 0, d, 8 + d), :, pl.ds(PAD, 80), :] = blank

    loads[1].wait()

    def add_col(i, tot):
        return tot + jnp.sum(xin[i].astype(F32).reshape(10, 8, 128), axis=0)

    sums = lax.fori_loop(0, 15, add_col, jnp.zeros((8, 128), F32))
    colsum = jnp.sum(sums, axis=0, keepdims=True)
    pre = jnp.dot(
        jnp.broadcast_to(colsum, (8, 128)), wpool[...].astype(F32),
        precision=lax.Precision.HIGHEST, preferred_element_type=F32,
    )[0:1]
    poolsrc[0] = pre

    for d in range(1, 4):
        pool_send(poolsrc.at[0], d - 1, at(y_=(y + d) % 4))

    def halo_wait(d):
        for side in range(2):
            pl.when(halo_in[side])(halo_copy(d, side).wait_recv)

    loads[2].wait()
    loads[3].wait()

    def compute(b, lo, hi):
        def body(j, carry):
            q = block_of(j, zl)
            if b == 0:
                lhs = xb[q + 3, :, rows, :].reshape(240, 128)
                res = jnp.dot(lhs, pwv[...], preferred_element_type=F32)
            else:
                taps = []
                for ro in (-1, 0, 1):
                    for co in (-1, 0, 1):
                        taps.append(
                            xb[q + 3 + co * b, :, pl.ds(PAD + ro * b * 12, 80), :].reshape(240, 128)
                        )
                res = jnp.dot(
                    jnp.concatenate(taps, axis=1), wav[b - 1].reshape(1152, 256),
                    preferred_element_type=F32,
                )
            res = res.astype(BF16).reshape(3, 80, 256)
            for t in range(3):
                s = 3 * j + t
                part[b, (s // 4) % 2, s // 8, s % 4] = res[t]
            return carry

        lax.fori_loop(lo, hi, body, 0)

    core_copies, x_copies, z_copies = {}, {}, {}

    def core_send(b, h):
        copy = remote(
            part.at[b, 1 - c, h], cbuf.at[b, h], cs.at[b, h], cr.at[b, h], at(c_=1 - c)
        )
        copy.start()
        core_copies[b, h] = copy

    def core_reduce(b, h):
        core_copies[b, h].wait_recv()

        def body(i, carry):
            mine = part[b, c, h, i].astype(F32) + cbuf[b, h, i].astype(F32)
            part[b, c, h, i] = mine.astype(BF16)
            return carry

        lax.fori_loop(0, 4, body, 0)
        first = flip if h == 0 else 3 - x
        x_copies[b, h] = []
        for i, col in enumerate((first, (x + 2) % 4)):
            copy = remote(
                part.at[b, c, h, col], xbuf.at[b, h, i], xs.at[b, h, i], xr.at[b, h, i],
                at(x_=first),
            )
            copy.start()
            x_copies[b, h].append(copy)

    flip = x + 1 - 2 * (x % 2)

    def x_half(b, h):
        second = 3 - x if h == 0 else flip
        for copy in x_copies[b, h]:
            copy.wait_recv()
        give = part[b, c, h, second].astype(F32) + xbuf[b, h, 1].astype(F32)
        part[b, c, h, second] = give.astype(BF16)
        copy = remote(
            part.at[b, c, h, second], xbuf.at[b, h, 2], xs.at[b, h, 2], xr.at[b, h, 2],
            at(x_=second),
        )
        copy.start()
        x_copies[b, h].append(copy)
        xacc[b, h] = part[b, c, h, x].astype(F32) + xbuf[b, h, 0].astype(F32)

    def x_reduce(b, h):
        x_copies[b, h][2].wait_recv()
        zsrc[b, h] = (xacc[b, h] + xbuf[b, h, 2].astype(F32)).astype(BF16)
        up = (zh == h).astype(jnp.int32)
        z_copies[b, h] = remote(
            zsrc.at[b, h], zbuf.at[b, 1 - up], zs.at[b, h], zr.at[b, 1 - up], at_z(12 - 8 * up)
        )
        z_copies[b, h].start()

    extra = (
        (3, 0, 0, 3, 4), (3, 0, 1, 0, 4), (3, 1, 0, 0, 4),
        (2, 0, 1, 2, 4), (2, 1, 0, 0, 4), (1, 1, 0, 1, 4),
    )

    def within(to, lo, hi):
        return jnp.logical_and(to >= lo, to < hi)

    def extra_compute(b):
        col = jnp.where(zl == 7, 0, 2)
        kernel = jnp.concatenate([wav[b - 1, r * 3 + col] for r in range(3)], axis=0)

        def body(j, carry):
            q = jnp.where(zl == 7, 8 - j - b, j + b - 4)
            lhs = jnp.concatenate(
                [
                    xb[q + 3, :, pl.ds(PAD + ro * b * 12, 80), :].reshape(240, 128)
                    for ro in (-1, 0, 1)
                ],
                axis=1,
            )
            res = jnp.dot(lhs, kernel, preferred_element_type=F32)
            res = res.astype(BF16).reshape(3, 80, 256)
            for t in range(3):
                s = 3 * j + t
                part2[b - 1, (s // 4) % 2, s // 8, s % 4] = res[t]
            return carry

        lax.fori_loop(4 - b, 4, body, 0)

    def extra_core(b, h, cc, lo, hi):
        n = hi - lo
        return remote(
            part2.at[b - 1, cc, h, pl.ds(lo, n)], cbuf2.at[b - 1, h, pl.ds(lo, n)],
            cs2.at[b - 1, h], cr2.at[b - 1, h], at(c_=1 - c),
        )

    def extra_core_send(b):
        for u in extra:
            if u[0] == b:
                pl.when(c != u[2])(extra_core(*u).start)

    def extra_x(b, h, d):
        to = (x + d) % 4
        return remote(
            part2.at[b - 1, c, h, to], xbuf2.at[b - 1, h, d - 1],
            xs2.at[b - 1, h, d - 1], xr2.at[b - 1, h, d - 1], at(x_=to),
        )

    def extra_z(b, h):
        zz = (7 - zl + 4 + 8 * h) % 16
        return remote(
            zsrc2.at[b - 1, h], zbuf2.at[b - 1, zh], zs2.at[b - 1, h], zr2.at[b - 1, zh],
            ((zz % 8) * 4 + y, (zz // 8) * 8 + x * 2 + c),
        )

    def extra_core_reduce(b, h, cc, lo, hi):
        @pl.when(c == cc)
        def _():
            extra_core(b, h, cc, lo, hi).wait_recv()
            for i in range(lo, hi):
                mine = part2[b - 1, cc, h, i].astype(F32) + cbuf2[b - 1, h, i].astype(F32)
                part2[b - 1, cc, h, i] = mine.astype(BF16)
            for d in (2, 1, 3):
                pl.when(within((x + d) % 4, lo, hi))(extra_x(b, h, d).start)

    def extra_x_reduce(b, h, cc, lo, hi):
        @pl.when(jnp.logical_and(c == cc, within(x, lo, hi)))
        def _():
            t = part2[b - 1, cc, h, x].astype(F32)
            for d in (2, 1, 3):
                extra_x(b, h, d).wait_recv()
                t = t + xbuf2[b - 1, h, d - 1].astype(F32)
            zsrc2[b - 1, h] = t.astype(BF16)
            extra_z(b, h).start()

    def extra_sent(b, h, cc, lo, hi):
        pl.when(c != cc)(extra_core(b, h, cc, lo, hi).wait_send)

        @pl.when(c == cc)
        def _():
            for d in (2, 1, 3):
                pl.when(within((x + d) % 4, lo, hi))(extra_x(b, h, d).wait_send)
            pl.when(within(x, lo, hi))(extra_z(b, h).wait_send)

    def extra_step(step):
        @pl.when(edge)
        def _():
            for u in extra:
                step(*u)

    compute(0, 0, 3)
    core_send(0, 0)
    compute(0, 3, 5)
    core_send(0, 1)
    own = poolsrc[0] + pool_get(0) + pool_get(1) + pool_get(2)
    poolsrc[1] = own
    pool_send(poolsrc.at[1], 9, at(c_=1 - c))
    reach_wait(1)
    reach_signal(2)
    compute(1, 0, 3)
    core_send(1, 0)
    both = own + pool_get(9)
    poolsrc[5] = both
    for d in range(1, 4):
        pool_send(poolsrc.at[5], 9 + d, at(x_=(x + d) % 4))
    core_reduce(0, 0)
    core_reduce(0, 1)

    @pl.when(edge)
    def _():
        for b in (3, 2, 1):
            extra_compute(b)
            extra_core_send(b)

    core_reduce(1, 0)
    reach_wait(2)
    reach_signal(3)
    extra_step(extra_core_reduce)
    halo_wait(0)
    compute(2, 0, 3)
    core_send(2, 0)
    compute(1, 3, 5)
    core_send(1, 1)
    reach_wait(3)
    here = both + pool_get(10) + pool_get(11) + pool_get(12)
    poolsrc[2] = here
    pool_send(poolsrc.at[2], 3, at_z(4))
    pool_send(poolsrc.at[2], 4, at_z(12))
    x_half(0, 0)
    x_half(0, 1)
    core_reduce(2, 0)
    core_reduce(1, 1)
    halo_wait(1)
    compute(3, 0, 3)
    core_send(3, 0)
    compute(2, 3, 5)
    core_send(2, 1)
    x_reduce(0, 0)
    x_reduce(0, 1)
    x_half(1, 0)
    core_reduce(3, 0)
    core_reduce(2, 1)
    three = here + pool_get(3) + pool_get(4)
    pool_send(poolbuf.at[4], 5, at_z(12))
    halo_wait(2)
    compute(3, 3, 5)
    core_send(3, 1)
    extra_step(extra_x_reduce)
    x_half(2, 0)
    x_half(1, 1)
    x_reduce(1, 0)
    core_reduce(3, 1)
    x_half(3, 0)
    x_half(2, 1)
    four = three + pool_get(5)
    poolsrc[3] = four
    pool_send(poolsrc.at[3], 6, at(zl_=zl + 1 - 2 * (zl % 2)))
    x_reduce(2, 0)
    x_reduce(1, 1)

    place = zl % 4
    middle = jnp.logical_or(place == 1, place == 2)

    def pool_copy(src, slot_i, dev):
        return remote(poolsrc.at[src], poolbuf.at[slot_i], ps.at[slot_i], pr.at[slot_i], dev)

    inward = pool_copy(6, 7, at(zl_=(zl + jnp.where(place == 1, 1, 7)) % 8))
    outward = pool_copy(4, 8, at(zl_=(zl + jnp.where(place == 1, 7, 1)) % 8))
    x_half(3, 1)
    x_reduce(3, 0)
    poolsrc[6] = four + pool_get(6)
    pl.when(middle)(inward.start)
    x_reduce(2, 1)
    x_reduce(3, 1)

    @pl.when(middle)
    def _():
        inward.wait_recv()
        poolsrc[4] = poolsrc[6] + poolbuf[7]
        outward.start()

    for load in loads[4:]:
        load.wait()

    proj = jnp.zeros((80, 256), F32)
    for b in range(4):
        if b == 3:
            @pl.when(jnp.logical_not(middle))
            def _():
                outward.wait_recv()
                poolsrc[4] = poolbuf[8]

            pre_all = poolsrc[4] * (1.0 / 38400.0)
            pooled = jnp.maximum(gain[4:5] * pre_all + shift[4:5], 0.0).astype(BF16)
            pool_term = jnp.dot(
                jnp.broadcast_to(pooled, (16, 256)), wprojv[pl.ds(1024, 256), :],
                preferred_element_type=F32,
            )[0:1]
        for way in range(2):
            remote(
                zsrc.at[b, 0], zbuf.at[b, way], zs.at[b, 0], zr.at[b, way], at_z(4)
            ).wait_recv()
        acc[b] = zbuf[b, 0].astype(F32) + zbuf[b, 1].astype(F32)
        if b > 0:
            over = jnp.zeros((), jnp.bool_)
            for eb, eh, ec, lo, hi in extra:
                if eb == b:
                    mine = jnp.logical_and(bit == eh, c == ec)
                    over = jnp.logical_or(over, jnp.logical_and(mine, within(x, lo, hi)))

            @pl.when(jnp.logical_and(edge_owner, over))
            def _():
                for half in range(2):
                    remote(
                        zsrc2.at[b - 1, 0], zbuf2.at[b - 1, half],
                        zs2.at[b - 1, 0], zr2.at[b - 1, half], at_z(4),
                    ).wait_recv()
                acc[b] += zbuf2[b - 1, 0].astype(F32) + zbuf2[b - 1, 1].astype(F32)

        act = jnp.maximum(acc[b] * gain[b : b + 1] + shift[b : b + 1], 0.0).astype(BF16)
        proj = proj + jnp.dot(act, wprojv[pl.ds(b * 256, 256), :], preferred_element_type=F32)
    head = jnp.maximum(gain[5:6] * (proj + pool_term) + shift[5:6], 0.0)
    head = jnp.concatenate([head, jnp.zeros((48, 256), F32)], axis=0)
    stage[...] = jnp.transpose(head).astype(BF16).reshape(16, 16, 128)

    def out_copy(d):
        return remote(stage.at[d], obuf.at[slot], os.at[d], orr.at[slot], (zl_dst * 4 + y_dst, d))

    def out_send(i, carry):
        @pl.when(has_col)
        def _():
            out_copy((ch + i) % 16).start()

        return carry

    lax.fori_loop(0, 16, out_send, 0)
    for copy in ycopies + list(psends.values()):
        copy.wait_send()
    for d in range(3):
        for side in range(2):
            pl.when(halo_out[side])(halo_copy(d, side).wait_send)

    @pl.when(middle)
    def _():
        inward.wait_send()
        outward.wait_send()

    @pl.when(edge)
    def _():
        for u in extra:
            extra_sent(*u)

    for u in core_copies:
        for copy in [core_copies[u], z_copies[u]] + x_copies[u]:
            copy.wait_send()

    def out_recv(i, carry):
        remote(stage.at[0], obuf.at[i], os.at[0], orr.at[i], east).wait_recv()
        return carry

    lax.fori_loop(0, 15, out_recv, 0)
    out[...] = obuf[:, :, 0:80]

    def out_sent(d, carry):
        @pl.when(has_col)
        def _():
            out_copy(d).wait_send()

        return carry

    lax.fori_loop(0, 16, out_sent, 0)


def local(features, pointwise_weight, w_atrous, w_pool, w_proj, norm_gain, norm_shift):
    feat = jnp.transpose(features, (1, 0, 2))
    vmem = pl.BlockSpec(memory_space=pltpu.VMEM)
    hbm = pl.BlockSpec(memory_space=pl.ANY)
    dma = pltpu.SemaphoreType.DMA
    out = pl.pallas_call(
        head_kernel,
        out_shape=pltpu.VMEM((15, 16, 80), BF16),
        in_specs=[hbm] * 7,
        out_specs=vmem,
        scratch_shapes=[
            pltpu.VMEM((15, 80, 128), BF16),
            pltpu.VMEM((11, 3, 80 + 2 * PAD, 128), BF16),
            pltpu.VMEM((4, 2, 2, 4, 80, 256), BF16),
            pltpu.VMEM((4, 2, 4, 80, 256), BF16),
            pltpu.VMEM((4, 2, 3, 80, 256), BF16),
            pltpu.VMEM((4, 2, 80, 256), BF16),
            pltpu.VMEM((4, 2, 80, 256), BF16),
            pltpu.VMEM((16, 16, 128), BF16),
            pltpu.VMEM((15, 16, 128), BF16),
            pltpu.VMEM((128, 256), BF16),
            pltpu.VMEM((3, 9, 128, 256), BF16),
            pltpu.VMEM((1280, 256), BF16),
            pltpu.VMEM((128, 256), BF16),
            pltpu.VMEM((6, 256), F32),
            pltpu.VMEM((6, 256), F32),
            pltpu.VMEM((7, 1, 256), F32),
            pltpu.VMEM((13, 1, 256), F32),
            pltpu.VMEM((3, 2, 2, 4, 80, 256), BF16),
            pltpu.VMEM((3, 2, 4, 80, 256), BF16),
            pltpu.VMEM((3, 2, 3, 80, 256), BF16),
            pltpu.VMEM((3, 2, 80, 256), BF16),
            pltpu.VMEM((3, 2, 80, 256), BF16),
            pltpu.VMEM((4, 80, 256), F32),
            pltpu.VMEM((4, 2, 80, 256), F32),
            dma((7,)),
            dma((3,)), dma((3,)),
            dma((6,)), dma((6,)),
            dma((4, 2)), dma((4, 2)),
            dma((4, 2, 3)), dma((4, 2, 3)),
            dma((4, 2)), dma((4, 2)),
            dma((16,)), dma((15,)),
            dma((13,)), dma((13,)),
            dma((3, 2)), dma((3, 2)),
            dma((3, 2, 3)), dma((3, 2, 3)),
            dma((3, 2)), dma((3, 2)),
            pltpu.SemaphoreType.REGULAR((4,)),
        ],
        compiler_params=pltpu.CompilerParams(collective_id=0, has_side_effects=True),
        name="aspp_head",
    )(
        feat, pointwise_weight, w_atrous.reshape(3, 9, 128, 256), w_pool, w_proj,
        norm_gain, norm_shift,
    )
    return jnp.transpose(out, (2, 0, 1))


def solution(mesh):
    return jax.shard_map(
        local,
        mesh=mesh,
        in_specs=(
            P(None, "lon", "ch"),
            P("ch", None),
            P(None, None, None, "ch", None),
            P("ch", None),
            P(),
            P(),
            P(),
        ),
        out_specs=P(None, "lon", "ch"),
        check_vma=False,
    )
```

```python
import jax
import jax.numpy as jnp
from jax import lax
from jax.experimental import pallas as pl
from jax.experimental.pallas import tpu as pltpu
from jax.sharding import PartitionSpec as P

MESH_ID = pl.DeviceIdType.MESH
F32 = jnp.float32
BF16 = jnp.bfloat16

PAD = 48


def head_kernel(
    feat, pw, wa, wpool_h, wproj, gain_h, shift_h, out,
    xin, xb, part, cbuf, xbuf, zsrc, zbuf, stage, obuf,
    pwv, wav, wprojv, wpool, gain, shift, poolsrc, poolbuf,
    part2, cbuf2, xbuf2, zsrc2, zbuf2, acc, xacc,
    ld_sem, ys, yr, hs, hr, cs, cr, xs, xr, zs, zr, os, orr, ps, pr,
    cs2, cr2, xs2, xr2, zs2, zr2,
):
    lon = lax.axis_index("lon")
    ch = lax.axis_index("ch")
    zl, y = lon // 4, lon % 4
    zh, x, c = ch // 8, (ch // 2) % 4, ch % 2
    z = zh * 8 + zl

    def at(zl_=None, y_=None, x_=None, c_=None):
        zz = zl if zl_ is None else zl_
        yy = y if y_ is None else y_
        xx = x if x_ is None else x_
        cc = c if c_ is None else c_
        return (zz * 4 + yy, zh * 8 + xx * 2 + cc)

    def at_z(dz):
        zz = (z + dz) % 16
        return ((zz % 8) * 4 + y, (zz // 8) * 8 + x * 2 + c)

    def block_of(j, level):
        q = (j + 1) % 5
        return jnp.where(level == 0, 4 - q, q)

    bit = ((z + 12) % 16) // 8
    zl_dst = (zl + 4) % 8
    k = bit * 8 + c * 4 + x
    kj, kt = k // 3, k % 3
    kq = block_of(kj, zl_dst)
    kg = 4 * kq + y
    y_dst = kg // 5
    slot = (kg % 5) * 3 + kt
    has_col = k < 15

    barrier = pltpu.get_barrier_semaphore()

    def hello(dev):
        pl.semaphore_signal(barrier, inc=1, device_id=dev, device_id_type=MESH_ID)

    east, west = at(zl_=(zl + 1) % 8), at(zl_=(zl + 7) % 8)
    edge = jnp.logical_or(zl == 0, zl == 7)
    edge_owner = jnp.logical_or(zl == 3, zl == 4)

    @pl.when(edge_owner)
    def _():
        far = jnp.where(zl == 4, 7, 0) * 4 + y
        hello((far, x * 2 + c))
        hello((far, 8 + x * 2 + c))

    @pl.when(zl < 7)
    def _():
        hello(east)

    @pl.when(zl > 0)
    def _():
        hello(west)

    hello(at_z(4))
    hello(at_z(12))

    for d in range(1, 4):
        hello(at(y_=(y + d) % 4))
        hello(at(x_=(x + d) % 4))
    hello(at(c_=1 - c))

    loads = [
        pltpu.make_async_copy(src, dst, ld_sem.at[i])
        for i, (src, dst) in enumerate((
            (feat, xin), (wpool_h, wpool), (pw, pwv), (wa, wav),
            (wproj, wprojv), (gain_h, gain), (shift_h, shift),
        ))
    ]
    for load in loads:
        load.start()

    pl.semaphore_wait(barrier, 11 + edge.astype(jnp.int32))

    def remote(src, dst, ssem, rsem, dev):
        return pltpu.make_async_remote_copy(
            src_ref=src, dst_ref=dst, send_sem=ssem, recv_sem=rsem,
            device_id=dev, device_id_type=MESH_ID,
        )

    rows = pl.ds(PAD, 80)
    ycopies = []
    for g in range(1, 4):
        q = (5 * y + g) // 4
        copy = remote(
            feat.at[pl.ds(3 * g, 3)], xb.at[q + 3, :, rows, :],
            ys.at[g - 1], yr.at[g - 1], at(y_=(y + g) % 4),
        )
        copy.start()
        ycopies.append(copy)
    psends = {}

    def pool_send(src, slot_i, dev):
        psends[slot_i] = remote(src, poolbuf.at[slot_i], ps.at[slot_i], pr.at[slot_i], dev)
        psends[slot_i].start()

    def pool_get(slot_i):
        psends[slot_i].wait_recv()
        return poolbuf[slot_i]

    loads[0].wait()
    xb[y + 3, :, rows, :] = xin[0:3]
    xb[y + 4, :, rows, :] = xin[12:15]
    zrow = jnp.zeros((3, PAD, 128), BF16)

    def clear(i, carry):
        xb[i, :, pl.ds(0, PAD), :] = zrow
        xb[i, :, pl.ds(PAD + 80, PAD), :] = zrow
        return carry

    lax.fori_loop(0, 11, clear, 0)
    for b in range(4):
        part[b, 1, 1, 3] = jnp.zeros((80, 256), BF16)

    blank = jnp.zeros((3, 80, 128), BF16)

    @pl.when(edge)
    def _():
        for d in range(3):
            xb[jnp.where(zl == 0, d, 8 + d), :, pl.ds(PAD, 80), :] = blank

    loads[1].wait()

    def add_col(i, tot):
        return tot + jnp.sum(xin[i].astype(F32).reshape(10, 8, 128), axis=0)

    sums = lax.fori_loop(0, 15, add_col, jnp.zeros((8, 128), F32))
    colsum = jnp.sum(sums, axis=0, keepdims=True)
    pre = jnp.dot(
        jnp.broadcast_to(colsum, (8, 128)), wpool[...].astype(F32),
        precision=lax.Precision.HIGHEST, preferred_element_type=F32,
    )[0:1]
    poolsrc[0] = pre

    for d in range(1, 4):
        pool_send(poolsrc.at[0], d - 1, at(y_=(y + d) % 4))

    def halo_copy(d, side):
        q = (4 - d) if side == 0 else d
        q_to = q - 5 if side == 0 else q + 5
        return remote(
            xb.at[q + 3, :, rows, :], xb.at[q_to + 3, :, rows, :],
            hs.at[2 * d + side], hr.at[2 * d + side], east if side == 0 else west,
        )

    halo_out = (zl < 7, zl > 0)
    halo_in = (zl > 0, zl < 7)
    for d, sides in ((0, (0,)), (0, (1,)), (1, (0,)), (1, (1,)), (2, (0, 1))):
        q = (4 - d) if sides[0] == 0 else d
        g = (4 * q + y) % 5

        @pl.when(jnp.logical_and(g > 0, g < 4))
        def _():
            gi = jnp.clip(g - 1, 0, 2)
            remote(
                xin.at[pl.ds(0, 3)], xb.at[q + 3, :, rows, :], ys.at[gi], yr.at[gi], east
            ).wait_recv()

        for side in sides:
            pl.when(halo_out[side])(halo_copy(d, side).start)

    def halo_wait(d):
        for side in range(2):
            pl.when(halo_in[side])(halo_copy(d, side).wait_recv)

    loads[2].wait()
    loads[3].wait()

    def compute(b, lo, hi):
        def body(j, carry):
            q = block_of(j, zl)
            if b == 0:
                lhs = xb[q + 3, :, rows, :].reshape(240, 128)
                res = jnp.dot(lhs, pwv[...], preferred_element_type=F32)
            else:
                taps = []
                for ro in (-1, 0, 1):
                    for co in (-1, 0, 1):
                        taps.append(
                            xb[q + 3 + co * b, :, pl.ds(PAD + ro * b * 12, 80), :].reshape(240, 128)
                        )
                res = jnp.dot(
                    jnp.concatenate(taps, axis=1), wav[b - 1].reshape(1152, 256),
                    preferred_element_type=F32,
                )
            res = res.astype(BF16).reshape(3, 80, 256)
            for t in range(3):
                s = 3 * j + t
                part[b, (s // 4) % 2, s // 8, s % 4] = res[t]
            return carry

        lax.fori_loop(lo, hi, body, 0)

    core_copies, x_copies, z_copies = {}, {}, {}

    def core_send(b, h):
        copy = remote(
            part.at[b, 1 - c, h], cbuf.at[b, h], cs.at[b, h], cr.at[b, h], at(c_=1 - c)
        )
        copy.start()
        core_copies[b, h] = copy

    def core_reduce(b, h):
        core_copies[b, h].wait_recv()

        def body(i, carry):
            mine = part[b, c, h, i].astype(F32) + cbuf[b, h, i].astype(F32)
            part[b, c, h, i] = mine.astype(BF16)
            return carry

        lax.fori_loop(0, 4, body, 0)
        first = flip if h == 0 else 3 - x
        x_copies[b, h] = []
        for i, col in enumerate((first, (x + 2) % 4)):
            copy = remote(
                part.at[b, c, h, col], xbuf.at[b, h, i], xs.at[b, h, i], xr.at[b, h, i],
                at(x_=first),
            )
            copy.start()
            x_copies[b, h].append(copy)

    flip = x + 1 - 2 * (x % 2)

    def x_half(b, h):
        second = 3 - x if h == 0 else flip
        for copy in x_copies[b, h]:
            copy.wait_recv()
        give = part[b, c, h, second].astype(F32) + xbuf[b, h, 1].astype(F32)
        part[b, c, h, second] = give.astype(BF16)
        copy = remote(
            part.at[b, c, h, second], xbuf.at[b, h, 2], xs.at[b, h, 2], xr.at[b, h, 2],
            at(x_=second),
        )
        copy.start()
        x_copies[b, h].append(copy)
        xacc[b, h] = part[b, c, h, x].astype(F32) + xbuf[b, h, 0].astype(F32)

    def x_reduce(b, h):
        x_copies[b, h][2].wait_recv()
        zsrc[b, h] = (xacc[b, h] + xbuf[b, h, 2].astype(F32)).astype(BF16)
        up = (zh == h).astype(jnp.int32)
        z_copies[b, h] = remote(
            zsrc.at[b, h], zbuf.at[b, 1 - up], zs.at[b, h], zr.at[b, 1 - up], at_z(12 - 8 * up)
        )
        z_copies[b, h].start()

    extra = (
        (3, 0, 0, 3, 4), (3, 0, 1, 0, 4), (3, 1, 0, 0, 4),
        (2, 0, 1, 2, 4), (2, 1, 0, 0, 4), (1, 1, 0, 1, 4),
    )

    def within(to, lo, hi):
        return jnp.logical_and(to >= lo, to < hi)

    def extra_compute(b):
        col = jnp.where(zl == 7, 0, 2)
        kernel = jnp.concatenate([wav[b - 1, r * 3 + col] for r in range(3)], axis=0)

        def body(j, carry):
            q = jnp.where(zl == 7, 8 - j - b, j + b - 4)
            lhs = jnp.concatenate(
                [
                    xb[q + 3, :, pl.ds(PAD + ro * b * 12, 80), :].reshape(240, 128)
                    for ro in (-1, 0, 1)
                ],
                axis=1,
            )
            res = jnp.dot(lhs, kernel, preferred_element_type=F32)
            res = res.astype(BF16).reshape(3, 80, 256)
            for t in range(3):
                s = 3 * j + t
                part2[b - 1, (s // 4) % 2, s // 8, s % 4] = res[t]
            return carry

        lax.fori_loop(4 - b, 4, body, 0)

    def extra_core(b, h, cc, lo, hi):
        n = hi - lo
        return remote(
            part2.at[b - 1, cc, h, pl.ds(lo, n)], cbuf2.at[b - 1, h, pl.ds(lo, n)],
            cs2.at[b - 1, h], cr2.at[b - 1, h], at(c_=1 - c),
        )

    def extra_core_send(b):
        for u in extra:
            if u[0] == b:
                pl.when(c != u[2])(extra_core(*u).start)

    def extra_x(b, h, d):
        to = (x + d) % 4
        return remote(
            part2.at[b - 1, c, h, to], xbuf2.at[b - 1, h, d - 1],
            xs2.at[b - 1, h, d - 1], xr2.at[b - 1, h, d - 1], at(x_=to),
        )

    def extra_z(b, h):
        zz = (7 - zl + 4 + 8 * h) % 16
        return remote(
            zsrc2.at[b - 1, h], zbuf2.at[b - 1, zh], zs2.at[b - 1, h], zr2.at[b - 1, zh],
            ((zz % 8) * 4 + y, (zz // 8) * 8 + x * 2 + c),
        )

    def extra_core_reduce(b, h, cc, lo, hi):
        @pl.when(c == cc)
        def _():
            extra_core(b, h, cc, lo, hi).wait_recv()
            for i in range(lo, hi):
                mine = part2[b - 1, cc, h, i].astype(F32) + cbuf2[b - 1, h, i].astype(F32)
                part2[b - 1, cc, h, i] = mine.astype(BF16)
            for d in (2, 1, 3):
                pl.when(within((x + d) % 4, lo, hi))(extra_x(b, h, d).start)

    def extra_x_reduce(b, h, cc, lo, hi):
        @pl.when(jnp.logical_and(c == cc, within(x, lo, hi)))
        def _():
            t = part2[b - 1, cc, h, x].astype(F32)
            for d in (2, 1, 3):
                extra_x(b, h, d).wait_recv()
                t = t + xbuf2[b - 1, h, d - 1].astype(F32)
            zsrc2[b - 1, h] = t.astype(BF16)
            extra_z(b, h).start()

    def extra_sent(b, h, cc, lo, hi):
        pl.when(c != cc)(extra_core(b, h, cc, lo, hi).wait_send)

        @pl.when(c == cc)
        def _():
            for d in (2, 1, 3):
                pl.when(within((x + d) % 4, lo, hi))(extra_x(b, h, d).wait_send)
            pl.when(within(x, lo, hi))(extra_z(b, h).wait_send)

    def extra_step(step):
        @pl.when(edge)
        def _():
            for u in extra:
                step(*u)

    own = poolsrc[0] + pool_get(0) + pool_get(1) + pool_get(2)
    poolsrc[1] = own
    pool_send(poolsrc.at[1], 9, at(c_=1 - c))
    compute(0, 0, 3)
    core_send(0, 0)
    compute(0, 3, 5)
    core_send(0, 1)
    compute(1, 0, 3)
    core_send(1, 0)
    both = own + pool_get(9)
    poolsrc[5] = both
    for d in range(1, 4):
        pool_send(poolsrc.at[5], 9 + d, at(x_=(x + d) % 4))
    core_reduce(0, 0)
    core_reduce(0, 1)

    @pl.when(edge)
    def _():
        for b in (3, 2, 1):
            extra_compute(b)
            extra_core_send(b)

    core_reduce(1, 0)
    extra_step(extra_core_reduce)
    here = both + pool_get(10) + pool_get(11) + pool_get(12)
    poolsrc[2] = here
    pool_send(poolsrc.at[2], 3, at_z(4))
    pool_send(poolsrc.at[2], 4, at_z(12))
    halo_wait(0)
    compute(2, 0, 3)
    core_send(2, 0)
    compute(1, 3, 5)
    core_send(1, 1)
    x_half(0, 0)
    x_half(0, 1)
    core_reduce(2, 0)
    core_reduce(1, 1)
    halo_wait(1)
    compute(3, 0, 3)
    core_send(3, 0)
    compute(2, 3, 5)
    core_send(2, 1)
    x_reduce(0, 0)
    x_reduce(0, 1)
    x_half(1, 0)
    core_reduce(3, 0)
    core_reduce(2, 1)
    three = here + pool_get(3) + pool_get(4)
    pool_send(poolbuf.at[4], 5, at_z(12))
    halo_wait(2)
    compute(3, 3, 5)
    core_send(3, 1)
    extra_step(extra_x_reduce)
    x_half(2, 0)
    x_half(1, 1)
    x_reduce(1, 0)
    core_reduce(3, 1)
    x_half(3, 0)
    x_half(2, 1)
    four = three + pool_get(5)
    poolsrc[3] = four
    pool_send(poolsrc.at[3], 6, at(zl_=zl + 1 - 2 * (zl % 2)))
    x_reduce(2, 0)
    x_reduce(1, 1)

    place = zl % 4
    middle = jnp.logical_or(place == 1, place == 2)

    def pool_copy(src, slot_i, dev):
        return remote(poolsrc.at[src], poolbuf.at[slot_i], ps.at[slot_i], pr.at[slot_i], dev)

    inward = pool_copy(6, 7, at(zl_=(zl + jnp.where(place == 1, 1, 7)) % 8))
    outward = pool_copy(4, 8, at(zl_=(zl + jnp.where(place == 1, 7, 1)) % 8))
    x_half(3, 1)
    x_reduce(3, 0)
    poolsrc[6] = four + pool_get(6)
    pl.when(middle)(inward.start)
    x_reduce(2, 1)
    x_reduce(3, 1)

    @pl.when(middle)
    def _():
        inward.wait_recv()
        poolsrc[4] = poolsrc[6] + poolbuf[7]
        outward.start()

    for load in loads[4:]:
        load.wait()

    proj = jnp.zeros((80, 256), F32)
    for b in range(4):
        if b == 3:
            @pl.when(jnp.logical_not(middle))
            def _():
                outward.wait_recv()
                poolsrc[4] = poolbuf[8]

            pre_all = poolsrc[4] * (1.0 / 38400.0)
            pooled = jnp.maximum(gain[4:5] * pre_all + shift[4:5], 0.0).astype(BF16)
            pool_term = jnp.dot(
                jnp.broadcast_to(pooled, (16, 256)), wprojv[pl.ds(1024, 256), :],
                preferred_element_type=F32,
            )[0:1]
        for way in range(2):
            remote(
                zsrc.at[b, 0], zbuf.at[b, way], zs.at[b, 0], zr.at[b, way], at_z(4)
            ).wait_recv()
        acc[b] = zbuf[b, 0].astype(F32) + zbuf[b, 1].astype(F32)
        if b > 0:
            over = jnp.zeros((), jnp.bool_)
            for eb, eh, ec, lo, hi in extra:
                if eb == b:
                    mine = jnp.logical_and(bit == eh, c == ec)
                    over = jnp.logical_or(over, jnp.logical_and(mine, within(x, lo, hi)))

            @pl.when(jnp.logical_and(edge_owner, over))
            def _():
                for half in range(2):
                    remote(
                        zsrc2.at[b - 1, 0], zbuf2.at[b - 1, half],
                        zs2.at[b - 1, 0], zr2.at[b - 1, half], at_z(4),
                    ).wait_recv()
                acc[b] += zbuf2[b - 1, 0].astype(F32) + zbuf2[b - 1, 1].astype(F32)

        act = jnp.maximum(acc[b] * gain[b : b + 1] + shift[b : b + 1], 0.0).astype(BF16)
        proj = proj + jnp.dot(act, wprojv[pl.ds(b * 256, 256), :], preferred_element_type=F32)
    head = jnp.maximum(gain[5:6] * (proj + pool_term) + shift[5:6], 0.0)
    head = jnp.concatenate([head, jnp.zeros((48, 256), F32)], axis=0)
    stage[...] = jnp.transpose(head).astype(BF16).reshape(16, 16, 128)

    def out_copy(d):
        return remote(stage.at[d], obuf.at[slot], os.at[d], orr.at[slot], (zl_dst * 4 + y_dst, d))

    def out_send(i, carry):
        @pl.when(has_col)
        def _():
            out_copy((ch + i) % 16).start()

        return carry

    lax.fori_loop(0, 16, out_send, 0)
    for copy in ycopies + list(psends.values()):
        copy.wait_send()
    for d in range(3):
        for side in range(2):
            pl.when(halo_out[side])(halo_copy(d, side).wait_send)

    @pl.when(middle)
    def _():
        inward.wait_send()
        outward.wait_send()

    @pl.when(edge)
    def _():
        for u in extra:
            extra_sent(*u)

    for u in core_copies:
        for copy in [core_copies[u], z_copies[u]] + x_copies[u]:
            copy.wait_send()

    def out_recv(i, carry):
        remote(stage.at[0], obuf.at[i], os.at[0], orr.at[i], east).wait_recv()
        return carry

    lax.fori_loop(0, 15, out_recv, 0)
    out[...] = obuf[:, :, 0:80]

    def out_sent(d, carry):
        @pl.when(has_col)
        def _():
            out_copy(d).wait_send()

        return carry

    lax.fori_loop(0, 16, out_sent, 0)


def local(features, pointwise_weight, w_atrous, w_pool, w_proj, norm_gain, norm_shift):
    feat = jnp.transpose(features, (1, 0, 2))
    vmem = pl.BlockSpec(memory_space=pltpu.VMEM)
    hbm = pl.BlockSpec(memory_space=pl.ANY)
    dma = pltpu.SemaphoreType.DMA
    out = pl.pallas_call(
        head_kernel,
        out_shape=pltpu.VMEM((15, 16, 80), BF16),
        in_specs=[hbm] * 7,
        out_specs=vmem,
        scratch_shapes=[
            pltpu.VMEM((15, 80, 128), BF16),
            pltpu.VMEM((11, 3, 80 + 2 * PAD, 128), BF16),
            pltpu.VMEM((4, 2, 2, 4, 80, 256), BF16),
            pltpu.VMEM((4, 2, 4, 80, 256), BF16),
            pltpu.VMEM((4, 2, 3, 80, 256), BF16),
            pltpu.VMEM((4, 2, 80, 256), BF16),
            pltpu.VMEM((4, 2, 80, 256), BF16),
            pltpu.VMEM((16, 16, 128), BF16),
            pltpu.VMEM((15, 16, 128), BF16),
            pltpu.VMEM((128, 256), BF16),
            pltpu.VMEM((3, 9, 128, 256), BF16),
            pltpu.VMEM((1280, 256), BF16),
            pltpu.VMEM((128, 256), BF16),
            pltpu.VMEM((6, 256), F32),
            pltpu.VMEM((6, 256), F32),
            pltpu.VMEM((7, 1, 256), F32),
            pltpu.VMEM((13, 1, 256), F32),
            pltpu.VMEM((3, 2, 2, 4, 80, 256), BF16),
            pltpu.VMEM((3, 2, 4, 80, 256), BF16),
            pltpu.VMEM((3, 2, 3, 80, 256), BF16),
            pltpu.VMEM((3, 2, 80, 256), BF16),
            pltpu.VMEM((3, 2, 80, 256), BF16),
            pltpu.VMEM((4, 80, 256), F32),
            pltpu.VMEM((4, 2, 80, 256), F32),
            dma((7,)),
            dma((3,)), dma((3,)),
            dma((6,)), dma((6,)),
            dma((4, 2)), dma((4, 2)),
            dma((4, 2, 3)), dma((4, 2, 3)),
            dma((4, 2)), dma((4, 2)),
            dma((16,)), dma((15,)),
            dma((13,)), dma((13,)),
            dma((3, 2)), dma((3, 2)),
            dma((3, 2, 3)), dma((3, 2, 3)),
            dma((3, 2)), dma((3, 2)),
        ],
        compiler_params=pltpu.CompilerParams(collective_id=0, has_side_effects=True),
        name="aspp_head",
    )(
        feat, pointwise_weight, w_atrous.reshape(3, 9, 128, 256), w_pool, w_proj,
        norm_gain, norm_shift,
    )
    return jnp.transpose(out, (2, 0, 1))


def solution(mesh):
    return jax.shard_map(
        local,
        mesh=mesh,
        in_specs=(
            P(None, "lon", "ch"),
            P("ch", None),
            P(None, None, None, "ch", None),
            P("ch", None),
            P(),
            P(),
            P(),
        ),
        out_specs=P(None, "lon", "ch"),
        check_vma=False,
    )
```

```python
import jax
import jax.numpy as jnp
from jax import lax
from jax.experimental import pallas as pl
from jax.experimental.pallas import tpu as pltpu
from jax.sharding import PartitionSpec as P

MESH_ID = pl.DeviceIdType.MESH
F32 = jnp.float32
BF16 = jnp.bfloat16

PAD = 48


def head_kernel(
    feat, pw, wa, wpool_h, wproj, gain_h, shift_h, out,
    xin, xb, part, cbuf, xbuf, zsrc, zbuf, stage, obuf,
    pwv, wav, wprojv, wpool, gain, shift, poolsrc, poolbuf,
    part2, cbuf2, xbuf2, zsrc2, zbuf2, acc, xacc,
    ld_sem, ys, yr, hs, hr, cs, cr, xs, xr, zs, zr, os, orr, ps, pr,
    cs2, cr2, xs2, xr2, zs2, zr2,
):
    lon = lax.axis_index("lon")
    ch = lax.axis_index("ch")
    zl, y = lon // 4, lon % 4
    zh, x, c = ch // 8, (ch // 2) % 4, ch % 2
    z = zh * 8 + zl

    def at(zl_=None, y_=None, x_=None, c_=None):
        zz = zl if zl_ is None else zl_
        yy = y if y_ is None else y_
        xx = x if x_ is None else x_
        cc = c if c_ is None else c_
        return (zz * 4 + yy, zh * 8 + xx * 2 + cc)

    def at_z(dz):
        zz = (z + dz) % 16
        return ((zz % 8) * 4 + y, (zz // 8) * 8 + x * 2 + c)

    def block_of(j, level):
        q = (j + 1) % 5
        return jnp.where(level == 0, 4 - q, q)

    bit = ((z + 12) % 16) // 8
    zl_dst = (zl + 4) % 8
    k = bit * 8 + c * 4 + x
    kj, kt = k // 3, k % 3
    kq = block_of(kj, zl_dst)
    kg = 4 * kq + y
    y_dst = kg // 5
    slot = (kg % 5) * 3 + kt
    has_col = k < 15

    barrier = pltpu.get_barrier_semaphore()

    def hello(dev):
        pl.semaphore_signal(barrier, inc=1, device_id=dev, device_id_type=MESH_ID)

    east, west = at(zl_=(zl + 1) % 8), at(zl_=(zl + 7) % 8)
    edge = jnp.logical_or(zl == 0, zl == 7)
    edge_owner = jnp.logical_or(zl == 3, zl == 4)

    @pl.when(edge_owner)
    def _():
        far = jnp.where(zl == 4, 7, 0) * 4 + y
        hello((far, x * 2 + c))
        hello((far, 8 + x * 2 + c))

    @pl.when(zl < 7)
    def _():
        hello(east)

    @pl.when(zl > 0)
    def _():
        hello(west)

    hello(at_z(4))
    hello(at_z(12))

    for d in range(1, 4):
        hello(at(y_=(y + d) % 4))
        hello(at(x_=(x + d) % 4))
    hello(at(c_=1 - c))

    loads = [
        pltpu.make_async_copy(src, dst, ld_sem.at[i])
        for i, (src, dst) in enumerate((
            (feat, xin), (wpool_h, wpool), (pw, pwv), (wa, wav),
            (wproj, wprojv), (gain_h, gain), (shift_h, shift),
        ))
    ]
    for load in loads:
        load.start()

    zrow = jnp.zeros((3, PAD, 128), BF16)

    def clear(i, carry):
        xb[i, :, pl.ds(0, PAD), :] = zrow
        xb[i, :, pl.ds(PAD + 80, PAD), :] = zrow
        return carry

    lax.fori_loop(0, 11, clear, 0)
    for b in range(4):
        part[b, 1, 1, 3] = jnp.zeros((80, 256), BF16)

    blank = jnp.zeros((3, 80, 128), BF16)

    @pl.when(edge)
    def _():
        for d in range(3):
            xb[jnp.where(zl == 0, d, 8 + d), :, pl.ds(PAD, 80), :] = blank

    loads[0].wait()
    loads[1].wait()
    xb[y + 3, :, pl.ds(PAD, 80), :] = xin[0:3]
    xb[y + 4, :, pl.ds(PAD, 80), :] = xin[12:15]

    def add_col(i, tot):
        return tot + jnp.sum(xin[i].astype(F32).reshape(10, 8, 128), axis=0)

    sums = lax.fori_loop(0, 15, add_col, jnp.zeros((8, 128), F32))
    colsum = jnp.sum(sums, axis=0, keepdims=True)
    pre = jnp.dot(
        jnp.broadcast_to(colsum, (8, 128)), wpool[...].astype(F32),
        precision=lax.Precision.HIGHEST, preferred_element_type=F32,
    )[0:1]
    poolsrc[0] = pre

    pl.semaphore_wait(barrier, 11 + edge.astype(jnp.int32))

    def remote(src, dst, ssem, rsem, dev):
        return pltpu.make_async_remote_copy(
            src_ref=src, dst_ref=dst, send_sem=ssem, recv_sem=rsem,
            device_id=dev, device_id_type=MESH_ID,
        )

    rows = pl.ds(PAD, 80)
    ycopies = []
    for g in range(1, 4):
        q = (5 * y + g) // 4
        copy = remote(
            xin.at[pl.ds(3 * g, 3)], xb.at[q + 3, :, rows, :],
            ys.at[g - 1], yr.at[g - 1], at(y_=(y + g) % 4),
        )
        copy.start()
        ycopies.append(copy)
    psends = {}

    def pool_send(src, slot_i, dev):
        psends[slot_i] = remote(src, poolbuf.at[slot_i], ps.at[slot_i], pr.at[slot_i], dev)
        psends[slot_i].start()

    def pool_get(slot_i):
        psends[slot_i].wait_recv()
        return poolbuf[slot_i]

    for d in range(1, 4):
        pool_send(poolsrc.at[0], d - 1, at(y_=(y + d) % 4))

    def halo_copy(d, side):
        q = (4 - d) if side == 0 else d
        q_to = q - 5 if side == 0 else q + 5
        return remote(
            xb.at[q + 3, :, rows, :], xb.at[q_to + 3, :, rows, :],
            hs.at[2 * d + side], hr.at[2 * d + side], east if side == 0 else west,
        )

    halo_out = (zl < 7, zl > 0)
    halo_in = (zl > 0, zl < 7)
    for d, sides in ((0, (0,)), (0, (1,)), (1, (0,)), (1, (1,)), (2, (0, 1))):
        q = (4 - d) if sides[0] == 0 else d
        g = (4 * q + y) % 5

        @pl.when(jnp.logical_and(g > 0, g < 4))
        def _():
            gi = jnp.clip(g - 1, 0, 2)
            remote(
                xin.at[pl.ds(0, 3)], xb.at[q + 3, :, rows, :], ys.at[gi], yr.at[gi], east
            ).wait_recv()

        for side in sides:
            pl.when(halo_out[side])(halo_copy(d, side).start)

    def halo_wait(d):
        for side in range(2):
            pl.when(halo_in[side])(halo_copy(d, side).wait_recv)

    loads[2].wait()
    loads[3].wait()

    def compute(b, lo, hi):
        def body(j, carry):
            q = block_of(j, zl)
            if b == 0:
                lhs = xb[q + 3, :, rows, :].reshape(240, 128)
                res = jnp.dot(lhs, pwv[...], preferred_element_type=F32)
            else:
                taps = []
                for ro in (-1, 0, 1):
                    for co in (-1, 0, 1):
                        taps.append(
                            xb[q + 3 + co * b, :, pl.ds(PAD + ro * b * 12, 80), :].reshape(240, 128)
                        )
                res = jnp.dot(
                    jnp.concatenate(taps, axis=1), wav[b - 1].reshape(1152, 256),
                    preferred_element_type=F32,
                )
            res = res.astype(BF16).reshape(3, 80, 256)
            for t in range(3):
                s = 3 * j + t
                part[b, (s // 4) % 2, s // 8, s % 4] = res[t]
            return carry

        lax.fori_loop(lo, hi, body, 0)

    core_copies, x_copies, z_copies = {}, {}, {}

    def core_send(b, h):
        copy = remote(
            part.at[b, 1 - c, h], cbuf.at[b, h], cs.at[b, h], cr.at[b, h], at(c_=1 - c)
        )
        copy.start()
        core_copies[b, h] = copy

    def core_reduce(b, h):
        core_copies[b, h].wait_recv()

        def body(i, carry):
            mine = part[b, c, h, i].astype(F32) + cbuf[b, h, i].astype(F32)
            part[b, c, h, i] = mine.astype(BF16)
            return carry

        lax.fori_loop(0, 4, body, 0)
        x_copies[b, h] = []
        if (b, h) in direct:
            for d in (2, 1, 3):
                to = (x + d) % 4
                copy = remote(
                    part.at[b, c, h, to], xbuf.at[b, h, d - 1],
                    xs.at[b, h, d - 1], xr.at[b, h, d - 1], at(x_=to),
                )
                copy.start()
                x_copies[b, h].append(copy)
            return
        first = flip if h == 0 else 3 - x
        for i, col in enumerate((first, (x + 2) % 4)):
            copy = remote(
                part.at[b, c, h, col], xbuf.at[b, h, i], xs.at[b, h, i], xr.at[b, h, i],
                at(x_=first),
            )
            copy.start()
            x_copies[b, h].append(copy)

    flip = x + 1 - 2 * (x % 2)
    direct = ((3, 1),)

    def x_half(b, h):
        second = 3 - x if h == 0 else flip
        for copy in x_copies[b, h]:
            copy.wait_recv()
        give = part[b, c, h, second].astype(F32) + xbuf[b, h, 1].astype(F32)
        part[b, c, h, second] = give.astype(BF16)
        copy = remote(
            part.at[b, c, h, second], xbuf.at[b, h, 2], xs.at[b, h, 2], xr.at[b, h, 2],
            at(x_=second),
        )
        copy.start()
        x_copies[b, h].append(copy)
        xacc[b, h] = part[b, c, h, x].astype(F32) + xbuf[b, h, 0].astype(F32)

    def x_reduce(b, h):
        if (b, h) in direct:
            total = part[b, c, h, x].astype(F32)
            for i, copy in enumerate(x_copies[b, h]):
                copy.wait_recv()
                total = total + xbuf[b, h, (1, 0, 2)[i]].astype(F32)
            zsrc[b, h] = total.astype(BF16)
        else:
            x_copies[b, h][2].wait_recv()
            zsrc[b, h] = (xacc[b, h] + xbuf[b, h, 2].astype(F32)).astype(BF16)
        up = (zh == h).astype(jnp.int32)
        z_copies[b, h] = remote(
            zsrc.at[b, h], zbuf.at[b, 1 - up], zs.at[b, h], zr.at[b, 1 - up], at_z(12 - 8 * up)
        )
        z_copies[b, h].start()

    extra = (
        (3, 0, 0, 3, 4), (3, 0, 1, 0, 4), (3, 1, 0, 0, 4),
        (2, 0, 1, 2, 4), (2, 1, 0, 0, 4), (1, 1, 0, 1, 4),
    )

    def within(to, lo, hi):
        return jnp.logical_and(to >= lo, to < hi)

    def extra_compute(b):
        col = jnp.where(zl == 7, 0, 2)
        kernel = jnp.concatenate([wav[b - 1, r * 3 + col] for r in range(3)], axis=0)

        def body(j, carry):
            q = jnp.where(zl == 7, 8 - j - b, j + b - 4)
            lhs = jnp.concatenate(
                [
                    xb[q + 3, :, pl.ds(PAD + ro * b * 12, 80), :].reshape(240, 128)
                    for ro in (-1, 0, 1)
                ],
                axis=1,
            )
            res = jnp.dot(lhs, kernel, preferred_element_type=F32)
            res = res.astype(BF16).reshape(3, 80, 256)
            for t in range(3):
                s = 3 * j + t
                part2[b - 1, (s // 4) % 2, s // 8, s % 4] = res[t]
            return carry

        lax.fori_loop(4 - b, 4, body, 0)

    def extra_core(b, h, cc, lo, hi):
        n = hi - lo
        return remote(
            part2.at[b - 1, cc, h, pl.ds(lo, n)], cbuf2.at[b - 1, h, pl.ds(lo, n)],
            cs2.at[b - 1, h], cr2.at[b - 1, h], at(c_=1 - c),
        )

    def extra_core_send(b):
        for u in extra:
            if u[0] == b:
                pl.when(c != u[2])(extra_core(*u).start)

    def extra_x(b, h, d):
        to = (x + d) % 4
        return remote(
            part2.at[b - 1, c, h, to], xbuf2.at[b - 1, h, d - 1],
            xs2.at[b - 1, h, d - 1], xr2.at[b - 1, h, d - 1], at(x_=to),
        )

    def extra_z(b, h):
        zz = (7 - zl + 4 + 8 * h) % 16
        return remote(
            zsrc2.at[b - 1, h], zbuf2.at[b - 1, zh], zs2.at[b - 1, h], zr2.at[b - 1, zh],
            ((zz % 8) * 4 + y, (zz // 8) * 8 + x * 2 + c),
        )

    def extra_core_reduce(b, h, cc, lo, hi):
        @pl.when(c == cc)
        def _():
            extra_core(b, h, cc, lo, hi).wait_recv()
            for i in range(lo, hi):
                mine = part2[b - 1, cc, h, i].astype(F32) + cbuf2[b - 1, h, i].astype(F32)
                part2[b - 1, cc, h, i] = mine.astype(BF16)
            for d in (2, 1, 3):
                pl.when(within((x + d) % 4, lo, hi))(extra_x(b, h, d).start)

    def extra_x_reduce(b, h, cc, lo, hi):
        @pl.when(jnp.logical_and(c == cc, within(x, lo, hi)))
        def _():
            t = part2[b - 1, cc, h, x].astype(F32)
            for d in (2, 1, 3):
                extra_x(b, h, d).wait_recv()
                t = t + xbuf2[b - 1, h, d - 1].astype(F32)
            zsrc2[b - 1, h] = t.astype(BF16)
            extra_z(b, h).start()

    def extra_sent(b, h, cc, lo, hi):
        pl.when(c != cc)(extra_core(b, h, cc, lo, hi).wait_send)

        @pl.when(c == cc)
        def _():
            for d in (2, 1, 3):
                pl.when(within((x + d) % 4, lo, hi))(extra_x(b, h, d).wait_send)
            pl.when(within(x, lo, hi))(extra_z(b, h).wait_send)

    def extra_step(step):
        @pl.when(edge)
        def _():
            for u in extra:
                step(*u)

    own = poolsrc[0] + pool_get(0) + pool_get(1) + pool_get(2)
    poolsrc[1] = own
    pool_send(poolsrc.at[1], 9, at(c_=1 - c))
    compute(0, 0, 3)
    core_send(0, 0)
    compute(0, 3, 5)
    core_send(0, 1)
    compute(1, 0, 3)
    core_send(1, 0)
    both = own + pool_get(9)
    poolsrc[5] = both
    for d in range(1, 4):
        pool_send(poolsrc.at[5], 9 + d, at(x_=(x + d) % 4))
    core_reduce(0, 0)
    core_reduce(0, 1)

    @pl.when(edge)
    def _():
        for b in (3, 2, 1):
            extra_compute(b)
            extra_core_send(b)

    core_reduce(1, 0)
    extra_step(extra_core_reduce)
    here = both + pool_get(10) + pool_get(11) + pool_get(12)
    poolsrc[2] = here
    pool_send(poolsrc.at[2], 3, at_z(4))
    pool_send(poolsrc.at[2], 4, at_z(12))
    halo_wait(0)
    compute(2, 0, 3)
    core_send(2, 0)
    compute(1, 3, 5)
    core_send(1, 1)
    x_half(0, 0)
    x_half(0, 1)
    core_reduce(2, 0)
    core_reduce(1, 1)
    halo_wait(1)
    compute(3, 0, 3)
    core_send(3, 0)
    compute(2, 3, 5)
    core_send(2, 1)
    x_reduce(0, 0)
    x_reduce(0, 1)
    x_half(1, 0)
    core_reduce(3, 0)
    core_reduce(2, 1)
    three = here + pool_get(3) + pool_get(4)
    pool_send(poolbuf.at[4], 5, at_z(12))
    halo_wait(2)
    compute(3, 3, 5)
    core_send(3, 1)
    extra_step(extra_x_reduce)
    core_reduce(3, 1)
    x_half(2, 0)
    x_half(1, 1)
    x_reduce(1, 0)
    x_half(3, 0)
    x_half(2, 1)
    four = three + pool_get(5)
    poolsrc[3] = four
    pool_send(poolsrc.at[3], 6, at(zl_=zl + 1 - 2 * (zl % 2)))
    x_reduce(2, 0)
    x_reduce(1, 1)

    place = zl % 4
    middle = jnp.logical_or(place == 1, place == 2)

    def pool_copy(src, slot_i, dev):
        return remote(poolsrc.at[src], poolbuf.at[slot_i], ps.at[slot_i], pr.at[slot_i], dev)

    inward = pool_copy(6, 7, at(zl_=(zl + jnp.where(place == 1, 1, 7)) % 8))
    outward = pool_copy(4, 8, at(zl_=(zl + jnp.where(place == 1, 7, 1)) % 8))
    x_reduce(3, 0)
    poolsrc[6] = four + pool_get(6)
    pl.when(middle)(inward.start)
    x_reduce(2, 1)
    x_reduce(3, 1)

    @pl.when(middle)
    def _():
        inward.wait_recv()
        poolsrc[4] = poolsrc[6] + poolbuf[7]
        outward.start()

    for load in loads[4:]:
        load.wait()

    proj = jnp.zeros((80, 256), F32)
    for b in range(4):
        if b == 3:
            @pl.when(jnp.logical_not(middle))
            def _():
                outward.wait_recv()
                poolsrc[4] = poolbuf[8]

            pre_all = poolsrc[4] * (1.0 / 38400.0)
            pooled = jnp.maximum(gain[4:5] * pre_all + shift[4:5], 0.0).astype(BF16)
            pool_term = jnp.dot(
                jnp.broadcast_to(pooled, (16, 256)), wprojv[pl.ds(1024, 256), :],
                preferred_element_type=F32,
            )[0:1]
        for way in range(2):
            remote(
                zsrc.at[b, 0], zbuf.at[b, way], zs.at[b, 0], zr.at[b, way], at_z(4)
            ).wait_recv()
        acc[b] = zbuf[b, 0].astype(F32) + zbuf[b, 1].astype(F32)
        if b > 0:
            over = jnp.zeros((), jnp.bool_)
            for eb, eh, ec, lo, hi in extra:
                if eb == b:
                    mine = jnp.logical_and(bit == eh, c == ec)
                    over = jnp.logical_or(over, jnp.logical_and(mine, within(x, lo, hi)))

            @pl.when(jnp.logical_and(edge_owner, over))
            def _():
                for half in range(2):
                    remote(
                        zsrc2.at[b - 1, 0], zbuf2.at[b - 1, half],
                        zs2.at[b - 1, 0], zr2.at[b - 1, half], at_z(4),
                    ).wait_recv()
                acc[b] += zbuf2[b - 1, 0].astype(F32) + zbuf2[b - 1, 1].astype(F32)

        act = jnp.maximum(acc[b] * gain[b : b + 1] + shift[b : b + 1], 0.0).astype(BF16)
        proj = proj + jnp.dot(act, wprojv[pl.ds(b * 256, 256), :], preferred_element_type=F32)
    head = jnp.maximum(gain[5:6] * (proj + pool_term) + shift[5:6], 0.0)
    head = jnp.concatenate([head, jnp.zeros((48, 256), F32)], axis=0)
    stage[...] = jnp.transpose(head).astype(BF16).reshape(16, 16, 128)

    def out_copy(d):
        return remote(stage.at[d], obuf.at[slot], os.at[d], orr.at[slot], (zl_dst * 4 + y_dst, d))

    def out_send(i, carry):
        @pl.when(has_col)
        def _():
            out_copy((ch + i) % 16).start()

        return carry

    lax.fori_loop(0, 16, out_send, 0)
    for copy in ycopies + list(psends.values()):
        copy.wait_send()
    for d in range(3):
        for side in range(2):
            pl.when(halo_out[side])(halo_copy(d, side).wait_send)

    @pl.when(middle)
    def _():
        inward.wait_send()
        outward.wait_send()

    @pl.when(edge)
    def _():
        for u in extra:
            extra_sent(*u)

    for u in core_copies:
        for copy in [core_copies[u], z_copies[u]] + x_copies[u]:
            copy.wait_send()

    def out_recv(i, carry):
        remote(stage.at[0], obuf.at[i], os.at[0], orr.at[i], east).wait_recv()
        return carry

    lax.fori_loop(0, 15, out_recv, 0)
    out[...] = obuf[:, :, 0:80]

    def out_sent(d, carry):
        @pl.when(has_col)
        def _():
            out_copy(d).wait_send()

        return carry

    lax.fori_loop(0, 16, out_sent, 0)


def local(features, pointwise_weight, w_atrous, w_pool, w_proj, norm_gain, norm_shift):
    feat = jnp.transpose(features, (1, 0, 2))
    vmem = pl.BlockSpec(memory_space=pltpu.VMEM)
    hbm = pl.BlockSpec(memory_space=pl.ANY)
    dma = pltpu.SemaphoreType.DMA
    out = pl.pallas_call(
        head_kernel,
        out_shape=pltpu.VMEM((15, 16, 80), BF16),
        in_specs=[hbm] * 7,
        out_specs=vmem,
        scratch_shapes=[
            pltpu.VMEM((15, 80, 128), BF16),
            pltpu.VMEM((11, 3, 80 + 2 * PAD, 128), BF16),
            pltpu.VMEM((4, 2, 2, 4, 80, 256), BF16),
            pltpu.VMEM((4, 2, 4, 80, 256), BF16),
            pltpu.VMEM((4, 2, 3, 80, 256), BF16),
            pltpu.VMEM((4, 2, 80, 256), BF16),
            pltpu.VMEM((4, 2, 80, 256), BF16),
            pltpu.VMEM((16, 16, 128), BF16),
            pltpu.VMEM((15, 16, 128), BF16),
            pltpu.VMEM((128, 256), BF16),
            pltpu.VMEM((3, 9, 128, 256), BF16),
            pltpu.VMEM((1280, 256), BF16),
            pltpu.VMEM((128, 256), BF16),
            pltpu.VMEM((6, 256), F32),
            pltpu.VMEM((6, 256), F32),
            pltpu.VMEM((7, 1, 256), F32),
            pltpu.VMEM((13, 1, 256), F32),
            pltpu.VMEM((3, 2, 2, 4, 80, 256), BF16),
            pltpu.VMEM((3, 2, 4, 80, 256), BF16),
            pltpu.VMEM((3, 2, 3, 80, 256), BF16),
            pltpu.VMEM((3, 2, 80, 256), BF16),
            pltpu.VMEM((3, 2, 80, 256), BF16),
            pltpu.VMEM((4, 80, 256), F32),
            pltpu.VMEM((4, 2, 80, 256), F32),
            dma((7,)),
            dma((3,)), dma((3,)),
            dma((6,)), dma((6,)),
            dma((4, 2)), dma((4, 2)),
            dma((4, 2, 3)), dma((4, 2, 3)),
            dma((4, 2)), dma((4, 2)),
            dma((16,)), dma((15,)),
            dma((13,)), dma((13,)),
            dma((3, 2)), dma((3, 2)),
            dma((3, 2, 3)), dma((3, 2, 3)),
            dma((3, 2)), dma((3, 2)),
        ],
        compiler_params=pltpu.CompilerParams(collective_id=0, has_side_effects=True),
        name="aspp_head",
    )(
        feat, pointwise_weight, w_atrous.reshape(3, 9, 128, 256), w_pool, w_proj,
        norm_gain, norm_shift,
    )
    return jnp.transpose(out, (2, 0, 1))


def solution(mesh):
    return jax.shard_map(
        local,
        mesh=mesh,
        in_specs=(
            P(None, "lon", "ch"),
            P("ch", None),
            P(None, None, None, "ch", None),
            P("ch", None),
            P(),
            P(),
            P(),
        ),
        out_specs=P(None, "lon", "ch"),
        check_vma=False,
    )
```

```python
import jax
import jax.numpy as jnp
from jax import lax
from jax.experimental import pallas as pl
from jax.experimental.pallas import tpu as pltpu
from jax.sharding import PartitionSpec as P

MESH_ID = pl.DeviceIdType.MESH
F32 = jnp.float32
BF16 = jnp.bfloat16

PAD = 48


def head_kernel(
    feat, pw, wa, wpool_h, wproj, gain_h, shift_h, out,
    xin, xb, part, cbuf, xbuf, zsrc, zbuf, stage, obuf,
    pwv, wav, wprojv, wpool, gain, shift, poolsrc, poolbuf,
    part2, cbuf2, xbuf2, zsrc2, zbuf2, acc, xacc,
    ld_sem, ys, yr, hs, hr, cs, cr, xs, xr, zs, zr, os, orr, ps, pr,
    cs2, cr2, xs2, xr2, zs2, zr2,
):
    lon = lax.axis_index("lon")
    ch = lax.axis_index("ch")
    zl, y = lon // 4, lon % 4
    zh, x, c = ch // 8, (ch // 2) % 4, ch % 2
    z = zh * 8 + zl

    def at(zl_=None, y_=None, x_=None, c_=None):
        zz = zl if zl_ is None else zl_
        yy = y if y_ is None else y_
        xx = x if x_ is None else x_
        cc = c if c_ is None else c_
        return (zz * 4 + yy, zh * 8 + xx * 2 + cc)

    def at_z(dz):
        zz = (z + dz) % 16
        return ((zz % 8) * 4 + y, (zz // 8) * 8 + x * 2 + c)

    def block_of(j, level):
        q = (j + 1) % 5
        return jnp.where(level == 0, 4 - q, q)

    bit = ((z + 12) % 16) // 8
    zl_dst = (zl + 4) % 8
    k = bit * 8 + c * 4 + x
    kj, kt = k // 3, k % 3
    kq = block_of(kj, zl_dst)
    kg = 4 * kq + y
    y_dst = kg // 5
    slot = (kg % 5) * 3 + kt
    has_col = k < 15

    barrier = pltpu.get_barrier_semaphore()

    def hello(dev):
        pl.semaphore_signal(barrier, inc=1, device_id=dev, device_id_type=MESH_ID)

    east, west = at(zl_=(zl + 1) % 8), at(zl_=(zl + 7) % 8)
    edge = jnp.logical_or(zl == 0, zl == 7)
    edge_owner = jnp.logical_or(zl == 3, zl == 4)

    @pl.when(edge_owner)
    def _():
        far = jnp.where(zl == 4, 7, 0) * 4 + y
        hello((far, x * 2 + c))
        hello((far, 8 + x * 2 + c))

    @pl.when(zl < 7)
    def _():
        hello(east)

    @pl.when(zl > 0)
    def _():
        hello(west)

    hello(at_z(4))
    hello(at_z(12))

    for d in range(1, 4):
        hello(at(y_=(y + d) % 4))
        hello(at(x_=(x + d) % 4))
    hello(at(c_=1 - c))

    loads = [
        pltpu.make_async_copy(src, dst, ld_sem.at[i])
        for i, (src, dst) in enumerate((
            (feat, xin), (wpool_h, wpool), (pw, pwv), (wa, wav),
            (wproj, wprojv), (gain_h, gain), (shift_h, shift),
        ))
    ]
    for load in loads:
        load.start()

    zrow = jnp.zeros((3, PAD, 128), BF16)

    def clear(i, carry):
        xb[i, :, pl.ds(0, PAD), :] = zrow
        xb[i, :, pl.ds(PAD + 80, PAD), :] = zrow
        return carry

    lax.fori_loop(0, 11, clear, 0)
    for b in range(4):
        part[b, 1, 1, 3] = jnp.zeros((80, 256), BF16)

    blank = jnp.zeros((3, 80, 128), BF16)

    @pl.when(edge)
    def _():
        for d in range(3):
            xb[jnp.where(zl == 0, d, 8 + d), :, pl.ds(PAD, 80), :] = blank

    loads[0].wait()
    loads[1].wait()
    xb[y + 3, :, pl.ds(PAD, 80), :] = xin[0:3]
    xb[y + 4, :, pl.ds(PAD, 80), :] = xin[12:15]

    def add_col(i, tot):
        return tot + jnp.sum(xin[i].astype(F32).reshape(10, 8, 128), axis=0)

    sums = lax.fori_loop(0, 15, add_col, jnp.zeros((8, 128), F32))
    colsum = jnp.sum(sums, axis=0, keepdims=True)
    pre = jnp.dot(
        jnp.broadcast_to(colsum, (8, 128)), wpool[...].astype(F32),
        precision=lax.Precision.HIGHEST, preferred_element_type=F32,
    )[0:1]
    poolsrc[0] = pre

    pl.semaphore_wait(barrier, 11 + edge.astype(jnp.int32))

    def remote(src, dst, ssem, rsem, dev):
        return pltpu.make_async_remote_copy(
            src_ref=src, dst_ref=dst, send_sem=ssem, recv_sem=rsem,
            device_id=dev, device_id_type=MESH_ID,
        )

    rows = pl.ds(PAD, 80)
    ycopies = []
    for g in range(1, 4):
        q = (5 * y + g) // 4
        copy = remote(
            xin.at[pl.ds(3 * g, 3)], xb.at[q + 3, :, rows, :],
            ys.at[g - 1], yr.at[g - 1], at(y_=(y + g) % 4),
        )
        copy.start()
        ycopies.append(copy)
    psends = {}

    def pool_send(src, slot_i, dev):
        psends[slot_i] = remote(src, poolbuf.at[slot_i], ps.at[slot_i], pr.at[slot_i], dev)
        psends[slot_i].start()

    def pool_get(slot_i):
        psends[slot_i].wait_recv()
        return poolbuf[slot_i]

    for d in range(1, 4):
        pool_send(poolsrc.at[0], d - 1, at(y_=(y + d) % 4))

    def halo_copy(d, side):
        q = (4 - d) if side == 0 else d
        q_to = q - 5 if side == 0 else q + 5
        return remote(
            xb.at[q + 3, :, rows, :], xb.at[q_to + 3, :, rows, :],
            hs.at[2 * d + side], hr.at[2 * d + side], east if side == 0 else west,
        )

    halo_out = (zl < 7, zl > 0)
    halo_in = (zl > 0, zl < 7)
    for d, sides in ((0, (0,)), (0, (1,)), (1, (0,)), (1, (1,)), (2, (0, 1))):
        q = (4 - d) if sides[0] == 0 else d
        g = (4 * q + y) % 5

        @pl.when(jnp.logical_and(g > 0, g < 4))
        def _():
            gi = jnp.clip(g - 1, 0, 2)
            remote(
                xin.at[pl.ds(0, 3)], xb.at[q + 3, :, rows, :], ys.at[gi], yr.at[gi], east
            ).wait_recv()

        for side in sides:
            pl.when(halo_out[side])(halo_copy(d, side).start)

    def halo_wait(d):
        for side in range(2):
            pl.when(halo_in[side])(halo_copy(d, side).wait_recv)

    loads[2].wait()
    loads[3].wait()

    def compute(b, lo, hi):
        def body(j, carry):
            q = block_of(j, zl)
            if b == 0:
                lhs = xb[q + 3, :, rows, :].reshape(240, 128)
                res = jnp.dot(lhs, pwv[...], preferred_element_type=F32)
            else:
                taps = []
                for ro in (-1, 0, 1):
                    for co in (-1, 0, 1):
                        taps.append(
                            xb[q + 3 + co * b, :, pl.ds(PAD + ro * b * 12, 80), :].reshape(240, 128)
                        )
                res = jnp.dot(
                    jnp.concatenate(taps, axis=1), wav[b - 1].reshape(1152, 256),
                    preferred_element_type=F32,
                )
            res = res.astype(BF16).reshape(3, 80, 256)
            for t in range(3):
                s = 3 * j + t
                part[b, (s // 4) % 2, s // 8, s % 4] = res[t]
            return carry

        lax.fori_loop(lo, hi, body, 0)

    core_copies, x_copies, z_copies = {}, {}, {}

    def core_send(b, h):
        copy = remote(
            part.at[b, 1 - c, h], cbuf.at[b, h], cs.at[b, h], cr.at[b, h], at(c_=1 - c)
        )
        copy.start()
        core_copies[b, h] = copy

    def core_reduce(b, h):
        core_copies[b, h].wait_recv()

        def body(i, carry):
            mine = part[b, c, h, i].astype(F32) + cbuf[b, h, i].astype(F32)
            part[b, c, h, i] = mine.astype(BF16)
            return carry

        lax.fori_loop(0, 4, body, 0)
        first = flip if h == 0 else 3 - x
        x_copies[b, h] = []
        for i, col in enumerate((first, (x + 2) % 4)):
            copy = remote(
                part.at[b, c, h, col], xbuf.at[b, h, i], xs.at[b, h, i], xr.at[b, h, i],
                at(x_=first),
            )
            copy.start()
            x_copies[b, h].append(copy)

    flip = x + 1 - 2 * (x % 2)

    def x_half(b, h):
        second = 3 - x if h == 0 else flip
        for copy in x_copies[b, h]:
            copy.wait_recv()
        give = part[b, c, h, second].astype(F32) + xbuf[b, h, 1].astype(F32)
        part[b, c, h, second] = give.astype(BF16)
        copy = remote(
            part.at[b, c, h, second], xbuf.at[b, h, 2], xs.at[b, h, 2], xr.at[b, h, 2],
            at(x_=second),
        )
        copy.start()
        x_copies[b, h].append(copy)
        xacc[b, h] = part[b, c, h, x].astype(F32) + xbuf[b, h, 0].astype(F32)

    def x_reduce(b, h):
        x_copies[b, h][2].wait_recv()
        zsrc[b, h] = (xacc[b, h] + xbuf[b, h, 2].astype(F32)).astype(BF16)
        up = (zh == h).astype(jnp.int32)
        z_copies[b, h] = remote(
            zsrc.at[b, h], zbuf.at[b, 1 - up], zs.at[b, h], zr.at[b, 1 - up], at_z(12 - 8 * up)
        )
        z_copies[b, h].start()

    extra = (
        (3, 0, 0, 3, 4), (3, 0, 1, 0, 4), (3, 1, 0, 0, 4),
        (2, 0, 1, 2, 4), (2, 1, 0, 0, 4), (1, 1, 0, 1, 4),
    )

    def within(to, lo, hi):
        return jnp.logical_and(to >= lo, to < hi)

    def extra_compute(b):
        col = jnp.where(zl == 7, 0, 2)
        kernel = jnp.concatenate([wav[b - 1, r * 3 + col] for r in range(3)], axis=0)

        def body(j, carry):
            q = jnp.where(zl == 7, 8 - j - b, j + b - 4)
            lhs = jnp.concatenate(
                [
                    xb[q + 3, :, pl.ds(PAD + ro * b * 12, 80), :].reshape(240, 128)
                    for ro in (-1, 0, 1)
                ],
                axis=1,
            )
            res = jnp.dot(lhs, kernel, preferred_element_type=F32)
            res = res.astype(BF16).reshape(3, 80, 256)
            for t in range(3):
                s = 3 * j + t
                part2[b - 1, (s // 4) % 2, s // 8, s % 4] = res[t]
            return carry

        lax.fori_loop(4 - b, 4, body, 0)

    def extra_core(b, h, cc, lo, hi):
        n = hi - lo
        return remote(
            part2.at[b - 1, cc, h, pl.ds(lo, n)], cbuf2.at[b - 1, h, pl.ds(lo, n)],
            cs2.at[b - 1, h], cr2.at[b - 1, h], at(c_=1 - c),
        )

    def extra_core_send(b):
        for u in extra:
            if u[0] == b:
                pl.when(c != u[2])(extra_core(*u).start)

    def extra_x(b, h, d):
        to = (x + d) % 4
        return remote(
            part2.at[b - 1, c, h, to], xbuf2.at[b - 1, h, d - 1],
            xs2.at[b - 1, h, d - 1], xr2.at[b - 1, h, d - 1], at(x_=to),
        )

    def extra_z(b, h):
        zz = (7 - zl + 4 + 8 * h) % 16
        return remote(
            zsrc2.at[b - 1, h], zbuf2.at[b - 1, zh], zs2.at[b - 1, h], zr2.at[b - 1, zh],
            ((zz % 8) * 4 + y, (zz // 8) * 8 + x * 2 + c),
        )

    def extra_core_reduce(b, h, cc, lo, hi):
        @pl.when(c == cc)
        def _():
            extra_core(b, h, cc, lo, hi).wait_recv()
            for i in range(lo, hi):
                mine = part2[b - 1, cc, h, i].astype(F32) + cbuf2[b - 1, h, i].astype(F32)
                part2[b - 1, cc, h, i] = mine.astype(BF16)
            for d in (2, 1, 3):
                pl.when(within((x + d) % 4, lo, hi))(extra_x(b, h, d).start)

    def extra_x_reduce(b, h, cc, lo, hi):
        @pl.when(jnp.logical_and(c == cc, within(x, lo, hi)))
        def _():
            t = part2[b - 1, cc, h, x].astype(F32)
            for d in (2, 1, 3):
                extra_x(b, h, d).wait_recv()
                t = t + xbuf2[b - 1, h, d - 1].astype(F32)
            zsrc2[b - 1, h] = t.astype(BF16)
            extra_z(b, h).start()

    def extra_sent(b, h, cc, lo, hi):
        pl.when(c != cc)(extra_core(b, h, cc, lo, hi).wait_send)

        @pl.when(c == cc)
        def _():
            for d in (2, 1, 3):
                pl.when(within((x + d) % 4, lo, hi))(extra_x(b, h, d).wait_send)
            pl.when(within(x, lo, hi))(extra_z(b, h).wait_send)

    def extra_step(step):
        @pl.when(edge)
        def _():
            for u in extra:
                step(*u)

    own = poolsrc[0] + pool_get(0) + pool_get(1) + pool_get(2)
    poolsrc[1] = own
    pool_send(poolsrc.at[1], 9, at(c_=1 - c))
    compute(0, 0, 3)
    core_send(0, 0)
    compute(0, 3, 5)
    core_send(0, 1)
    compute(1, 0, 3)
    core_send(1, 0)
    both = own + pool_get(9)
    poolsrc[5] = both
    for d in range(1, 4):
        pool_send(poolsrc.at[5], 9 + d, at(x_=(x + d) % 4))
    core_reduce(0, 0)
    core_reduce(0, 1)

    @pl.when(edge)
    def _():
        for b in (3, 2, 1):
            extra_compute(b)
            extra_core_send(b)

    core_reduce(1, 0)
    extra_step(extra_core_reduce)
    here = both + pool_get(10) + pool_get(11) + pool_get(12)
    poolsrc[2] = here
    pool_send(poolsrc.at[2], 3, at_z(4))
    pool_send(poolsrc.at[2], 4, at_z(12))
    halo_wait(0)
    compute(2, 0, 3)
    core_send(2, 0)
    compute(1, 3, 5)
    core_send(1, 1)
    x_half(0, 0)
    x_half(0, 1)
    core_reduce(2, 0)
    core_reduce(1, 1)
    halo_wait(1)
    compute(3, 0, 3)
    core_send(3, 0)
    compute(2, 3, 5)
    core_send(2, 1)
    x_reduce(0, 0)
    x_reduce(0, 1)
    x_half(1, 0)
    core_reduce(3, 0)
    core_reduce(2, 1)
    three = here + pool_get(3) + pool_get(4)
    pool_send(poolbuf.at[4], 5, at_z(12))
    halo_wait(2)
    compute(3, 3, 5)
    core_send(3, 1)
    extra_step(extra_x_reduce)
    x_half(2, 0)
    x_half(1, 1)
    x_reduce(1, 0)
    core_reduce(3, 1)
    x_half(3, 0)
    x_half(2, 1)
    four = three + pool_get(5)
    poolsrc[3] = four
    pool_send(poolsrc.at[3], 6, at(zl_=zl + 1 - 2 * (zl % 2)))
    x_reduce(2, 0)
    x_reduce(1, 1)

    place = zl % 4
    middle = jnp.logical_or(place == 1, place == 2)

    def pool_copy(src, slot_i, dev):
        return remote(poolsrc.at[src], poolbuf.at[slot_i], ps.at[slot_i], pr.at[slot_i], dev)

    inward = pool_copy(6, 7, at(zl_=(zl + jnp.where(place == 1, 1, 7)) % 8))
    outward = pool_copy(4, 8, at(zl_=(zl + jnp.where(place == 1, 7, 1)) % 8))
    x_half(3, 1)
    x_reduce(3, 0)
    poolsrc[6] = four + pool_get(6)
    pl.when(middle)(inward.start)
    x_reduce(2, 1)
    x_reduce(3, 1)

    @pl.when(middle)
    def _():
        inward.wait_recv()
        poolsrc[4] = poolsrc[6] + poolbuf[7]
        outward.start()

    for load in loads[4:]:
        load.wait()

    proj = jnp.zeros((80, 256), F32)
    for b in range(4):
        if b == 3:
            @pl.when(jnp.logical_not(middle))
            def _():
                outward.wait_recv()
                poolsrc[4] = poolbuf[8]

            pre_all = poolsrc[4] * (1.0 / 38400.0)
            pooled = jnp.maximum(gain[4:5] * pre_all + shift[4:5], 0.0).astype(BF16)
            pool_term = jnp.dot(
                jnp.broadcast_to(pooled, (16, 256)), wprojv[pl.ds(1024, 256), :],
                preferred_element_type=F32,
            )[0:1]
        for way in range(2):
            remote(
                zsrc.at[b, 0], zbuf.at[b, way], zs.at[b, 0], zr.at[b, way], at_z(4)
            ).wait_recv()
        acc[b] = zbuf[b, 0].astype(F32) + zbuf[b, 1].astype(F32)
        if b > 0:
            over = jnp.zeros((), jnp.bool_)
            for eb, eh, ec, lo, hi in extra:
                if eb == b:
                    mine = jnp.logical_and(bit == eh, c == ec)
                    over = jnp.logical_or(over, jnp.logical_and(mine, within(x, lo, hi)))

            @pl.when(jnp.logical_and(edge_owner, over))
            def _():
                for half in range(2):
                    remote(
                        zsrc2.at[b - 1, 0], zbuf2.at[b - 1, half],
                        zs2.at[b - 1, 0], zr2.at[b - 1, half], at_z(4),
                    ).wait_recv()
                acc[b] += zbuf2[b - 1, 0].astype(F32) + zbuf2[b - 1, 1].astype(F32)

        act = jnp.maximum(acc[b] * gain[b : b + 1] + shift[b : b + 1], 0.0).astype(BF16)
        proj = proj + jnp.dot(act, wprojv[pl.ds(b * 256, 256), :], preferred_element_type=F32)
    head = jnp.maximum(gain[5:6] * (proj + pool_term) + shift[5:6], 0.0)
    head = jnp.concatenate([head, jnp.zeros((48, 256), F32)], axis=0)
    stage[...] = jnp.transpose(head).astype(BF16).reshape(16, 16, 128)

    def out_copy(d):
        return remote(stage.at[d], obuf.at[slot], os.at[d], orr.at[slot], (zl_dst * 4 + y_dst, d))

    @pl.when(has_col)
    def _():
        for dx in (2, 1, 3, 0):
            for cc in range(2):
                for half in range(2):
                    out_copy(half * 8 + (x + dx) % 4 * 2 + cc).start()

    for copy in ycopies + list(psends.values()):
        copy.wait_send()
    for d in range(3):
        for side in range(2):
            pl.when(halo_out[side])(halo_copy(d, side).wait_send)

    @pl.when(middle)
    def _():
        inward.wait_send()
        outward.wait_send()

    @pl.when(edge)
    def _():
        for u in extra:
            extra_sent(*u)

    for u in core_copies:
        for copy in [core_copies[u], z_copies[u]] + x_copies[u]:
            copy.wait_send()

    def out_recv(i, carry):
        remote(stage.at[0], obuf.at[i], os.at[0], orr.at[i], east).wait_recv()
        return carry

    lax.fori_loop(0, 15, out_recv, 0)
    out[...] = obuf[:, :, 0:80]

    def out_sent(d, carry):
        @pl.when(has_col)
        def _():
            out_copy(d).wait_send()

        return carry

    lax.fori_loop(0, 16, out_sent, 0)


def local(features, pointwise_weight, w_atrous, w_pool, w_proj, norm_gain, norm_shift):
    feat = jnp.transpose(features, (1, 0, 2))
    vmem = pl.BlockSpec(memory_space=pltpu.VMEM)
    hbm = pl.BlockSpec(memory_space=pl.ANY)
    dma = pltpu.SemaphoreType.DMA
    out = pl.pallas_call(
        head_kernel,
        out_shape=pltpu.VMEM((15, 16, 80), BF16),
        in_specs=[hbm] * 7,
        out_specs=vmem,
        scratch_shapes=[
            pltpu.VMEM((15, 80, 128), BF16),
            pltpu.VMEM((11, 3, 80 + 2 * PAD, 128), BF16),
            pltpu.VMEM((4, 2, 2, 4, 80, 256), BF16),
            pltpu.VMEM((4, 2, 4, 80, 256), BF16),
            pltpu.VMEM((4, 2, 3, 80, 256), BF16),
            pltpu.VMEM((4, 2, 80, 256), BF16),
            pltpu.VMEM((4, 2, 80, 256), BF16),
            pltpu.VMEM((16, 16, 128), BF16),
            pltpu.VMEM((15, 16, 128), BF16),
            pltpu.VMEM((128, 256), BF16),
            pltpu.VMEM((3, 9, 128, 256), BF16),
            pltpu.VMEM((1280, 256), BF16),
            pltpu.VMEM((128, 256), BF16),
            pltpu.VMEM((6, 256), F32),
            pltpu.VMEM((6, 256), F32),
            pltpu.VMEM((7, 1, 256), F32),
            pltpu.VMEM((13, 1, 256), F32),
            pltpu.VMEM((3, 2, 2, 4, 80, 256), BF16),
            pltpu.VMEM((3, 2, 4, 80, 256), BF16),
            pltpu.VMEM((3, 2, 3, 80, 256), BF16),
            pltpu.VMEM((3, 2, 80, 256), BF16),
            pltpu.VMEM((3, 2, 80, 256), BF16),
            pltpu.VMEM((4, 80, 256), F32),
            pltpu.VMEM((4, 2, 80, 256), F32),
            dma((7,)),
            dma((3,)), dma((3,)),
            dma((6,)), dma((6,)),
            dma((4, 2)), dma((4, 2)),
            dma((4, 2, 3)), dma((4, 2, 3)),
            dma((4, 2)), dma((4, 2)),
            dma((16,)), dma((15,)),
            dma((13,)), dma((13,)),
            dma((3, 2)), dma((3, 2)),
            dma((3, 2, 3)), dma((3, 2, 3)),
            dma((3, 2)), dma((3, 2)),
        ],
        compiler_params=pltpu.CompilerParams(collective_id=0, has_side_effects=True),
        name="aspp_head",
    )(
        feat, pointwise_weight, w_atrous.reshape(3, 9, 128, 256), w_pool, w_proj,
        norm_gain, norm_shift,
    )
    return jnp.transpose(out, (2, 0, 1))


def solution(mesh):
    return jax.shard_map(
        local,
        mesh=mesh,
        in_specs=(
            P(None, "lon", "ch"),
            P("ch", None),
            P(None, None, None, "ch", None),
            P("ch", None),
            P(),
            P(),
            P(),
        ),
        out_specs=P(None, "lon", "ch"),
        check_vma=False,
    )
```

```python
import jax
import jax.numpy as jnp
from jax import lax
from jax.experimental import pallas as pl
from jax.experimental.pallas import tpu as pltpu
from jax.sharding import PartitionSpec as P

MESH_ID = pl.DeviceIdType.MESH
F32 = jnp.float32
BF16 = jnp.bfloat16

PAD = 48


def head_kernel(
    feat, pw, wa, wpool_h, wproj, gain_h, shift_h, out,
    xin, xb, part, cbuf, xbuf, zsrc, zbuf, stage, obuf,
    pwv, wav, wprojv, wpool, gain, shift, poolsrc, poolbuf,
    part2, cbuf2, xbuf2, zsrc2, zbuf2, acc, xacc,
    ld_sem, ys, yr, hs, hr, cs, cr, xs, xr, zs, zr, os, orr, ps, pr,
    cs2, cr2, xs2, xr2, zs2, zr2,
):
    lon = lax.axis_index("lon")
    ch = lax.axis_index("ch")
    zl, y = lon // 4, lon % 4
    zh, x, c = ch // 8, (ch // 2) % 4, ch % 2
    z = zh * 8 + zl

    def at(zl_=None, y_=None, x_=None, c_=None):
        zz = zl if zl_ is None else zl_
        yy = y if y_ is None else y_
        xx = x if x_ is None else x_
        cc = c if c_ is None else c_
        return (zz * 4 + yy, zh * 8 + xx * 2 + cc)

    def at_z(dz):
        zz = (z + dz) % 16
        return ((zz % 8) * 4 + y, (zz // 8) * 8 + x * 2 + c)

    def block_of(j, level):
        q = (j + 1) % 5
        return jnp.where(level == 0, 4 - q, q)

    bit = ((z + 12) % 16) // 8
    zl_dst = (zl + 4) % 8
    k = bit * 8 + c * 4 + x
    kj, kt = k // 3, k % 3
    kq = block_of(kj, zl_dst)
    kg = 4 * kq + y
    y_dst = kg // 5
    slot = (kg % 5) * 3 + kt
    has_col = k < 15

    barrier = pltpu.get_barrier_semaphore()

    def hello(dev):
        pl.semaphore_signal(barrier, inc=1, device_id=dev, device_id_type=MESH_ID)

    east, west = at(zl_=(zl + 1) % 8), at(zl_=(zl + 7) % 8)
    edge = jnp.logical_or(zl == 0, zl == 7)
    edge_owner = jnp.logical_or(zl == 3, zl == 4)

    @pl.when(edge_owner)
    def _():
        far = jnp.where(zl == 4, 7, 0) * 4 + y
        hello((far, x * 2 + c))
        hello((far, 8 + x * 2 + c))

    @pl.when(zl < 7)
    def _():
        hello(east)

    @pl.when(zl > 0)
    def _():
        hello(west)

    hello(at_z(4))
    hello(at_z(12))

    for d in range(1, 4):
        hello(at(y_=(y + d) % 4))
        hello(at(x_=(x + d) % 4))
    hello(at(c_=1 - c))

    loads = [
        pltpu.make_async_copy(src, dst, ld_sem.at[i])
        for i, (src, dst) in enumerate((
            (feat, xin), (wpool_h, wpool), (pw, pwv), (wa, wav),
            (wproj, wprojv), (gain_h, gain), (shift_h, shift),
        ))
    ]
    for load in loads:
        load.start()

    zrow = jnp.zeros((3, PAD, 128), BF16)

    def clear(i, carry):
        xb[i, :, pl.ds(0, PAD), :] = zrow
        xb[i, :, pl.ds(PAD + 80, PAD), :] = zrow
        return carry

    lax.fori_loop(0, 11, clear, 0)
    for b in range(4):
        part[b, 1, 1, 3] = jnp.zeros((80, 256), BF16)

    blank = jnp.zeros((3, 80, 128), BF16)

    @pl.when(edge)
    def _():
        for d in range(3):
            xb[jnp.where(zl == 0, d, 8 + d), :, pl.ds(PAD, 80), :] = blank

    loads[0].wait()
    loads[1].wait()
    xb[y + 3, :, pl.ds(PAD, 80), :] = xin[0:3]
    xb[y + 4, :, pl.ds(PAD, 80), :] = xin[12:15]

    def add_col(i, tot):
        return tot + jnp.sum(xin[i].astype(F32).reshape(10, 8, 128), axis=0)

    sums = lax.fori_loop(0, 15, add_col, jnp.zeros((8, 128), F32))
    colsum = jnp.sum(sums, axis=0, keepdims=True)
    pre = jnp.dot(
        jnp.broadcast_to(colsum, (8, 128)), wpool[...].astype(F32),
        precision=lax.Precision.HIGHEST, preferred_element_type=F32,
    )[0:1]
    poolsrc[0] = pre

    pl.semaphore_wait(barrier, 11 + edge.astype(jnp.int32))

    def remote(src, dst, ssem, rsem, dev):
        return pltpu.make_async_remote_copy(
            src_ref=src, dst_ref=dst, send_sem=ssem, recv_sem=rsem,
            device_id=dev, device_id_type=MESH_ID,
        )

    rows = pl.ds(PAD, 80)
    ycopies = []
    for g in range(1, 4):
        q = (5 * y + g) // 4
        copy = remote(
            xin.at[pl.ds(3 * g, 3)], xb.at[q + 3, :, rows, :],
            ys.at[g - 1], yr.at[g - 1], at(y_=(y + g) % 4),
        )
        copy.start()
        ycopies.append(copy)
    psends = {}

    def pool_send(src, slot_i, dev):
        psends[slot_i] = remote(src, poolbuf.at[slot_i], ps.at[slot_i], pr.at[slot_i], dev)
        psends[slot_i].start()

    def pool_get(slot_i):
        psends[slot_i].wait_recv()
        return poolbuf[slot_i]

    for d in range(1, 4):
        pool_send(poolsrc.at[0], d - 1, at(y_=(y + d) % 4))

    def halo_copy(d, side):
        q = (4 - d) if side == 0 else d
        q_to = q - 5 if side == 0 else q + 5
        return remote(
            xb.at[q + 3, :, rows, :], xb.at[q_to + 3, :, rows, :],
            hs.at[2 * d + side], hr.at[2 * d + side], east if side == 0 else west,
        )

    halo_out = (zl < 7, zl > 0)
    halo_in = (zl > 0, zl < 7)
    for d, sides in ((0, (0,)), (0, (1,)), (1, (0,)), (1, (1,)), (2, (0, 1))):
        q = (4 - d) if sides[0] == 0 else d
        g = (4 * q + y) % 5

        @pl.when(jnp.logical_and(g > 0, g < 4))
        def _():
            gi = jnp.clip(g - 1, 0, 2)
            remote(
                xin.at[pl.ds(0, 3)], xb.at[q + 3, :, rows, :], ys.at[gi], yr.at[gi], east
            ).wait_recv()

        for side in sides:
            pl.when(halo_out[side])(halo_copy(d, side).start)

    def halo_wait(d):
        for side in range(2):
            pl.when(halo_in[side])(halo_copy(d, side).wait_recv)

    loads[2].wait()
    loads[3].wait()

    def compute(b, lo, hi):
        def body(j, carry):
            q = block_of(j, zl)
            if b == 0:
                lhs = xb[q + 3, :, rows, :].reshape(240, 128)
                res = jnp.dot(lhs, pwv[...], preferred_element_type=F32)
            else:
                taps = []
                for ro in (-1, 0, 1):
                    for co in (-1, 0, 1):
                        taps.append(
                            xb[q + 3 + co * b, :, pl.ds(PAD + ro * b * 12, 80), :].reshape(240, 128)
                        )
                res = jnp.dot(
                    jnp.concatenate(taps, axis=1), wav[b - 1].reshape(1152, 256),
                    preferred_element_type=F32,
                )
            res = res.astype(BF16).reshape(3, 80, 256)
            for t in range(3):
                s = 3 * j + t
                part[b, (s // 4) % 2, s // 8, s % 4] = res[t]
            return carry

        lax.fori_loop(lo, hi, body, 0)

    core_copies, x_copies, z_copies = {}, {}, {}

    def core_send(b, h):
        copy = remote(
            part.at[b, 1 - c, h], cbuf.at[b, h], cs.at[b, h], cr.at[b, h], at(c_=1 - c)
        )
        copy.start()
        core_copies[b, h] = copy

    def core_reduce(b, h):
        core_copies[b, h].wait_recv()

        def body(i, carry):
            mine = part[b, c, h, i].astype(F32) + cbuf[b, h, i].astype(F32)
            part[b, c, h, i] = mine.astype(BF16)
            return carry

        lax.fori_loop(0, 4, body, 0)
        first = flip if h == 0 else 3 - x
        x_copies[b, h] = []
        for i, col in enumerate((first, (x + 2) % 4)):
            copy = remote(
                part.at[b, c, h, col], xbuf.at[b, h, i], xs.at[b, h, i], xr.at[b, h, i],
                at(x_=first),
            )
            copy.start()
            x_copies[b, h].append(copy)

    flip = x + 1 - 2 * (x % 2)

    def x_half(b, h):
        second = 3 - x if h == 0 else flip
        for copy in x_copies[b, h]:
            copy.wait_recv()
        give = part[b, c, h, second].astype(F32) + xbuf[b, h, 1].astype(F32)
        part[b, c, h, second] = give.astype(BF16)
        copy = remote(
            part.at[b, c, h, second], xbuf.at[b, h, 2], xs.at[b, h, 2], xr.at[b, h, 2],
            at(x_=second),
        )
        copy.start()
        x_copies[b, h].append(copy)
        xacc[b, h] = part[b, c, h, x].astype(F32) + xbuf[b, h, 0].astype(F32)

    def x_reduce(b, h):
        x_copies[b, h][2].wait_recv()
        zsrc[b, h] = (xacc[b, h] + xbuf[b, h, 2].astype(F32)).astype(BF16)
        up = (zh == h).astype(jnp.int32)
        z_copies[b, h] = remote(
            zsrc.at[b, h], zbuf.at[b, 1 - up], zs.at[b, h], zr.at[b, 1 - up], at_z(12 - 8 * up)
        )
        z_copies[b, h].start()

    extra = (
        (3, 0, 0, 3, 4), (3, 0, 1, 0, 4), (3, 1, 0, 0, 4),
        (2, 0, 1, 2, 4), (2, 1, 0, 0, 4), (1, 1, 0, 1, 4),
    )

    def within(to, lo, hi):
        return jnp.logical_and(to >= lo, to < hi)

    def extra_compute(b):
        col = jnp.where(zl == 7, 0, 2)
        kernel = jnp.concatenate([wav[b - 1, r * 3 + col] for r in range(3)], axis=0)

        def body(j, carry):
            q = jnp.where(zl == 7, 8 - j - b, j + b - 4)
            lhs = jnp.concatenate(
                [
                    xb[q + 3, :, pl.ds(PAD + ro * b * 12, 80), :].reshape(240, 128)
                    for ro in (-1, 0, 1)
                ],
                axis=1,
            )
            res = jnp.dot(lhs, kernel, preferred_element_type=F32)
            res = res.astype(BF16).reshape(3, 80, 256)
            for t in range(3):
                s = 3 * j + t
                part2[b - 1, (s // 4) % 2, s // 8, s % 4] = res[t]
            return carry

        lax.fori_loop(4 - b, 4, body, 0)

    def extra_core(b, h, cc, lo, hi):
        n = hi - lo
        return remote(
            part2.at[b - 1, cc, h, pl.ds(lo, n)], cbuf2.at[b - 1, h, pl.ds(lo, n)],
            cs2.at[b - 1, h], cr2.at[b - 1, h], at(c_=1 - c),
        )

    def extra_core_send(b):
        for u in extra:
            if u[0] == b:
                pl.when(c != u[2])(extra_core(*u).start)

    def extra_x(b, h, d):
        to = (x + d) % 4
        return remote(
            part2.at[b - 1, c, h, to], xbuf2.at[b - 1, h, d - 1],
            xs2.at[b - 1, h, d - 1], xr2.at[b - 1, h, d - 1], at(x_=to),
        )

    def extra_z(b, h):
        zz = (7 - zl + 4 + 8 * h) % 16
        return remote(
            zsrc2.at[b - 1, h], zbuf2.at[b - 1, zh], zs2.at[b - 1, h], zr2.at[b - 1, zh],
            ((zz % 8) * 4 + y, (zz // 8) * 8 + x * 2 + c),
        )

    def extra_core_reduce(b, h, cc, lo, hi):
        @pl.when(c == cc)
        def _():
            extra_core(b, h, cc, lo, hi).wait_recv()
            for i in range(lo, hi):
                mine = part2[b - 1, cc, h, i].astype(F32) + cbuf2[b - 1, h, i].astype(F32)
                part2[b - 1, cc, h, i] = mine.astype(BF16)
            for d in (2, 1, 3):
                pl.when(within((x + d) % 4, lo, hi))(extra_x(b, h, d).start)

    def extra_x_reduce(b, h, cc, lo, hi):
        @pl.when(jnp.logical_and(c == cc, within(x, lo, hi)))
        def _():
            t = part2[b - 1, cc, h, x].astype(F32)
            for d in (2, 1, 3):
                extra_x(b, h, d).wait_recv()
                t = t + xbuf2[b - 1, h, d - 1].astype(F32)
            zsrc2[b - 1, h] = t.astype(BF16)
            extra_z(b, h).start()

    def extra_sent(b, h, cc, lo, hi):
        pl.when(c != cc)(extra_core(b, h, cc, lo, hi).wait_send)

        @pl.when(c == cc)
        def _():
            for d in (2, 1, 3):
                pl.when(within((x + d) % 4, lo, hi))(extra_x(b, h, d).wait_send)
            pl.when(within(x, lo, hi))(extra_z(b, h).wait_send)

    def extra_step(step):
        @pl.when(edge)
        def _():
            for u in extra:
                step(*u)

    own = poolsrc[0] + pool_get(0) + pool_get(1) + pool_get(2)
    poolsrc[1] = own
    pool_send(poolsrc.at[1], 9, at(c_=1 - c))
    compute(0, 0, 3)
    core_send(0, 0)
    compute(0, 3, 5)
    core_send(0, 1)
    compute(1, 0, 3)
    core_send(1, 0)
    both = own + pool_get(9)
    poolsrc[5] = both
    for d in range(1, 4):
        pool_send(poolsrc.at[5], 9 + d, at(x_=(x + d) % 4))
    core_reduce(0, 0)
    core_reduce(0, 1)

    @pl.when(edge)
    def _():
        for b in (3, 2, 1):
            extra_compute(b)
            extra_core_send(b)

    core_reduce(1, 0)
    here = both + pool_get(10) + pool_get(11) + pool_get(12)
    poolsrc[2] = here
    pool_send(poolsrc.at[2], 3, at_z(4))
    pool_send(poolsrc.at[2], 4, at_z(12))
    halo_wait(0)
    compute(2, 0, 3)
    core_send(2, 0)
    compute(1, 3, 5)
    core_send(1, 1)
    extra_step(extra_core_reduce)
    x_half(0, 0)
    x_half(0, 1)
    core_reduce(2, 0)
    core_reduce(1, 1)
    halo_wait(1)
    compute(3, 0, 3)
    core_send(3, 0)
    compute(2, 3, 5)
    core_send(2, 1)
    x_reduce(0, 0)
    x_reduce(0, 1)
    x_half(1, 0)
    core_reduce(3, 0)
    core_reduce(2, 1)
    three = here + pool_get(3) + pool_get(4)
    pool_send(poolbuf.at[4], 5, at_z(12))
    halo_wait(2)
    compute(3, 3, 5)
    core_send(3, 1)
    extra_step(extra_x_reduce)
    x_half(2, 0)
    x_half(1, 1)
    x_reduce(1, 0)
    core_reduce(3, 1)
    x_half(3, 0)
    x_half(2, 1)
    four = three + pool_get(5)
    poolsrc[3] = four
    pool_send(poolsrc.at[3], 6, at(zl_=zl + 1 - 2 * (zl % 2)))
    x_reduce(2, 0)
    x_reduce(1, 1)

    place = zl % 4
    middle = jnp.logical_or(place == 1, place == 2)

    def pool_copy(src, slot_i, dev):
        return remote(poolsrc.at[src], poolbuf.at[slot_i], ps.at[slot_i], pr.at[slot_i], dev)

    inward = pool_copy(6, 7, at(zl_=(zl + jnp.where(place == 1, 1, 7)) % 8))
    outward = pool_copy(4, 8, at(zl_=(zl + jnp.where(place == 1, 7, 1)) % 8))
    x_half(3, 1)
    x_reduce(3, 0)
    poolsrc[6] = four + pool_get(6)
    pl.when(middle)(inward.start)
    x_reduce(2, 1)
    x_reduce(3, 1)

    @pl.when(middle)
    def _():
        inward.wait_recv()
        poolsrc[4] = poolsrc[6] + poolbuf[7]
        outward.start()

    for load in loads[4:]:
        load.wait()

    proj = jnp.zeros((80, 256), F32)
    for b in range(4):
        if b == 3:
            @pl.when(jnp.logical_not(middle))
            def _():
                outward.wait_recv()
                poolsrc[4] = poolbuf[8]

            pre_all = poolsrc[4] * (1.0 / 38400.0)
            pooled = jnp.maximum(gain[4:5] * pre_all + shift[4:5], 0.0).astype(BF16)
            pool_term = jnp.dot(
                jnp.broadcast_to(pooled, (16, 256)), wprojv[pl.ds(1024, 256), :],
                preferred_element_type=F32,
            )[0:1]
        for way in range(2):
            remote(
                zsrc.at[b, 0], zbuf.at[b, way], zs.at[b, 0], zr.at[b, way], at_z(4)
            ).wait_recv()
        acc[b] = zbuf[b, 0].astype(F32) + zbuf[b, 1].astype(F32)
        if b > 0:
            over = jnp.zeros((), jnp.bool_)
            for eb, eh, ec, lo, hi in extra:
                if eb == b:
                    mine = jnp.logical_and(bit == eh, c == ec)
                    over = jnp.logical_or(over, jnp.logical_and(mine, within(x, lo, hi)))

            @pl.when(jnp.logical_and(edge_owner, over))
            def _():
                for half in range(2):
                    remote(
                        zsrc2.at[b - 1, 0], zbuf2.at[b - 1, half],
                        zs2.at[b - 1, 0], zr2.at[b - 1, half], at_z(4),
                    ).wait_recv()
                acc[b] += zbuf2[b - 1, 0].astype(F32) + zbuf2[b - 1, 1].astype(F32)

        act = jnp.maximum(acc[b] * gain[b : b + 1] + shift[b : b + 1], 0.0).astype(BF16)
        proj = proj + jnp.dot(act, wprojv[pl.ds(b * 256, 256), :], preferred_element_type=F32)
    head = jnp.maximum(gain[5:6] * (proj + pool_term) + shift[5:6], 0.0)
    head = jnp.concatenate([head, jnp.zeros((48, 256), F32)], axis=0)
    stage[...] = jnp.transpose(head).astype(BF16).reshape(16, 16, 128)

    def out_copy(d):
        return remote(stage.at[d], obuf.at[slot], os.at[d], orr.at[slot], (zl_dst * 4 + y_dst, d))

    def out_send(i, carry):
        @pl.when(has_col)
        def _():
            out_copy((ch + i) % 16).start()

        return carry

    lax.fori_loop(0, 16, out_send, 0)
    for copy in ycopies + list(psends.values()):
        copy.wait_send()
    for d in range(3):
        for side in range(2):
            pl.when(halo_out[side])(halo_copy(d, side).wait_send)

    @pl.when(middle)
    def _():
        inward.wait_send()
        outward.wait_send()

    @pl.when(edge)
    def _():
        for u in extra:
            extra_sent(*u)

    for u in core_copies:
        for copy in [core_copies[u], z_copies[u]] + x_copies[u]:
            copy.wait_send()

    def out_recv(i, carry):
        remote(stage.at[0], obuf.at[i], os.at[0], orr.at[i], east).wait_recv()
        return carry

    lax.fori_loop(0, 15, out_recv, 0)
    out[...] = obuf[:, :, 0:80]

    def out_sent(d, carry):
        @pl.when(has_col)
        def _():
            out_copy(d).wait_send()

        return carry

    lax.fori_loop(0, 16, out_sent, 0)


def local(features, pointwise_weight, w_atrous, w_pool, w_proj, norm_gain, norm_shift):
    feat = jnp.transpose(features, (1, 0, 2))
    vmem = pl.BlockSpec(memory_space=pltpu.VMEM)
    hbm = pl.BlockSpec(memory_space=pl.ANY)
    dma = pltpu.SemaphoreType.DMA
    out = pl.pallas_call(
        head_kernel,
        out_shape=pltpu.VMEM((15, 16, 80), BF16),
        in_specs=[hbm] * 7,
        out_specs=vmem,
        scratch_shapes=[
            pltpu.VMEM((15, 80, 128), BF16),
            pltpu.VMEM((11, 3, 80 + 2 * PAD, 128), BF16),
            pltpu.VMEM((4, 2, 2, 4, 80, 256), BF16),
            pltpu.VMEM((4, 2, 4, 80, 256), BF16),
            pltpu.VMEM((4, 2, 3, 80, 256), BF16),
            pltpu.VMEM((4, 2, 80, 256), BF16),
            pltpu.VMEM((4, 2, 80, 256), BF16),
            pltpu.VMEM((16, 16, 128), BF16),
            pltpu.VMEM((15, 16, 128), BF16),
            pltpu.VMEM((128, 256), BF16),
            pltpu.VMEM((3, 9, 128, 256), BF16),
            pltpu.VMEM((1280, 256), BF16),
            pltpu.VMEM((128, 256), BF16),
            pltpu.VMEM((6, 256), F32),
            pltpu.VMEM((6, 256), F32),
            pltpu.VMEM((7, 1, 256), F32),
            pltpu.VMEM((13, 1, 256), F32),
            pltpu.VMEM((3, 2, 2, 4, 80, 256), BF16),
            pltpu.VMEM((3, 2, 4, 80, 256), BF16),
            pltpu.VMEM((3, 2, 3, 80, 256), BF16),
            pltpu.VMEM((3, 2, 80, 256), BF16),
            pltpu.VMEM((3, 2, 80, 256), BF16),
            pltpu.VMEM((4, 80, 256), F32),
            pltpu.VMEM((4, 2, 80, 256), F32),
            dma((7,)),
            dma((3,)), dma((3,)),
            dma((6,)), dma((6,)),
            dma((4, 2)), dma((4, 2)),
            dma((4, 2, 3)), dma((4, 2, 3)),
            dma((4, 2)), dma((4, 2)),
            dma((16,)), dma((15,)),
            dma((13,)), dma((13,)),
            dma((3, 2)), dma((3, 2)),
            dma((3, 2, 3)), dma((3, 2, 3)),
            dma((3, 2)), dma((3, 2)),
        ],
        compiler_params=pltpu.CompilerParams(collective_id=0, has_side_effects=True),
        name="aspp_head",
    )(
        feat, pointwise_weight, w_atrous.reshape(3, 9, 128, 256), w_pool, w_proj,
        norm_gain, norm_shift,
    )
    return jnp.transpose(out, (2, 0, 1))


def solution(mesh):
    return jax.shard_map(
        local,
        mesh=mesh,
        in_specs=(
            P(None, "lon", "ch"),
            P("ch", None),
            P(None, None, None, "ch", None),
            P("ch", None),
            P(),
            P(),
            P(),
        ),
        out_specs=P(None, "lon", "ch"),
        check_vma=False,
    )
```

```python
import jax
import jax.numpy as jnp
from jax import lax
from jax.experimental import pallas as pl
from jax.experimental.pallas import tpu as pltpu
from jax.sharding import PartitionSpec as P

MESH_ID = pl.DeviceIdType.MESH
F32 = jnp.float32
BF16 = jnp.bfloat16

PAD = 48


def head_kernel(
    feat, pw, wa, wpool_h, wproj, gain_h, shift_h, out,
    xin, xb, part, cbuf, xbuf, zsrc, zbuf, stage, obuf,
    pwv, wav, wprojv, wpool, gain, shift, poolsrc, poolbuf,
    part2, cbuf2, xbuf2, zsrc2, zbuf2, acc, xacc,
    ld_sem, ys, yr, hs, hr, cs, cr, xs, xr, zs, zr, os, orr, ps, pr,
    cs2, cr2, xs2, xr2, zs2, zr2,
):
    lon = lax.axis_index("lon")
    ch = lax.axis_index("ch")
    zl, y = lon // 4, lon % 4
    zh, x, c = ch // 8, (ch // 2) % 4, ch % 2
    z = zh * 8 + zl

    def at(zl_=None, y_=None, x_=None, c_=None):
        zz = zl if zl_ is None else zl_
        yy = y if y_ is None else y_
        xx = x if x_ is None else x_
        cc = c if c_ is None else c_
        return (zz * 4 + yy, zh * 8 + xx * 2 + cc)

    def at_z(dz):
        zz = (z + dz) % 16
        return ((zz % 8) * 4 + y, (zz // 8) * 8 + x * 2 + c)

    def block_of(j, level):
        q = (j + 1) % 5
        return jnp.where(level == 0, 4 - q, q)

    bit = ((z + 12) % 16) // 8
    zl_dst = (zl + 4) % 8
    k = bit * 8 + c * 4 + x
    kj, kt = k // 3, k % 3
    kq = block_of(kj, zl_dst)
    kg = 4 * kq + y
    y_dst = kg // 5
    slot = (kg % 5) * 3 + kt
    has_col = k < 15

    barrier = pltpu.get_barrier_semaphore()

    def hello(dev):
        pl.semaphore_signal(barrier, inc=1, device_id=dev, device_id_type=MESH_ID)

    east, west = at(zl_=(zl + 1) % 8), at(zl_=(zl + 7) % 8)
    edge = jnp.logical_or(zl == 0, zl == 7)
    edge_owner = jnp.logical_or(zl == 3, zl == 4)

    @pl.when(edge_owner)
    def _():
        far = jnp.where(zl == 4, 7, 0) * 4 + y
        hello((far, x * 2 + c))
        hello((far, 8 + x * 2 + c))

    @pl.when(zl < 7)
    def _():
        hello(east)

    @pl.when(zl > 0)
    def _():
        hello(west)

    hello(at_z(4))
    hello(at_z(12))

    for d in range(1, 4):
        hello(at(y_=(y + d) % 4))
        hello(at(x_=(x + d) % 4))
    hello(at(c_=1 - c))

    loads = [
        pltpu.make_async_copy(src, dst, ld_sem.at[i])
        for i, (src, dst) in enumerate((
            (feat, xin), (wpool_h, wpool), (pw, pwv), (wa, wav),
            (wproj, wprojv), (gain_h, gain), (shift_h, shift),
        ))
    ]
    for load in loads:
        load.start()

    zrow = jnp.zeros((3, PAD, 128), BF16)

    def clear(i, carry):
        xb[i, :, pl.ds(0, PAD), :] = zrow
        xb[i, :, pl.ds(PAD + 80, PAD), :] = zrow
        return carry

    lax.fori_loop(0, 11, clear, 0)
    for b in range(4):
        part[b, 1, 1, 3] = jnp.zeros((80, 256), BF16)

    blank = jnp.zeros((3, 80, 128), BF16)

    @pl.when(edge)
    def _():
        for d in range(3):
            xb[jnp.where(zl == 0, d, 8 + d), :, pl.ds(PAD, 80), :] = blank

    loads[0].wait()
    loads[1].wait()
    xb[y + 3, :, pl.ds(PAD, 80), :] = xin[0:3]
    xb[y + 4, :, pl.ds(PAD, 80), :] = xin[12:15]

    def add_col(i, tot):
        return tot + jnp.sum(xin[i].astype(F32).reshape(10, 8, 128), axis=0)

    sums = lax.fori_loop(0, 15, add_col, jnp.zeros((8, 128), F32))
    colsum = jnp.sum(sums, axis=0, keepdims=True)
    pre = jnp.dot(
        jnp.broadcast_to(colsum, (8, 128)), wpool[...].astype(F32),
        precision=lax.Precision.HIGHEST, preferred_element_type=F32,
    )[0:1]
    poolsrc[0] = pre

    pl.semaphore_wait(barrier, 11 + edge.astype(jnp.int32))

    def remote(src, dst, ssem, rsem, dev):
        return pltpu.make_async_remote_copy(
            src_ref=src, dst_ref=dst, send_sem=ssem, recv_sem=rsem,
            device_id=dev, device_id_type=MESH_ID,
        )

    rows = pl.ds(PAD, 80)
    ycopies = []
    for g in range(1, 4):
        q = (5 * y + g) // 4
        copy = remote(
            xin.at[pl.ds(3 * g, 3)], xb.at[q + 3, :, rows, :],
            ys.at[g - 1], yr.at[g - 1], at(y_=(y + g) % 4),
        )
        copy.start()
        ycopies.append(copy)
    psends = {}

    def pool_send(src, slot_i, dev):
        psends[slot_i] = remote(src, poolbuf.at[slot_i], ps.at[slot_i], pr.at[slot_i], dev)
        psends[slot_i].start()

    def pool_get(slot_i):
        psends[slot_i].wait_recv()
        return poolbuf[slot_i]

    for d in range(1, 4):
        pool_send(poolsrc.at[0], d - 1, at(y_=(y + d) % 4))

    def halo_copy(d, side):
        q = (4 - d) if side == 0 else d
        q_to = q - 5 if side == 0 else q + 5
        return remote(
            xb.at[q + 3, :, rows, :], xb.at[q_to + 3, :, rows, :],
            hs.at[2 * d + side], hr.at[2 * d + side], east if side == 0 else west,
        )

    halo_out = (zl < 7, zl > 0)
    halo_in = (zl > 0, zl < 7)
    for d, sides in ((0, (0,)), (0, (1,)), (1, (0,)), (1, (1,)), (2, (0, 1))):
        q = (4 - d) if sides[0] == 0 else d
        g = (4 * q + y) % 5

        @pl.when(jnp.logical_and(g > 0, g < 4))
        def _():
            gi = jnp.clip(g - 1, 0, 2)
            remote(
                xin.at[pl.ds(0, 3)], xb.at[q + 3, :, rows, :], ys.at[gi], yr.at[gi], east
            ).wait_recv()

        for side in sides:
            pl.when(halo_out[side])(halo_copy(d, side).start)

    def halo_wait(d):
        for side in range(2):
            pl.when(halo_in[side])(halo_copy(d, side).wait_recv)

    loads[2].wait()
    loads[3].wait()

    def compute(b, lo, hi):
        def body(j, carry):
            q = block_of(j, zl)
            if b == 0:
                lhs = xb[q + 3, :, rows, :].reshape(240, 128)
                res = jnp.dot(lhs, pwv[...], preferred_element_type=F32)
            else:
                taps = []
                for ro in (-1, 0, 1):
                    for co in (-1, 0, 1):
                        taps.append(
                            xb[q + 3 + co * b, :, pl.ds(PAD + ro * b * 12, 80), :].reshape(240, 128)
                        )
                res = jnp.dot(
                    jnp.concatenate(taps, axis=1), wav[b - 1].reshape(1152, 256),
                    preferred_element_type=F32,
                )
            res = res.astype(BF16).reshape(3, 80, 256)
            for t in range(3):
                s = 3 * j + t
                part[b, (s // 4) % 2, s // 8, s % 4] = res[t]
            return carry

        lax.fori_loop(lo, hi, body, 0)

    core_copies, x_copies, z_copies = {}, {}, {}

    def core_send(b, h):
        copy = remote(
            part.at[b, 1 - c, h], cbuf.at[b, h], cs.at[b, h], cr.at[b, h], at(c_=1 - c)
        )
        copy.start()
        core_copies[b, h] = copy

    def core_reduce(b, h):
        core_copies[b, h].wait_recv()

        def body(i, carry):
            mine = part[b, c, h, i].astype(F32) + cbuf[b, h, i].astype(F32)
            part[b, c, h, i] = mine.astype(BF16)
            return carry

        lax.fori_loop(0, 4, body, 0)
        first = flip if h == 0 else 3 - x
        x_copies[b, h] = []
        for i, col in enumerate((first, (x + 2) % 4)):
            copy = remote(
                part.at[b, c, h, col], xbuf.at[b, h, i], xs.at[b, h, i], xr.at[b, h, i],
                at(x_=first),
            )
            copy.start()
            x_copies[b, h].append(copy)

    flip = x + 1 - 2 * (x % 2)

    def x_half(b, h):
        second = 3 - x if h == 0 else flip
        for copy in x_copies[b, h]:
            copy.wait_recv()
        give = part[b, c, h, second].astype(F32) + xbuf[b, h, 1].astype(F32)
        part[b, c, h, second] = give.astype(BF16)
        copy = remote(
            part.at[b, c, h, second], xbuf.at[b, h, 2], xs.at[b, h, 2], xr.at[b, h, 2],
            at(x_=second),
        )
        copy.start()
        x_copies[b, h].append(copy)
        xacc[b, h] = part[b, c, h, x].astype(F32) + xbuf[b, h, 0].astype(F32)

    def x_reduce(b, h):
        x_copies[b, h][2].wait_recv()
        zsrc[b, h] = (xacc[b, h] + xbuf[b, h, 2].astype(F32)).astype(BF16)
        up = (zh == h).astype(jnp.int32)
        z_copies[b, h] = remote(
            zsrc.at[b, h], zbuf.at[b, 1 - up], zs.at[b, h], zr.at[b, 1 - up], at_z(12 - 8 * up)
        )
        z_copies[b, h].start()

    extra = (
        (3, 0, 0, 3, 4), (3, 0, 1, 0, 4), (3, 1, 0, 0, 4),
        (2, 0, 1, 2, 4), (2, 1, 0, 0, 4), (1, 1, 0, 1, 4),
    )

    def within(to, lo, hi):
        return jnp.logical_and(to >= lo, to < hi)

    def extra_compute(b):
        col = jnp.where(zl == 7, 0, 2)
        kernel = jnp.concatenate([wav[b - 1, r * 3 + col] for r in range(3)], axis=0)

        def body(j, carry):
            q = jnp.where(zl == 7, 8 - j - b, j + b - 4)
            lhs = jnp.concatenate(
                [
                    xb[q + 3, :, pl.ds(PAD + ro * b * 12, 80), :].reshape(240, 128)
                    for ro in (-1, 0, 1)
                ],
                axis=1,
            )
            res = jnp.dot(lhs, kernel, preferred_element_type=F32)
            res = res.astype(BF16).reshape(3, 80, 256)
            for t in range(3):
                s = 3 * j + t
                part2[b - 1, (s // 4) % 2, s // 8, s % 4] = res[t]
            return carry

        lax.fori_loop(4 - b, 4, body, 0)

    def extra_core(b, h, cc, lo, hi):
        n = hi - lo
        return remote(
            part2.at[b - 1, cc, h, pl.ds(lo, n)], cbuf2.at[b - 1, h, pl.ds(lo, n)],
            cs2.at[b - 1, h], cr2.at[b - 1, h], at(c_=1 - c),
        )

    def extra_core_send(b):
        for u in extra:
            if u[0] == b:
                pl.when(c != u[2])(extra_core(*u).start)

    def extra_x(b, h, d):
        to = (x + d) % 4
        return remote(
            part2.at[b - 1, c, h, to], xbuf2.at[b - 1, h, d - 1],
            xs2.at[b - 1, h, d - 1], xr2.at[b - 1, h, d - 1], at(x_=to),
        )

    def extra_z(b, h):
        zz = (7 - zl + 4 + 8 * h) % 16
        return remote(
            zsrc2.at[b - 1, h], zbuf2.at[b - 1, zh], zs2.at[b - 1, h], zr2.at[b - 1, zh],
            ((zz % 8) * 4 + y, (zz // 8) * 8 + x * 2 + c),
        )

    def extra_core_reduce(b, h, cc, lo, hi):
        @pl.when(c == cc)
        def _():
            extra_core(b, h, cc, lo, hi).wait_recv()
            for i in range(lo, hi):
                mine = part2[b - 1, cc, h, i].astype(F32) + cbuf2[b - 1, h, i].astype(F32)
                part2[b - 1, cc, h, i] = mine.astype(BF16)
            for d in (2, 1, 3):
                pl.when(within((x + d) % 4, lo, hi))(extra_x(b, h, d).start)

    def extra_x_reduce(b, h, cc, lo, hi):
        @pl.when(jnp.logical_and(c == cc, within(x, lo, hi)))
        def _():
            t = part2[b - 1, cc, h, x].astype(F32)
            for d in (2, 1, 3):
                extra_x(b, h, d).wait_recv()
                t = t + xbuf2[b - 1, h, d - 1].astype(F32)
            zsrc2[b - 1, h] = t.astype(BF16)
            extra_z(b, h).start()

    def extra_sent(b, h, cc, lo, hi):
        pl.when(c != cc)(extra_core(b, h, cc, lo, hi).wait_send)

        @pl.when(c == cc)
        def _():
            for d in (2, 1, 3):
                pl.when(within((x + d) % 4, lo, hi))(extra_x(b, h, d).wait_send)
            pl.when(within(x, lo, hi))(extra_z(b, h).wait_send)

    def extra_step(step):
        @pl.when(edge)
        def _():
            for u in extra:
                step(*u)

    own = poolsrc[0] + pool_get(0) + pool_get(1) + pool_get(2)
    poolsrc[1] = own
    pool_send(poolsrc.at[1], 9, at(c_=1 - c))
    compute(0, 0, 3)
    core_send(0, 0)
    compute(0, 3, 5)
    core_send(0, 1)
    compute(1, 0, 3)
    core_send(1, 0)
    both = own + pool_get(9)
    poolsrc[5] = both
    for d in range(1, 4):
        pool_send(poolsrc.at[5], 9 + d, at(x_=(x + d) % 4))
    core_reduce(0, 0)
    core_reduce(0, 1)

    @pl.when(edge)
    def _():
        for b in (3, 2, 1):
            extra_compute(b)
            extra_core_send(b)

    core_reduce(1, 0)
    extra_step(extra_core_reduce)
    here = both + pool_get(10) + pool_get(11) + pool_get(12)
    poolsrc[2] = here
    pool_send(poolsrc.at[2], 3, at_z(4))
    pool_send(poolsrc.at[2], 4, at_z(12))
    halo_wait(0)
    compute(2, 0, 3)
    core_send(2, 0)
    compute(1, 3, 5)
    core_send(1, 1)
    x_half(0, 0)
    x_half(0, 1)
    core_reduce(2, 0)
    core_reduce(1, 1)
    halo_wait(1)
    compute(3, 0, 3)
    core_send(3, 0)
    compute(2, 3, 5)
    core_send(2, 1)
    x_reduce(0, 0)
    x_reduce(0, 1)
    x_half(1, 0)
    core_reduce(3, 0)
    core_reduce(2, 1)
    extra_step(extra_x_reduce)
    three = here + pool_get(3) + pool_get(4)
    pool_send(poolbuf.at[4], 5, at_z(12))
    halo_wait(2)
    compute(3, 3, 5)
    core_send(3, 1)
    x_half(2, 0)
    x_half(1, 1)
    x_reduce(1, 0)
    core_reduce(3, 1)
    x_half(3, 0)
    x_half(2, 1)
    four = three + pool_get(5)
    poolsrc[3] = four
    pool_send(poolsrc.at[3], 6, at(zl_=zl + 1 - 2 * (zl % 2)))
    x_reduce(2, 0)
    x_reduce(1, 1)

    place = zl % 4
    middle = jnp.logical_or(place == 1, place == 2)

    def pool_copy(src, slot_i, dev):
        return remote(poolsrc.at[src], poolbuf.at[slot_i], ps.at[slot_i], pr.at[slot_i], dev)

    inward = pool_copy(6, 7, at(zl_=(zl + jnp.where(place == 1, 1, 7)) % 8))
    outward = pool_copy(4, 8, at(zl_=(zl + jnp.where(place == 1, 7, 1)) % 8))
    x_half(3, 1)
    x_reduce(3, 0)
    poolsrc[6] = four + pool_get(6)
    pl.when(middle)(inward.start)
    x_reduce(2, 1)
    x_reduce(3, 1)

    @pl.when(middle)
    def _():
        inward.wait_recv()
        poolsrc[4] = poolsrc[6] + poolbuf[7]
        outward.start()

    for load in loads[4:]:
        load.wait()

    proj = jnp.zeros((80, 256), F32)
    for b in range(4):
        if b == 3:
            @pl.when(jnp.logical_not(middle))
            def _():
                outward.wait_recv()
                poolsrc[4] = poolbuf[8]

            pre_all = poolsrc[4] * (1.0 / 38400.0)
            pooled = jnp.maximum(gain[4:5] * pre_all + shift[4:5], 0.0).astype(BF16)
            pool_term = jnp.dot(
                jnp.broadcast_to(pooled, (16, 256)), wprojv[pl.ds(1024, 256), :],
                preferred_element_type=F32,
            )[0:1]
        for way in range(2):
            remote(
                zsrc.at[b, 0], zbuf.at[b, way], zs.at[b, 0], zr.at[b, way], at_z(4)
            ).wait_recv()
        acc[b] = zbuf[b, 0].astype(F32) + zbuf[b, 1].astype(F32)
        if b > 0:
            over = jnp.zeros((), jnp.bool_)
            for eb, eh, ec, lo, hi in extra:
                if eb == b:
                    mine = jnp.logical_and(bit == eh, c == ec)
                    over = jnp.logical_or(over, jnp.logical_and(mine, within(x, lo, hi)))

            @pl.when(jnp.logical_and(edge_owner, over))
            def _():
                for half in range(2):
                    remote(
                        zsrc2.at[b - 1, 0], zbuf2.at[b - 1, half],
                        zs2.at[b - 1, 0], zr2.at[b - 1, half], at_z(4),
                    ).wait_recv()
                acc[b] += zbuf2[b - 1, 0].astype(F32) + zbuf2[b - 1, 1].astype(F32)

        act = jnp.maximum(acc[b] * gain[b : b + 1] + shift[b : b + 1], 0.0).astype(BF16)
        proj = proj + jnp.dot(act, wprojv[pl.ds(b * 256, 256), :], preferred_element_type=F32)
    head = jnp.maximum(gain[5:6] * (proj + pool_term) + shift[5:6], 0.0)
    head = jnp.concatenate([head, jnp.zeros((48, 256), F32)], axis=0)
    stage[...] = jnp.transpose(head).astype(BF16).reshape(16, 16, 128)

    def out_copy(d):
        return remote(stage.at[d], obuf.at[slot], os.at[d], orr.at[slot], (zl_dst * 4 + y_dst, d))

    def out_send(i, carry):
        @pl.when(has_col)
        def _():
            out_copy((ch + i) % 16).start()

        return carry

    lax.fori_loop(0, 16, out_send, 0)
    for copy in ycopies + list(psends.values()):
        copy.wait_send()
    for d in range(3):
        for side in range(2):
            pl.when(halo_out[side])(halo_copy(d, side).wait_send)

    @pl.when(middle)
    def _():
        inward.wait_send()
        outward.wait_send()

    @pl.when(edge)
    def _():
        for u in extra:
            extra_sent(*u)

    for u in core_copies:
        for copy in [core_copies[u], z_copies[u]] + x_copies[u]:
            copy.wait_send()

    def out_recv(i, carry):
        remote(stage.at[0], obuf.at[i], os.at[0], orr.at[i], east).wait_recv()
        return carry

    lax.fori_loop(0, 15, out_recv, 0)
    out[...] = obuf[:, :, 0:80]

    def out_sent(d, carry):
        @pl.when(has_col)
        def _():
            out_copy(d).wait_send()

        return carry

    lax.fori_loop(0, 16, out_sent, 0)


def local(features, pointwise_weight, w_atrous, w_pool, w_proj, norm_gain, norm_shift):
    feat = jnp.transpose(features, (1, 0, 2))
    vmem = pl.BlockSpec(memory_space=pltpu.VMEM)
    hbm = pl.BlockSpec(memory_space=pl.ANY)
    dma = pltpu.SemaphoreType.DMA
    out = pl.pallas_call(
        head_kernel,
        out_shape=pltpu.VMEM((15, 16, 80), BF16),
        in_specs=[hbm] * 7,
        out_specs=vmem,
        scratch_shapes=[
            pltpu.VMEM((15, 80, 128), BF16),
            pltpu.VMEM((11, 3, 80 + 2 * PAD, 128), BF16),
            pltpu.VMEM((4, 2, 2, 4, 80, 256), BF16),
            pltpu.VMEM((4, 2, 4, 80, 256), BF16),
            pltpu.VMEM((4, 2, 3, 80, 256), BF16),
            pltpu.VMEM((4, 2, 80, 256), BF16),
            pltpu.VMEM((4, 2, 80, 256), BF16),
            pltpu.VMEM((16, 16, 128), BF16),
            pltpu.VMEM((15, 16, 128), BF16),
            pltpu.VMEM((128, 256), BF16),
            pltpu.VMEM((3, 9, 128, 256), BF16),
            pltpu.VMEM((1280, 256), BF16),
            pltpu.VMEM((128, 256), BF16),
            pltpu.VMEM((6, 256), F32),
            pltpu.VMEM((6, 256), F32),
            pltpu.VMEM((7, 1, 256), F32),
            pltpu.VMEM((13, 1, 256), F32),
            pltpu.VMEM((3, 2, 2, 4, 80, 256), BF16),
            pltpu.VMEM((3, 2, 4, 80, 256), BF16),
            pltpu.VMEM((3, 2, 3, 80, 256), BF16),
            pltpu.VMEM((3, 2, 80, 256), BF16),
            pltpu.VMEM((3, 2, 80, 256), BF16),
            pltpu.VMEM((4, 80, 256), F32),
            pltpu.VMEM((4, 2, 80, 256), F32),
            dma((7,)),
            dma((3,)), dma((3,)),
            dma((6,)), dma((6,)),
            dma((4, 2)), dma((4, 2)),
            dma((4, 2, 3)), dma((4, 2, 3)),
            dma((4, 2)), dma((4, 2)),
            dma((16,)), dma((15,)),
            dma((13,)), dma((13,)),
            dma((3, 2)), dma((3, 2)),
            dma((3, 2, 3)), dma((3, 2, 3)),
            dma((3, 2)), dma((3, 2)),
        ],
        compiler_params=pltpu.CompilerParams(collective_id=0, has_side_effects=True),
        name="aspp_head",
    )(
        feat, pointwise_weight, w_atrous.reshape(3, 9, 128, 256), w_pool, w_proj,
        norm_gain, norm_shift,
    )
    return jnp.transpose(out, (2, 0, 1))


def solution(mesh):
    return jax.shard_map(
        local,
        mesh=mesh,
        in_specs=(
            P(None, "lon", "ch"),
            P("ch", None),
            P(None, None, None, "ch", None),
            P("ch", None),
            P(),
            P(),
            P(),
        ),
        out_specs=P(None, "lon", "ch"),
        check_vma=False,
    )
```
